32 devices in a mesh: dp: 2 (over y), seq: 16 (over z, x, core).
Axes of the slice: x: 2, y: 2, z: 4, core: 2. Of those that a mesh axis runs over, the one named last changes fastest.
Arguments:
- patch_features: bfloat16 [4, 768, 1664], P('dp', 'seq'), may hold values from -6 to 6
- text_embeds: bfloat16 [4, 384, 1024], P('dp', 'seq'), may hold values from -6 to 6
- text_lengths: int32 [4, 3], P('dp'), may hold values from 1 to 192, 288 in all within a row
- w_in: bfloat16 [1664, 1024], P(None, ('dp', 'seq')), may hold values from -0.15625 to 0.15625
- b_in: bfloat16 [1024], P(('dp', 'seq')), may hold values from -3 to 3
- gain_attn: bfloat16 [1024], P(('dp', 'seq')), may hold values from 0.5 to 1.5
- w_query: bfloat16 [1024, 1024], P(None, ('dp', 'seq')), may hold values from -0.09375 to 0.09375
- w_key: bfloat16 [1024, 1024], P(None, ('dp', 'seq')), may hold values from -0.09375 to 0.09375
- w_value: bfloat16 [1024, 1024], P(None, ('dp', 'seq')), may hold values from -0.1875 to 0.1875
- w_out: bfloat16 [1024, 1024], P(None, ('dp', 'seq')), may hold values from -0.75 to 0.75
- gain_ffn: bfloat16 [1024], P(('dp', 'seq')), may hold values from 0.5 to 1.5
- w_gate: bfloat16 [1024, 2816], P(None, ('dp', 'seq')), may hold values from -0.1875 to 0.1875
- w_up: bfloat16 [1024, 2816], P(None, ('dp', 'seq')), may hold values from -0.1875 to 0.1875
- w_down: bfloat16 [2816, 1024], P(None, ('dp', 'seq')), may hold values from -0.109375 to 0.109375
- position_bias: bfloat16 [512], P(('dp', 'seq')), may hold values from -4 to 4
- d_patch: bfloat16 [4, 768, 1024], P('dp', 'seq'), may hold values from -6 to 6
- d_text: bfloat16 [4, 384, 1024], P('dp', 'seq'), may hold values from -6 to 6
Outputs:
- patch_out: bfloat16 [4, 768, 1024], P('dp', 'seq')
- text_out: bfloat16 [4, 384, 1024], P('dp', 'seq')
- feature_grad: float32 [4, 768, 1664], P('dp', 'seq')
- text_grad: float32 [4, 384, 1024], P('dp', 'seq')
- grad_w_in: float32 [1664, 1024], P(None, ('dp', 'seq'))
- grad_b_in: float32 [1024], P(('dp', 'seq'))
- grad_gain_attn: float32 [1024], P(('dp', 'seq'))
- grad_w_query: float32 [1024, 1024], P(None, ('dp', 'seq'))
- grad_w_key: float32 [1024, 1024], P(None, ('dp', 'seq'))
- grad_w_value: float32 [1024, 1024], P(None, ('dp', 'seq'))
- grad_w_out: float32 [1024, 1024], P(None, ('dp', 'seq'))
- grad_gain_ffn: float32 [1024], P(('dp', 'seq'))
- grad_w_gate: float32 [1024, 2816], P(None, ('dp', 'seq'))
- grad_w_up: float32 [1024, 2816], P(None, ('dp', 'seq'))
- grad_w_down: float32 [2816, 1024], P(None, ('dp', 'seq'))
- grad_position_bias: float32 [512], P(('dp', 'seq'))
The draws below stay inside these ranges and needn't reach their ends.
Inputs may be any that keep to these rules, and one draw needn't show every extreme that they name: `text_lengths`: each row's 3 text lengths sum to 288, and the longest is exactly 192; the texts fill the slots in order of fill index, the rest are padding.
All inputs are finite; a program needn't handle non-finite values.
Results may differ from the reference program's by a relative error of at most 0.015.
Values may be sent and summed in bfloat16 or wider, within the bound.
No kernel may reach another device: no remote copies, remote signals or barrier semaphores. Data moves between devices by JAX's collectives and lax.ppermute only.
A program may use at most 384 MiB of HBM per device.

```python
import math
import jax
import jax.numpy as jnp
import numpy as np
from jax import lax

D = 1024
HEADS = 16
HEAD_DIM = 64
FF = 2816
VIT = 1664
BUCKETS = 32
PATCHES_IMG = 256
ROW = 1152
PATCHES_ROW = 768
TEXT_SLOTS = 384
IMAGES = 3
TEXT_TOTAL = 288
TEXT_MOST = 192
ROWS = 4


def level_of(rng, extent, pieces, low, largest):
    factor_of = 1.0
    for axis_at, shards_of in pieces:
        draws = jax.random.uniform(jax.random.fold_in(jax.random.fold_in(rng, 6), axis_at), (shards_of,), jnp.float32, low / len(pieces), largest / len(pieces))
        factor_of = factor_of * jnp.repeat(jnp.exp(draws), extent[axis_at] // shards_of).reshape((-1,) + (1,) * (len(extent) - 1 - axis_at))
    return factor_of


def length_profile(number_of, total, reach, slope):
    weights = [(1 << 20) // math.isqrt(standing ** slope) + 1 for standing in range(2, number_of + 1)]
    rest, holding = total - reach - (number_of - 1), [1] * (number_of - 1)
    while rest > 0:
        free = [i for i in range(number_of - 1) if holding[i] < reach]
        pool, budget = sum([weights[i] for i in free]), rest
        for i in free:
            more = min(reach - holding[i], max(1, budget * weights[i] // pool), rest)
            holding[i] = holding[i] + more
            rest = rest - more
    return np.array([reach] + holding)


def ragged_sizes(rng, count, total, limit, lean):
    if count == 2:
        one = jax.random.randint(rng, (), max(1, total - limit), min(limit, total - 1) + 1)
        return jnp.stack([one, total - one])
    tallies = jnp.asarray(length_profile(count, total, limit, lean), jnp.int32)
    twos = (count - 1) // 2
    giver, taker = tallies[1:1 + 2 * twos:2], tallies[2:2 + 2 * twos:2]
    slack = jnp.minimum(giver - 1, limit - taker)
    passed = jax.random.randint(jax.random.fold_in(rng, 1), (twos,), 0, 1 << 20) % (slack + 1)
    tallies = tallies.at[1:1 + 2 * twos:2].set(giver - passed).at[2:2 + 2 * twos:2].set(taker + passed)
    return tallies[jax.random.permutation(jax.random.fold_in(rng, 2), count)]


def normal_values(own_key, extent, scale, reach, shards=(), kind=jnp.bfloat16):
    values = jax.random.normal(own_key, extent, jnp.float32) * scale
    if len(shards) > 0:
        values = level_of(own_key, extent, shards, -0.22, 0.18) * values
    return jnp.clip(values, min=-reach, max=reach).astype(kind)


def setup_inputs(seed: int = 0) -> dict:
    seeds = jax.random.split(jax.random.key(seed), 18)
    patch_features = normal_values(seeds[0], (ROWS, PATCHES_ROW, VIT), 1.0, 6.0, ((0, 2), (1, 16)))
    text_embeds = normal_values(seeds[1], (ROWS, TEXT_SLOTS, D), 1.0, 6.0, ((0, 2), (1, 16)))
    text_lengths = jax.vmap(lambda own: ragged_sizes(own, IMAGES, TEXT_TOTAL, TEXT_MOST, 2))(jax.random.split(seeds[2], ROWS)).reshape((ROWS, IMAGES)).astype(jnp.int32)
    w_in = normal_values(seeds[3], (VIT, D), VIT ** -0.5, 0.15625, ((1, 32),))
    b_in = normal_values(seeds[4], (D,), 0.5, 3.0, ((0, 32),))
    gain_attn = jnp.clip(1.0 + 0.1 * jax.random.normal(seeds[5], (D,), jnp.float32), 0.5, 1.5).astype(jnp.bfloat16)
    w_query = normal_values(seeds[6], (D, D), (4 * D) ** -0.5, 0.09375, ((1, 32),))
    w_key = normal_values(seeds[7], (D, D), (4 * D) ** -0.5, 0.09375, ((1, 32),))
    w_value = normal_values(seeds[8], (D, D), D ** -0.5, 0.1875, ((1, 32),))
    w_out = normal_values(seeds[9], (D, D), (D // 16) ** -0.5, 0.75, ((1, 32),))
    gain_ffn = jnp.clip(1.0 + 0.1 * jax.random.normal(seeds[10], (D,), jnp.float32), 0.5, 1.5).astype(jnp.bfloat16)
    w_gate = normal_values(seeds[11], (D, FF), D ** -0.5, 0.1875, ((1, 32),))
    w_up = normal_values(seeds[12], (D, FF), D ** -0.5, 0.1875, ((1, 32),))
    w_down = normal_values(seeds[13], (FF, D), FF ** -0.5, 0.109375, ((1, 32),))
    position_bias = normal_values(seeds[14], (BUCKETS * HEADS,), 1.0, 4.0, ((0, 32),))
    d_patch = normal_values(seeds[15], (ROWS, PATCHES_ROW, D), 1.0, 6.0, ((0, 2), (1, 16)))
    d_text = normal_values(seeds[16], (ROWS, TEXT_SLOTS, D), 1.0, 6.0, ((0, 2), (1, 16)))
    return dict(patch_features=patch_features, text_embeds=text_embeds, text_lengths=text_lengths, w_in=w_in, b_in=b_in, gain_attn=gain_attn, w_query=w_query, w_key=w_key, w_value=w_value, w_out=w_out, gain_ffn=gain_ffn, w_gate=w_gate, w_up=w_up, w_down=w_down, position_bias=position_bias, d_patch=d_patch, d_text=d_text)


@jax.custom_vjp
def low(v):
    return lax.optimization_barrier(v.astype(jnp.bfloat16)).astype(jnp.float32)

@jax.custom_vjp
def low_back(v):
    return v

def low_keep(v):
    return (low(v), None)

def low_pass(kept, grad):
    return (grad,)

def back_keep(v):
    return (v, None)

def back_low(kept, grad):
    return (low(grad),)
low.defvjp(low_keep, low_pass)
low_back.defvjp(back_keep, back_low)
EPSILON = 1e-06
BORDERS = (12, 16, 23, 32, 46, 64, 91)
MASKED = -1e+30
HIGH = lax.Precision.HIGHEST

def both_ways(v):
    return low(low_back(v))

def bucket_table(query_pos, key_pos):
    pos_delta = query_pos[:, None] - key_pos[None, :]
    magnitude = jnp.abs(pos_delta)
    far_bucket = jnp.full(magnitude.shape, 8, jnp.int32)
    for border in BORDERS:
        far_bucket = far_bucket + (magnitude >= border).astype(jnp.int32)
    near_bucket = jnp.where(magnitude < 8, magnitude, far_bucket)
    return (jnp.where(pos_delta < 0, 16, 0) + near_bucket).astype(jnp.int32)

def patch_layout(patch_count):
    patch_ids = jnp.arange(patch_count, dtype=jnp.int32)
    return ((patch_ids // PATCHES_IMG + 1).astype(jnp.int32), (patch_ids % PATCHES_IMG).astype(jnp.int32))

def text_layout(lengths, slot_count):
    image_count = lengths.shape[0]
    text_ends = jnp.cumsum(lengths).astype(jnp.int32)
    slot_ids = jnp.arange(slot_count, dtype=jnp.int32)
    fill_ids = ((slot_ids + slot_count // 2) % slot_count).astype(jnp.int32)
    text_index = lax.optimization_barrier(jnp.sum((fill_ids[:, None] >= text_ends[None, :]).astype(jnp.int32), axis=1)).astype(jnp.int32)
    text_starts = jnp.concatenate([(text_ends - lengths).astype(jnp.int32), text_ends[image_count - 1:]])
    matches = text_index[:, None] == jnp.arange(image_count + 1, dtype=jnp.int32)[None, :]
    text_begin = lax.optimization_barrier(jnp.sum(jnp.where(matches, text_starts[None, :], 0), axis=1)).astype(jnp.int32)
    segment = jnp.where(text_index < image_count, text_index + 1, 0).astype(jnp.int32)
    return (segment, (PATCHES_IMG + fill_ids - text_begin).astype(jnp.int32))

def rms_norm(values, gain):
    return values * lax.rsqrt(lax.optimization_barrier(jnp.mean(values * values, axis=-1, keepdims=True)) + EPSILON) * gain

def gelu_tanh(values):
    return 0.5 * values * (1.0 + jnp.tanh(0.7978845608 * (values + 0.044715 * values * values * values)))

def gated_unit(gate_pre, up_pre):
    return gelu_tanh(gate_pre) * up_pre

def row_forward(weights, row_feat, row_embed, lengths, patch_seg, patch_pos):
    w_in, b_in, gain_attn, w_query, w_key, w_value, w_out, gain_ffn, w_gate, w_up, w_down, position_bias = weights
    text_seg, text_pos = text_layout(lengths, TEXT_SLOTS)
    segments = jnp.concatenate([patch_seg, text_seg])
    positions = jnp.concatenate([patch_pos, text_pos])
    buckets = bucket_table(positions, positions)
    allowed = segments[:, None] == segments[None, :]
    table = position_bias.reshape(BUCKETS, HEADS)
    patch_rows = low_back(jnp.dot(row_feat, w_in, precision=HIGH)) + b_in
    resid = jnp.concatenate([patch_rows, row_embed], axis=0)
    normed_one = low(rms_norm(resid, gain_attn))
    queries = both_ways(jnp.dot(normed_one, w_query, precision=HIGH)).reshape(ROW, HEADS, HEAD_DIM)
    keys_all = both_ways(jnp.dot(normed_one, w_key, precision=HIGH)).reshape(ROW, HEADS, HEAD_DIM)
    values_all = both_ways(jnp.dot(normed_one, w_value, precision=HIGH)).reshape(ROW, HEADS, HEAD_DIM)
    block_rows = math.gcd(ROW, 512)
    block_count = ROW // block_rows

    def attend(block_data):
        query_block, bucket_block, allowed_block = block_data
        raw_scores = low_back(jnp.einsum('qhd,khd->hqk', query_block, keys_all, precision=HIGH))
        bias_block = jnp.transpose(table[bucket_block], (2, 0, 1))
        scores = jnp.where(allowed_block[None], raw_scores + bias_block, MASKED)
        top_score = lax.optimization_barrier(jnp.max(scores, axis=-1, keepdims=True))
        expd = jnp.exp(scores - top_score)
        probs = low(expd / lax.optimization_barrier(jnp.sum(expd, axis=-1, keepdims=True)))
        return jnp.einsum('hqk,khd->qhd', probs, values_all, precision=HIGH)
    mixed = lax.map(jax.checkpoint(attend), (queries.reshape(block_count, block_rows, HEADS, HEAD_DIM), buckets.reshape(block_count, block_rows, ROW), allowed.reshape(block_count, block_rows, ROW)))
    attn_out = both_ways(mixed.reshape(ROW, D))
    resid_one = resid + low_back(jnp.dot(attn_out, w_out, precision=HIGH))
    normed_two = low(rms_norm(resid_one, gain_ffn))
    gate_pre = low_back(jnp.dot(normed_two, w_gate, precision=HIGH))
    up_pre = low_back(jnp.dot(normed_two, w_up, precision=HIGH))
    hidden = low(gated_unit(gate_pre, up_pre))
    return resid_one + jnp.dot(hidden, w_down, precision=HIGH)

def reference(patch_features, text_embeds, text_lengths, w_in, b_in, gain_attn, w_query, w_key, w_value, w_out, gain_ffn, w_gate, w_up, w_down, position_bias, d_patch, d_text):
    weights = tuple((item.astype(jnp.float32) for item in (w_in, b_in, gain_attn, w_query, w_key, w_value, w_out, gain_ffn, w_gate, w_up, w_down, position_bias)))
    features = patch_features.astype(jnp.float32)
    embeds = text_embeds.astype(jnp.float32)
    patch_seg, patch_pos = patch_layout(PATCHES_ROW)

    def forward(weights, features, embeds):

        def one_row(carry, row_data):
            row_feat, row_embed, lengths = row_data
            return (carry, row_forward(weights, row_feat, row_embed, lengths, patch_seg, patch_pos))
        _, result = lax.scan(jax.checkpoint(one_row), jnp.zeros((), jnp.float32), (features, embeds, text_lengths))
        return result
    result, pullback = jax.vjp(forward, weights, features, embeds)
    cotangent = jnp.concatenate([d_patch, d_text], axis=1).astype(jnp.float32)
    grad_weights, grad_features, grad_embeds = pullback(cotangent)
    low_result = result.astype(jnp.bfloat16)
    return (low_result[:, :PATCHES_ROW], low_result[:, PATCHES_ROW:], grad_features, grad_embeds, grad_weights[0], grad_weights[1], grad_weights[2], grad_weights[3], grad_weights[4], grad_weights[5], grad_weights[6], grad_weights[7], grad_weights[8], grad_weights[9], grad_weights[10], grad_weights[11])
```

```python
import jax
import jax.numpy as jnp
from jax import lax
from jax.experimental import pallas as pl
from jax.experimental.pallas import tpu as pltpu
from jax.sharding import PartitionSpec as P

HEADS = 16
HEAD_DIM = 64
BUCKETS = 32
PATCHES_IMG = 256
TEXT_MOST = 192

EPSILON = 1e-06
MASKED = -1e30
STARTS = (0, 1, 2, 3, 4, 5, 6, 7, 8, 12, 16, 23, 32, 46, 64, 91)
BF16 = jnp.bfloat16
F32 = jnp.float32
INTERPRET = False

SEG_Q = PATCHES_IMG + TEXT_MOST
SEG_K = 2 * PATCHES_IMG
TEXT_K = SEG_K - PATCHES_IMG
TEXT_PITCH = 32


def dot_nt(left, right):
    return lax.dot_general(left, right, (((1,), (1,)), ((), ())), preferred_element_type=F32)


def dot_nn(left, right):
    return lax.dot_general(left, right, (((1,), (0,)), ((), ())), preferred_element_type=F32)


def dot_tn(left, right):
    return lax.dot_general(left, right, (((0,), (0,)), ((), ())), preferred_element_type=F32)


def rms_norm(values, gain):
    return values * lax.rsqrt(jnp.mean(values * values, axis=-1, keepdims=True) + EPSILON) * gain


def gelu_tanh(values):
    return (
        0.5
        * values
        * (1.0 + jnp.tanh(0.7978845608 * (values + 0.044715 * values * values * values)))
    )


def gated_unit(gate_pre, up_pre):
    return gelu_tanh(gate_pre) * up_pre


def swap(array, step):
    axis, bit = step
    count = lax.axis_size(axis)
    return lax.ppermute(array, axis, [(i, i ^ (1 << bit)) for i in range(count)])


def my_bit(step):
    axis, bit = step
    return (lax.axis_index(axis) >> bit) & 1


def rank(step):
    return (1000 if step[0] == "dp" else 0) + step[1]


def gather(block, order, absolute):
    rows, width = block.shape
    have = []
    for step in order:
        other = swap(block, step)
        at = sum(1 for done in have if rank(done) > rank(step))
        shape = [2] * len(have) + [rows, width]
        shape.insert(at, 1)
        mine, other = block.reshape(shape), other.reshape(shape)
        if absolute:
            bit = my_bit(step) == 1
            mine, other = jnp.where(bit, other, mine), jnp.where(bit, mine, other)
        have.append(step)
        block = jnp.concatenate([mine, other], axis=at).reshape((2 ** len(have)) * rows, width)
    return block


def scatter_add(grads, order, every, absolute, wide=()):
    every = sorted(every, key=rank, reverse=True)
    width = grads.shape[1]
    for step in order:
        at = every.index(step)
        rows = grads.shape[0] // 2
        view = grads.reshape(2**at, 2, rows // 2**at, width)
        if absolute:
            bit = my_bit(step)
            keep = lax.dynamic_slice_in_dim(view, bit, 1, 1)
            send = lax.dynamic_slice_in_dim(view, 1 - bit, 1, 1)
        else:
            keep = view[:, 0:1]
            send = view[:, 1:2]
        keep = keep.reshape(rows, width)
        send = send.reshape(rows, width)
        kind = F32 if step in wide else BF16
        got = swap(send.astype(kind), step)
        grads = keep.astype(F32) + got.astype(F32)
        every = [other for other in every if other != step]
    return grads


def bias_kernel(table_ref, out_ref):
    delta = lax.broadcasted_iota(jnp.int32, out_ref.shape, 0) - lax.broadcasted_iota(
        jnp.int32, out_ref.shape, 1
    )
    value = jnp.full(out_ref.shape, table_ref[0, BUCKETS - 1], F32)
    for which in range(14, 0, -1):
        value = jnp.where(delta > -STARTS[which + 1], table_ref[0, 16 + which], value)
    for which in range(16):
        value = jnp.where(delta >= STARTS[which], table_ref[0, which], value)
    out_ref[...] = value


def bucket_kernel(d_ref, out_ref):
    shape = d_ref.shape
    delta = lax.broadcasted_iota(jnp.int32, shape, 0) - lax.broadcasted_iota(jnp.int32, shape, 1)
    values = d_ref[...]
    rows = []
    for which in range(BUCKETS):
        low = STARTS[which % 16]
        high = STARTS[which % 16 + 1] if which % 16 < 15 else 1 << 20
        if which < 16:
            inside = (delta >= low) & (delta < high)
        else:
            inside = (delta <= -max(low, 1)) & (delta > -high)
        rows.append(jnp.sum(jnp.where(inside, values, 0.0), axis=0, keepdims=True))
    sums = jnp.sum(jnp.concatenate(rows, axis=0), axis=1, keepdims=True)
    out_ref[...] = jnp.broadcast_to(sums, out_ref.shape)


def unpack(source_ref, where, row, pat_ref, txt_ref, patch_dev, text_dev, lanes):
    tail = TEXT_PITCH - text_dev
    for place in range(source_ref.shape[0]):
        block = where(place)
        patches = block[0:patch_dev, lanes]
        text = block[patch_dev : patch_dev + text_dev, lanes]
        pat_ref[row, place * patch_dev : (place + 1) * patch_dev, :] = patches
        txt_ref[row, place * TEXT_PITCH : place * TEXT_PITCH + text_dev, :] = text
        if tail:
            txt_ref[row, place * TEXT_PITCH + text_dev : (place + 1) * TEXT_PITCH, :] = jnp.zeros(
                (tail, text.shape[1]), text.dtype
            )


def picker(count, text_rows, text_dev, slot_count, first, length):
    shape = (count, text_rows)
    column = lax.broadcasted_iota(jnp.int32, shape, 1)
    inner = column & (TEXT_PITCH - 1)
    slot = (column // TEXT_PITCH) * text_dev + inner
    fill = jnp.where(slot >= slot_count // 2, slot - slot_count // 2, slot + slot_count // 2)
    line = lax.broadcasted_iota(jnp.int32, shape, 0)
    hit = (fill == first + line) & (line < length) & (inner < text_dev)
    return hit.astype(F32).astype(BF16)


def softmax(scores):
    top = jnp.max(scores, axis=-1, keepdims=True)
    expd = jnp.exp(scores - top)
    return expd / jnp.sum(expd, axis=-1, keepdims=True)


def segment_start(len_ref, row, which):
    return lax.fori_loop(0, which, lambda at, total: total + len_ref[row, at], jnp.int32(0))


def forward_kernel(dims, me_ref, len_ref, bias_ref, qkv_ref, o_ref, pat, txt, opat, otxt):
    rows, images, patch_dev, text_dev, slots = dims
    seq_count = qkv_ref.shape[0]
    text_rows = seq_count * TEXT_PITCH
    for row in range(rows):
        unpack(
            qkv_ref,
            lambda place, row=row: qkv_ref.at[place ^ me_ref[0], row],
            row, pat, txt, patch_dev, text_dev, slice(None),
        )
    otxt[...] = jnp.zeros_like(otxt)

    def attend(compact, queries, keys, length):
        q = compact[:queries, :HEAD_DIM]
        k = compact[:keys, HEAD_DIM : 2 * HEAD_DIM]
        v = compact[:keys, 2 * HEAD_DIM :]
        scores = dot_nt(q, k) + bias_ref[:queries, :keys]
        column = lax.broadcasted_iota(jnp.int32, scores.shape, 1)
        probs = softmax(jnp.where(column < length, scores, MASKED)).astype(BF16)
        return dot_nn(probs, v).astype(BF16)

    def one_segment(step, carry):
        row, image = step // images, step % images
        length = len_ref[row, image]
        first = segment_start(len_ref, row, image)
        pick = picker(TEXT_K, text_rows, text_dev, slots, first, length)
        text = dot_nn(pick, txt[row]).astype(BF16)
        at = pl.multiple_of(image * PATCHES_IMG, PATCHES_IMG)
        compact = jnp.concatenate([pat[row, pl.ds(at, PATCHES_IMG), :], text], axis=0)
        out = attend(compact, SEG_Q, SEG_K, PATCHES_IMG + length)
        opat[row, pl.ds(at, PATCHES_IMG), :] = out[:PATCHES_IMG]
        otxt[row] = otxt[row] + dot_tn(pick[:TEXT_MOST], out[PATCHES_IMG:])
        return carry

    lax.fori_loop(0, rows * images, one_segment, 0)
    pad_q = slots // 4
    pad_k = -(-pad_q // 128) * 128
    for row in range(rows):
        first = segment_start(len_ref, row, images)
        pick = picker(pad_k, text_rows, text_dev, slots, first, pad_q)
        compact = dot_nn(pick, txt[row]).astype(BF16)
        out = attend(compact, pad_q, pad_k, pad_q)
        otxt[row] = otxt[row] + dot_tn(pick[:pad_q], out)
    for place in range(seq_count):
        o_ref[place, 0:patch_dev, :] = jnp.concatenate(
            [opat[row, place * patch_dev : (place + 1) * patch_dev, :] for row in range(rows)],
            axis=1,
        )
        low = place * TEXT_PITCH
        o_ref[place, patch_dev : patch_dev + text_dev, :] = jnp.concatenate(
            [otxt[row, low : low + text_dev, :].astype(BF16) for row in range(rows)], axis=1
        )


def backward_kernel(
    dims, me_ref, len_ref, bias_ref, qkv_ref, do_ref, dqkv_ref, dbias_ref,
    pat, txt, dpat, dtxt, gpat, gtxt,
):
    rows, images, patch_dev, text_dev, slots = dims
    seq_count = qkv_ref.shape[0]
    text_rows = seq_count * TEXT_PITCH
    for row in range(rows):
        unpack(
            qkv_ref,
            lambda place, row=row: qkv_ref.at[place ^ me_ref[0], row],
            row, pat, txt, patch_dev, text_dev, slice(None),
        )
        unpack(
            do_ref,
            lambda place: do_ref.at[place],
            row, dpat, dtxt, patch_dev, text_dev,
            slice(row * HEAD_DIM, (row + 1) * HEAD_DIM),
        )
    gtxt[...] = jnp.zeros_like(gtxt)
    dbias_ref[...] = jnp.zeros_like(dbias_ref)

    def attend_back(compact, d_out, queries, keys, length):
        q = compact[:queries, :HEAD_DIM]
        k = compact[:keys, HEAD_DIM : 2 * HEAD_DIM]
        v = compact[:keys, 2 * HEAD_DIM :]
        scores = dot_nt(q, k) + bias_ref[:queries, :keys]
        column = lax.broadcasted_iota(jnp.int32, scores.shape, 1)
        probs = softmax(jnp.where(column < length, scores, MASKED))
        d_probs = dot_nt(d_out, v)
        centre = jnp.sum(d_probs * probs, axis=-1, keepdims=True)
        d_scores = probs * (d_probs - centre)
        d_low = d_scores.astype(BF16)
        d_q = dot_nn(d_low, k).astype(BF16)
        d_k = dot_tn(d_low, q).astype(BF16)
        d_v = dot_tn(probs.astype(BF16), d_out).astype(BF16)
        return d_scores, jnp.concatenate([d_q, d_k[:queries], d_v[:queries]], axis=1)

    def one_segment(step, carry):
        row, image = step // images, step % images
        length = len_ref[row, image]
        first = segment_start(len_ref, row, image)
        pick = picker(TEXT_K, text_rows, text_dev, slots, first, length)
        at = pl.multiple_of(image * PATCHES_IMG, PATCHES_IMG)
        text = dot_nn(pick, txt[row]).astype(BF16)
        compact = jnp.concatenate([pat[row, pl.ds(at, PATCHES_IMG), :], text], axis=0)
        text_do = dot_nn(pick[:TEXT_MOST], dtxt[row]).astype(BF16)
        d_out = jnp.concatenate([dpat[row, pl.ds(at, PATCHES_IMG), :], text_do], axis=0)
        d_scores, grads = attend_back(compact, d_out, SEG_Q, SEG_K, PATCHES_IMG + length)
        dbias_ref[...] = dbias_ref[...] + d_scores
        gpat[row, pl.ds(at, PATCHES_IMG), :] = grads[:PATCHES_IMG]
        gtxt[row] = gtxt[row] + dot_tn(pick[:TEXT_MOST], grads[PATCHES_IMG:])
        return carry

    lax.fori_loop(0, rows * images, one_segment, 0)
    pad_q = slots // 4
    pad_k = -(-pad_q // 128) * 128
    for row in range(rows):
        first = segment_start(len_ref, row, images)
        pick = picker(pad_k, text_rows, text_dev, slots, first, pad_q)
        compact = dot_nn(pick, txt[row]).astype(BF16)
        d_out = dot_nn(pick[:pad_q], dtxt[row]).astype(BF16)
        d_scores, grads = attend_back(compact, d_out, pad_q, pad_k, pad_q)
        dbias_ref[:pad_q, :pad_k] = dbias_ref[:pad_q, :pad_k] + d_scores
        gtxt[row] = gtxt[row] + dot_tn(pick[:pad_q], grads)
    for row in range(rows):
        for place in range(seq_count):
            source = place ^ me_ref[0]
            dqkv_ref[source, row, 0:patch_dev, :] = gpat[
                row, place * patch_dev : (place + 1) * patch_dev, :
            ]
            low = place * TEXT_PITCH
            dqkv_ref[source, row, patch_dev : patch_dev + text_dev, :] = gtxt[
                row, low : low + text_dev, :
            ].astype(BF16)


SMEM = pl.BlockSpec(memory_space=pltpu.SMEM)
VMEM = pl.BlockSpec(memory_space=pltpu.VMEM)


def call(kernel, out_shape, in_specs, scratch=(), flops=0, bytes_accessed=0):
    single = not isinstance(out_shape, (tuple, list))
    return pl.pallas_call(
        kernel,
        out_shape=out_shape,
        in_specs=in_specs,
        out_specs=VMEM if single else [VMEM] * len(out_shape),
        scratch_shapes=list(scratch),
        cost_estimate=pl.CostEstimate(
            flops=flops, bytes_accessed=bytes_accessed, transcendentals=0
        ),
        compiler_params=pltpu.CompilerParams(vmem_limit_bytes=48 << 20),
        interpret=INTERPRET,
    )


def local(
    patch_features, text_embeds, text_lengths, w_in, b_in, gain_attn, w_query, w_key, w_value,
    w_out, gain_ffn, w_gate, w_up, w_down, position_bias, d_patch, d_text,
):
    seq_count, dp_count = lax.axis_size("seq"), lax.axis_size("dp")
    dev_count = seq_count * dp_count
    seq_index, dp_index = lax.axis_index("seq"), lax.axis_index("dp")
    rows, patch_dev, vit = patch_features.shape
    text_dev = text_embeds.shape[1]
    tok = patch_dev + text_dev
    mine = rows * tok
    d_model = text_embeds.shape[2]
    cols = w_in.shape[1]
    images = text_lengths.shape[1]
    slots = text_dev * seq_count
    seq_high = [("seq", bit) for bit in range(seq_count.bit_length() - 2, 1, -1)]
    near, core = ("seq", 1), ("seq", 0)
    dp_bits = [("dp", bit) for bit in range(dp_count.bit_length() - 1)]
    every = dp_bits + seq_high + [near, core]
    both = ("dp", "seq")

    bias_count = position_bias.shape[0]
    extra = jnp.zeros((cols, 128), BF16)
    extra = extra.at[:, 0].set(b_in).at[:, 1].set(gain_attn).at[:, 2].set(gain_ffn)
    extra = extra.at[:bias_count, 3].set(position_bias)
    pack = jnp.concatenate([w_in.T, extra], axis=1)
    wide = vit + 128
    half_in = wide // 256 * 128
    in_low = gather(pack[:, :half_in], seq_high + dp_bits + [near, core], True)
    in_high = gather(pack[:, half_in:], seq_high + [near] + dp_bits + [core], True)

    per_head = dev_count // HEADS
    twins = seq_count // HEADS
    head = seq_index // twins
    twin = seq_index % twins
    place_in_head = dp_index * twins + twin
    row_count = rows // twins
    three = jnp.concatenate([w_query.T, w_key.T, w_value.T], axis=0)

    def to_rank(which_head, place):
        return (place // twins) * seq_count + which_head * twins + place % twins

    def rounds(turn, back):
        pairs = []
        for which_head in range(HEADS):
            for i in range(per_head):
                owner = which_head * per_head + i
                user = to_rank(which_head, (i + turn) % per_head)
                pairs.append((user, owner) if back else (owner, user))
        return pairs

    pieces = jnp.stack([lax.ppermute(three, both, rounds(turn, False)) for turn in range(per_head)])
    pieces = pieces.reshape(per_head, 3, cols, d_model)
    ordered = [
        lax.dynamic_index_in_dim(pieces, (place_in_head - i) % per_head, 0, keepdims=False)
        for i in range(per_head)
    ]
    w_head = jnp.stack(ordered, axis=1).reshape(3 * HEAD_DIM, d_model)

    ff_order = seq_high + dp_bits
    units = w_gate.shape[1]
    down_out = jnp.transpose(w_down.reshape(dev_count, units, cols), (0, 2, 1))
    down_in = lax.all_to_all(down_out, both, 0, 0, tiled=True).reshape(d_model, units)
    full_gate = gather(w_gate.T, ff_order, False)
    full_up = gather(w_up.T, ff_order, False)
    full_down = gather(down_in.T, ff_order, False)
    full_out = gather(w_out.T, seq_high + [near] + dp_bits + [core], True)

    features = patch_features.reshape(rows * patch_dev, vit)
    ones = jnp.zeros((rows * patch_dev, 128), BF16).at[:, 0].set(1)
    features_more = jnp.concatenate([features, ones], axis=1)
    patch_rows = dot_nt(features_more[:, :half_in], in_low) + dot_nt(
        features_more[:, half_in:], in_high
    )
    units_eye = jnp.eye(8, 128, dtype=BF16)
    small = dot_nt(units_eye, in_high[:, wide - half_in - 128 :])
    gain_one, gain_two = small[1], small[2]
    table = small[3].reshape(dev_count, cols)[:, :bias_count].reshape(BUCKETS, HEADS)
    my_table = lax.dynamic_slice_in_dim(table, head, 1, 1).reshape(1, BUCKETS)
    resid = jnp.concatenate(
        [patch_rows.reshape(rows, patch_dev, d_model), text_embeds.astype(F32)], axis=1
    ).reshape(mine, d_model)
    normed_one = rms_norm(resid, gain_one).astype(BF16)
    half = d_model // 2
    order_low = seq_high + [near, core]
    order_high = [near] + seq_high + [core]
    all_low = gather(normed_one[:, :half], order_low, False)
    all_high = gather(normed_one[:, half:], order_high, False)

    def my_rows(array):
        view = array.reshape(seq_count, rows, tok, array.shape[1])
        view = lax.dynamic_slice_in_dim(view, twin * row_count, row_count, 1)
        return view.reshape(seq_count * row_count * tok, array.shape[1])

    if twins > 1:
        all_low, all_high = my_rows(all_low), my_rows(all_high)
    qkv = (dot_nt(all_low, w_head[:, :half]) + dot_nt(all_high, w_head[:, half:])).astype(BF16)
    qkv = qkv.reshape(seq_count, row_count, tok, 3 * HEAD_DIM)
    lengths = lax.dynamic_slice_in_dim(text_lengths, twin * row_count, row_count, 0)
    me = seq_index.reshape(1).astype(jnp.int32)
    dims = (row_count, images, patch_dev, text_dev, slots)
    bias = call(
        bias_kernel, jax.ShapeDtypeStruct((SEG_Q, SEG_K), F32), [SMEM], (), 1 << 24, 1 << 20
    )(my_table)
    text_rows = seq_count * TEXT_PITCH
    patches = seq_count * patch_dev
    packed_shape = jax.ShapeDtypeStruct((seq_count, tok, row_count * HEAD_DIM), BF16)
    mixed = call(
        lambda *refs: forward_kernel(dims, *refs),
        packed_shape,
        [SMEM, SMEM, VMEM, VMEM],
        (
            pltpu.VMEM((row_count, patches, 3 * HEAD_DIM), BF16),
            pltpu.VMEM((row_count, text_rows, 3 * HEAD_DIM), BF16),
            pltpu.VMEM((row_count, patches, HEAD_DIM), BF16),
            pltpu.VMEM((row_count, text_rows, HEAD_DIM), F32),
        ),
        1 << 30,
        4 << 20,
    )(me, lengths, bias, qkv)
    mixed = lax.all_to_all(mixed, "seq", 0, 0, tiled=True)
    mixed = mixed.reshape(HEADS, twins, tok, row_count, HEAD_DIM)
    attn_out = jnp.transpose(mixed, (1, 3, 2, 0, 4)).reshape(mine, d_model)
    resid_one = resid + dot_nt(attn_out, full_out)
    normed_two = rms_norm(resid_one, gain_two).astype(BF16)
    team = [near, core]
    upstream = jnp.concatenate([d_patch, d_text], axis=1).reshape(mine, d_model)
    team_up = gather(upstream, team, False)
    team_normed = gather(normed_two, team, False)
    gate_pre = dot_nt(team_normed, full_gate)
    up_pre = dot_nt(team_normed, full_up)
    hidden, gated_back = jax.vjp(gated_unit, gate_pre, up_pre)
    hidden = hidden.astype(BF16)
    out_part = dot_nn(hidden, full_down)
    result = resid_one + scatter_add(out_part, [core, near], team, False, (core,))
    result = result.astype(BF16).reshape(rows, tok, d_model)

    d_hidden = dot_nt(team_up, full_down)
    d_gate, d_up = gated_back(d_hidden)
    d_gate, d_up = d_gate.astype(BF16), d_up.astype(BF16)
    d_normed_two = scatter_add(
        dot_nn(d_gate, full_gate) + dot_nn(d_up, full_up), [core, near], team, False, (core,)
    )
    back = ff_order[::-1]
    grad_down = scatter_add(dot_tn(hidden, team_up), back, ff_order, False)
    grad_gate = scatter_add(dot_tn(d_gate, team_normed), back, ff_order, False)
    grad_up = scatter_add(dot_tn(d_up, team_normed), back, ff_order, False)
    down_back = grad_down.T.reshape(dev_count, cols, units)
    down_back = lax.all_to_all(down_back, both, 0, 0, tiled=True)
    grad_down = jnp.transpose(down_back, (0, 2, 1)).reshape(dev_count * units, cols)

    _, norm_back_two = jax.vjp(rms_norm, resid_one, gain_two)
    d_resid_one, grad_gain_two = norm_back_two(d_normed_two)
    d_resid_one = d_resid_one + upstream.astype(F32)
    d_mix = d_resid_one.astype(BF16)
    grad_out = scatter_add(
        dot_tn(d_mix, attn_out), [core] + dp_bits[::-1] + [near] + seq_high[::-1], every, True
    )
    d_attn = dot_nn(d_mix, full_out).astype(BF16)
    d_attn = d_attn.reshape(twins, row_count, tok, HEADS, HEAD_DIM)
    d_attn = jnp.transpose(d_attn, (3, 0, 2, 1, 4)).reshape(packed_shape.shape)
    d_attn = lax.all_to_all(d_attn, "seq", 0, 0, tiled=True)
    d_qkv, d_bias = call(
        lambda *refs: backward_kernel(dims, *refs),
        (
            jax.ShapeDtypeStruct(qkv.shape, BF16),
            jax.ShapeDtypeStruct((SEG_Q, SEG_K), F32),
        ),
        [SMEM, SMEM, VMEM, VMEM, VMEM],
        (
            pltpu.VMEM((row_count, patches, 3 * HEAD_DIM), BF16),
            pltpu.VMEM((row_count, text_rows, 3 * HEAD_DIM), BF16),
            pltpu.VMEM((row_count, patches, HEAD_DIM), BF16),
            pltpu.VMEM((row_count, text_rows, HEAD_DIM), BF16),
            pltpu.VMEM((row_count, patches, 3 * HEAD_DIM), BF16),
            pltpu.VMEM((row_count, text_rows, 3 * HEAD_DIM), F32),
        ),
        3 << 30,
        8 << 20,
    )(me, lengths, bias, qkv, d_attn)
    d_table = call(
        bucket_kernel, jax.ShapeDtypeStruct((BUCKETS, 128), F32), [VMEM], (), 1 << 25, 1 << 20
    )(d_bias)[:, 0]
    d_qkv = d_qkv.reshape(seq_count * row_count * tok, 3 * HEAD_DIM)
    d_head = jnp.concatenate([dot_tn(d_qkv, all_low), dot_tn(d_qkv, all_high)], axis=1)
    d_head = d_head.reshape(3, per_head, cols, d_model).astype(BF16)
    d_three = 0.0
    for turn in range(per_head):
        piece = lax.dynamic_index_in_dim(
            d_head, (place_in_head - turn) % per_head, 1, keepdims=False
        )
        got = lax.ppermute(piece.reshape(3 * cols, d_model), both, rounds(turn, True))
        d_three = d_three + got.astype(F32)

    def all_rows(array):
        if twins == 1:
            return array
        view = array.reshape(seq_count, row_count, tok, array.shape[1])
        zero = jnp.zeros((seq_count, rows, tok, array.shape[1]), array.dtype)
        view = lax.dynamic_update_slice_in_dim(zero, view, twin * row_count, 1)
        return view.reshape(seq_count * mine, array.shape[1])

    seq_bits = seq_high + [near, core]
    d_normed_one = jnp.concatenate(
        [
            scatter_add(
                all_rows(dot_nn(d_qkv, w_head[:, :half])), order_low[::-1], seq_bits, False
            ),
            scatter_add(
                all_rows(dot_nn(d_qkv, w_head[:, half:])), order_high[::-1], seq_bits, False
            ),
        ],
        axis=1,
    )
    _, norm_back_one = jax.vjp(rms_norm, resid, gain_one)
    d_resid, grad_gain_one = norm_back_one(d_normed_one)
    d_resid = (d_resid + d_resid_one).reshape(rows, tok, d_model)
    text_grad = d_resid[:, patch_dev:]
    d_patch_rows = d_resid[:, :patch_dev].reshape(rows * patch_dev, d_model)
    d_low = d_patch_rows.astype(BF16)
    feature_grad = jnp.concatenate(
        [dot_nn(d_low, in_low), dot_nn(d_low, in_high[:, : vit - half_in])], axis=1
    ).reshape(rows, patch_dev, vit)
    pos_grads = d_table[:, None] * (jnp.arange(HEADS)[None, :] == head).astype(F32)
    pos_grads = jnp.pad(
        pos_grads.reshape(dev_count, bias_count), ((0, 0), (0, cols - bias_count))
    ).reshape(1, d_model)
    small_grads = jnp.concatenate(
        [
            jnp.sum(d_patch_rows, axis=0)[None],
            grad_gain_one[None],
            grad_gain_two[None],
            pos_grads,
            jnp.zeros((12, d_model), F32),
        ],
        axis=0,
    ).astype(BF16)
    left = jnp.concatenate([d_low, small_grads], axis=0)
    right = jnp.concatenate(
        [
            jnp.pad(features, ((0, 0), (0, 128))),
            jnp.pad(jnp.eye(16, 128, dtype=BF16), ((0, 0), (vit, 0))),
        ],
        axis=0,
    )
    in_grads = jnp.concatenate(
        [
            scatter_add(
                dot_tn(left, right[:, :half_in]),
                [core, near] + dp_bits[::-1] + seq_high[::-1],
                every,
                True,
            ),
            scatter_add(
                dot_tn(left, right[:, half_in:]),
                [core] + dp_bits[::-1] + [near] + seq_high[::-1],
                every,
                True,
            ),
        ],
        axis=1,
    )
    small_out = in_grads[:, vit:]
    d_three = d_three.reshape(3, cols, d_model)
    return (
        result[:, :patch_dev],
        result[:, patch_dev:],
        feature_grad,
        text_grad,
        in_grads[:, :vit].T,
        small_out[:, 0],
        small_out[:, 1],
        d_three[0].T,
        d_three[1].T,
        d_three[2].T,
        grad_out.T,
        small_out[:, 2],
        grad_gate.T,
        grad_up.T,
        grad_down,
        small_out[:bias_count, 3],
    )


def solution(mesh):
    token = P("dp", "seq", None)
    matrix = P(None, ("dp", "seq"))
    vector = P(("dp", "seq"))
    return jax.shard_map(
        local,
        mesh=mesh,
        in_specs=(
            token, token, P("dp", None), matrix, vector, vector, matrix, matrix, matrix, matrix,
            vector, matrix, matrix, matrix, vector, token, token,
        ),
        out_specs=(
            token, token, token, token, matrix, vector, vector, matrix, matrix, matrix, matrix,
            vector, matrix, matrix, matrix, vector,
        ),
        check_vma=False,
    )
```

```python
import jax
import jax.numpy as jnp
from jax import lax
from jax.experimental import pallas as pl
from jax.experimental.pallas import tpu as pltpu
from jax.sharding import PartitionSpec as P

HEADS = 16
HEAD_DIM = 64
BUCKETS = 32
PATCHES_IMG = 256
TEXT_MOST = 192

EPSILON = 1e-06
MASKED = -1e30
STARTS = (0, 1, 2, 3, 4, 5, 6, 7, 8, 12, 16, 23, 32, 46, 64, 91)
BF16 = jnp.bfloat16
F32 = jnp.float32
INTERPRET = False

SEG_Q = PATCHES_IMG + TEXT_MOST
SEG_K = 2 * PATCHES_IMG
TEXT_K = SEG_K - PATCHES_IMG
TEXT_PITCH = 32


def dot_nt(left, right):
    return lax.dot_general(left, right, (((1,), (1,)), ((), ())), preferred_element_type=F32)


def dot_nn(left, right):
    return lax.dot_general(left, right, (((1,), (0,)), ((), ())), preferred_element_type=F32)


def dot_tn(left, right):
    return lax.dot_general(left, right, (((0,), (0,)), ((), ())), preferred_element_type=F32)


def rms_norm(values, gain):
    return values * lax.rsqrt(jnp.mean(values * values, axis=-1, keepdims=True) + EPSILON) * gain


def gelu_tanh(values):
    return (
        0.5
        * values
        * (1.0 + jnp.tanh(0.7978845608 * (values + 0.044715 * values * values * values)))
    )


def gated_unit(gate_pre, up_pre):
    return gelu_tanh(gate_pre) * up_pre


def swap(array, step):
    axis, bit = step
    count = lax.axis_size(axis)
    return lax.ppermute(array, axis, [(i, i ^ (1 << bit)) for i in range(count)])


def my_bit(step):
    axis, bit = step
    return (lax.axis_index(axis) >> bit) & 1


def rank(step):
    return (1000 if step[0] == "dp" else 0) + step[1]


def after(value, signal):
    return value + (signal[(0,) * signal.ndim] * 0).astype(value.dtype)


def gather(block, order, absolute, hold=None):
    have = []
    stages = []
    for number, step in enumerate(order):
        if hold and number in hold:
            block = after(block, hold[number])
        other = swap(block, step)
        at = sum(1 for done in have if rank(done) > rank(step))
        mine = block
        if absolute:
            bit = my_bit(step) == 1
            mine, other = jnp.where(bit, other, mine), jnp.where(bit, mine, other)
        outer = 2**at
        size = block.shape[0] // outer
        parts = []
        for which in range(outer):
            parts += [mine[which * size : (which + 1) * size], other[which * size : (which + 1) * size]]
        have.append(step)
        block = jnp.concatenate(parts, axis=0)
        stages.append(block)
    return stages


def scatter_add(grads, order, every, absolute, wide=(), hold=None):
    every = sorted(every, key=rank, reverse=True)
    width = grads.shape[1]
    stages = []
    for number, step in enumerate(order):
        at = every.index(step)
        rows = grads.shape[0] // 2
        if absolute:
            view = grads.reshape(2**at, 2, rows // 2**at, width)
            bit = my_bit(step)
            keep = lax.dynamic_slice_in_dim(view, bit, 1, 1).reshape(rows, width)
            send = lax.dynamic_slice_in_dim(view, 1 - bit, 1, 1).reshape(rows, width)
        elif at == 0:
            keep, send = grads[:rows], grads[rows:]
        else:
            view = grads.reshape(2**at, 2, rows // 2**at, width)
            keep, send = view[:, 0].reshape(rows, width), view[:, 1].reshape(rows, width)
        if hold and number in hold:
            send = after(send, hold[number])
        kind = F32 if step in wide else BF16
        got = swap(send.astype(kind), step)
        grads = keep.astype(F32) + got.astype(F32)
        every = [other for other in every if other != step]
        stages.append(grads)
    return stages


def bias_kernel(table_ref, out_ref):
    delta = lax.broadcasted_iota(jnp.int32, out_ref.shape, 0) - lax.broadcasted_iota(
        jnp.int32, out_ref.shape, 1
    )
    value = jnp.full(out_ref.shape, table_ref[0, BUCKETS - 1], F32)
    for which in range(14, 0, -1):
        value = jnp.where(delta > -STARTS[which + 1], table_ref[0, 16 + which], value)
    for which in range(16):
        value = jnp.where(delta >= STARTS[which], table_ref[0, which], value)
    out_ref[...] = value


def bucket_kernel(d_ref, out_ref):
    shape = d_ref.shape
    delta = lax.broadcasted_iota(jnp.int32, shape, 0) - lax.broadcasted_iota(jnp.int32, shape, 1)
    values = d_ref[...]
    rows = []
    for which in range(BUCKETS):
        low = STARTS[which % 16]
        high = STARTS[which % 16 + 1] if which % 16 < 15 else 1 << 20
        if which < 16:
            inside = (delta >= low) & (delta < high)
        else:
            inside = (delta <= -max(low, 1)) & (delta > -high)
        rows.append(jnp.sum(jnp.where(inside, values, 0.0), axis=0, keepdims=True))
    sums = jnp.sum(jnp.concatenate(rows, axis=0), axis=1, keepdims=True)
    out_ref[...] = jnp.broadcast_to(sums, out_ref.shape)


def unpack(seq_count, where, row, pat_ref, txt_ref, patch_dev, text_dev, lanes):
    tail = TEXT_PITCH - text_dev
    for place in range(seq_count):
        block = where(place)
        patches = block[0:patch_dev, lanes]
        text = block[patch_dev : patch_dev + text_dev, lanes]
        pat_ref[row, place * patch_dev : (place + 1) * patch_dev, :] = patches
        txt_ref[row, place * TEXT_PITCH : place * TEXT_PITCH + text_dev, :] = text
        if tail:
            txt_ref[row, place * TEXT_PITCH + text_dev : (place + 1) * TEXT_PITCH, :] = jnp.zeros(
                (tail, text.shape[1]), text.dtype
            )


def picker(count, text_rows, text_dev, slot_count, first, length):
    shape = (count, text_rows)
    column = lax.broadcasted_iota(jnp.int32, shape, 1)
    inner = column & (TEXT_PITCH - 1)
    slot = (column // TEXT_PITCH) * text_dev + inner
    fill = jnp.where(slot >= slot_count // 2, slot - slot_count // 2, slot + slot_count // 2)
    line = lax.broadcasted_iota(jnp.int32, shape, 0)
    hit = (fill == first + line) & (line < length) & (inner < text_dev)
    return hit.astype(F32).astype(BF16)


def softmax(scores):
    top = jnp.max(scores, axis=-1, keepdims=True)
    expd = jnp.exp(scores - top)
    return expd / jnp.sum(expd, axis=-1, keepdims=True)


def segment_start(len_ref, row, which):
    return lax.fori_loop(0, which, lambda at, total: total + len_ref[row, at], jnp.int32(0))


class Halves:
    def __init__(self, me, own_ref, other_ref, row):
        self.me, self.own, self.other, self.row = me, own_ref, other_ref, row

    def at(self, place):
        apart = place ^ self.me
        return apart & 1, apart >> 1

    def __call__(self, place):
        odd, index = self.at(place)
        return jnp.where(odd == 1, self.other[index, self.row], self.own[index, self.row])


def forward_kernel(dims, me_ref, len_ref, bias_ref, own_ref, other_ref, o_ref, pat, txt, opat, otxt):
    rows, images, patch_dev, text_dev, slots = dims
    seq_count = 2 * own_ref.shape[0]
    text_rows = seq_count * TEXT_PITCH
    for row in range(rows):
        unpack(
            seq_count, Halves(me_ref[0], own_ref, other_ref, row),
            row, pat, txt, patch_dev, text_dev, slice(None),
        )
    otxt[...] = jnp.zeros_like(otxt)

    def attend(compact, queries, keys, length):
        q = compact[:queries, :HEAD_DIM]
        k = compact[:keys, HEAD_DIM : 2 * HEAD_DIM]
        v = compact[:keys, 2 * HEAD_DIM :]
        scores = dot_nt(q, k) + bias_ref[:queries, :keys]
        column = lax.broadcasted_iota(jnp.int32, scores.shape, 1)
        probs = softmax(jnp.where(column < length, scores, MASKED)).astype(BF16)
        return dot_nn(probs, v).astype(BF16)

    def one_segment(step, carry):
        row, image = step // images, step % images
        length = len_ref[row, image]
        first = segment_start(len_ref, row, image)
        pick = picker(TEXT_K, text_rows, text_dev, slots, first, length)
        text = dot_nn(pick, txt[row]).astype(BF16)
        at = pl.multiple_of(image * PATCHES_IMG, PATCHES_IMG)
        compact = jnp.concatenate([pat[row, pl.ds(at, PATCHES_IMG), :], text], axis=0)
        out = attend(compact, SEG_Q, SEG_K, PATCHES_IMG + length)
        opat[row, pl.ds(at, PATCHES_IMG), :] = out[:PATCHES_IMG]
        otxt[row] = otxt[row] + dot_tn(pick[:TEXT_MOST], out[PATCHES_IMG:])
        return carry

    lax.fori_loop(0, rows * images, one_segment, 0)
    pad_q = slots // 4
    pad_k = -(-pad_q // 128) * 128
    for row in range(rows):
        first = segment_start(len_ref, row, images)
        pick = picker(pad_k, text_rows, text_dev, slots, first, pad_q)
        compact = dot_nn(pick, txt[row]).astype(BF16)
        out = attend(compact, pad_q, pad_k, pad_q)
        otxt[row] = otxt[row] + dot_tn(pick[:pad_q], out)
    for place in range(seq_count):
        o_ref[place, 0:patch_dev, :] = jnp.concatenate(
            [opat[row, place * patch_dev : (place + 1) * patch_dev, :] for row in range(rows)],
            axis=1,
        )
        low = place * TEXT_PITCH
        o_ref[place, patch_dev : patch_dev + text_dev, :] = jnp.concatenate(
            [otxt[row, low : low + text_dev, :].astype(BF16) for row in range(rows)], axis=1
        )


def backward_kernel(
    dims, me_ref, len_ref, bias_ref, own_ref, other_ref, do_ref, down_ref, dother_ref, dbias_ref,
    pat, txt, dpat, dtxt, gpat, gtxt,
):
    rows, images, patch_dev, text_dev, slots = dims
    seq_count = 2 * own_ref.shape[0]
    text_rows = seq_count * TEXT_PITCH
    for row in range(rows):
        unpack(
            seq_count, Halves(me_ref[0], own_ref, other_ref, row),
            row, pat, txt, patch_dev, text_dev, slice(None),
        )
        unpack(
            seq_count, lambda place: do_ref.at[place],
            row, dpat, dtxt, patch_dev, text_dev,
            slice(row * HEAD_DIM, (row + 1) * HEAD_DIM),
        )
    gtxt[...] = jnp.zeros_like(gtxt)
    dbias_ref[...] = jnp.zeros_like(dbias_ref)

    def attend_back(compact, d_out, queries, keys, length):
        q = compact[:queries, :HEAD_DIM]
        k = compact[:keys, HEAD_DIM : 2 * HEAD_DIM]
        v = compact[:keys, 2 * HEAD_DIM :]
        scores = dot_nt(q, k) + bias_ref[:queries, :keys]
        column = lax.broadcasted_iota(jnp.int32, scores.shape, 1)
        probs = softmax(jnp.where(column < length, scores, MASKED))
        d_probs = dot_nt(d_out, v)
        centre = jnp.sum(d_probs * probs, axis=-1, keepdims=True)
        d_scores = probs * (d_probs - centre)
        d_low = d_scores.astype(BF16)
        d_q = dot_nn(d_low, k).astype(BF16)
        d_k = dot_tn(d_low, q).astype(BF16)
        d_v = dot_tn(probs.astype(BF16), d_out).astype(BF16)
        return d_scores, jnp.concatenate([d_q, d_k[:queries], d_v[:queries]], axis=1)

    def one_segment(step, carry):
        row, image = step // images, step % images
        length = len_ref[row, image]
        first = segment_start(len_ref, row, image)
        pick = picker(TEXT_K, text_rows, text_dev, slots, first, length)
        at = pl.multiple_of(image * PATCHES_IMG, PATCHES_IMG)
        text = dot_nn(pick, txt[row]).astype(BF16)
        compact = jnp.concatenate([pat[row, pl.ds(at, PATCHES_IMG), :], text], axis=0)
        text_do = dot_nn(pick[:TEXT_MOST], dtxt[row]).astype(BF16)
        d_out = jnp.concatenate([dpat[row, pl.ds(at, PATCHES_IMG), :], text_do], axis=0)
        d_scores, grads = attend_back(compact, d_out, SEG_Q, SEG_K, PATCHES_IMG + length)
        dbias_ref[...] = dbias_ref[...] + d_scores
        gpat[row, pl.ds(at, PATCHES_IMG), :] = grads[:PATCHES_IMG]
        gtxt[row] = gtxt[row] + dot_tn(pick[:TEXT_MOST], grads[PATCHES_IMG:])
        return carry

    lax.fori_loop(0, rows * images, one_segment, 0)
    pad_q = slots // 4
    pad_k = -(-pad_q // 128) * 128
    for row in range(rows):
        first = segment_start(len_ref, row, images)
        pick = picker(pad_k, text_rows, text_dev, slots, first, pad_q)
        compact = dot_nn(pick, txt[row]).astype(BF16)
        d_out = dot_nn(pick[:pad_q], dtxt[row]).astype(BF16)
        d_scores, grads = attend_back(compact, d_out, pad_q, pad_k, pad_q)
        dbias_ref[:pad_q, :pad_k] = dbias_ref[:pad_q, :pad_k] + d_scores
        gtxt[row] = gtxt[row] + dot_tn(pick[:pad_q], grads)
    for row in range(rows):
        for place in range(seq_count):
            odd, index = Halves(me_ref[0], own_ref, other_ref, row).at(place)
            low = place * TEXT_PITCH
            patches = gpat[row, place * patch_dev : (place + 1) * patch_dev, :]
            text = gtxt[row, low : low + text_dev, :].astype(BF16)

            def put(target):
                target[index, row, 0:patch_dev, :] = patches
                target[index, row, patch_dev : patch_dev + text_dev, :] = text

            pl.when(odd == 0)(lambda: put(down_ref))
            pl.when(odd == 1)(lambda: put(dother_ref))


SMEM = pl.BlockSpec(memory_space=pltpu.SMEM)
VMEM = pl.BlockSpec(memory_space=pltpu.VMEM)


def call(kernel, out_shape, in_specs, scratch=(), flops=0, bytes_accessed=0, vmem=16):
    single = not isinstance(out_shape, (tuple, list))
    return pl.pallas_call(
        kernel,
        out_shape=out_shape,
        in_specs=in_specs,
        out_specs=VMEM if single else [VMEM] * len(out_shape),
        scratch_shapes=list(scratch),
        cost_estimate=pl.CostEstimate(
            flops=flops, bytes_accessed=bytes_accessed, transcendentals=0
        ),
        compiler_params=pltpu.CompilerParams(vmem_limit_bytes=vmem << 20),
        interpret=INTERPRET,
    )


def local(
    patch_features, text_embeds, text_lengths, w_in, b_in, gain_attn, w_query, w_key, w_value,
    w_out, gain_ffn, w_gate, w_up, w_down, position_bias, d_patch, d_text,
):
    seq_count, dp_count = lax.axis_size("seq"), lax.axis_size("dp")
    dev_count = seq_count * dp_count
    seq_index, dp_index = lax.axis_index("seq"), lax.axis_index("dp")
    rows, patch_dev, vit = patch_features.shape
    text_dev = text_embeds.shape[1]
    tok = patch_dev + text_dev
    mine = rows * tok
    d_model = text_embeds.shape[2]
    cols = w_in.shape[1]
    images = text_lengths.shape[1]
    slots = text_dev * seq_count
    core, near, team_bit = ("seq", 0), ("seq", 1), ("seq", 2)
    seq_high = [("seq", bit) for bit in range(seq_count.bit_length() - 2, 1, -1)]
    dp_bits = [("dp", bit) for bit in range(dp_count.bit_length() - 1)]
    every = dp_bits + seq_high + [near, core]
    both = ("dp", "seq")

    bias_count = position_bias.shape[0]
    pack = jnp.concatenate(
        [
            w_in,
            b_in[None],
            gain_attn[None],
            gain_ffn[None],
            jnp.pad(position_bias, (0, cols - bias_count))[None],
            jnp.zeros((124, cols), BF16),
        ],
        axis=0,
    ).T
    wide = vit + 128
    half_in = wide // 256 * 128
    in_low_stages = gather(pack[:, :half_in], seq_high + dp_bits + [near, core], True)
    in_high_stages = gather(pack[:, half_in:], seq_high + [near] + dp_bits + [core], True)
    in_low, in_high = in_low_stages[-1], in_high_stages[-1]
    in_part = in_low_stages[len(seq_high) - 1]

    per_head = dev_count // HEADS
    twins = seq_count // HEADS
    head = seq_index // twins
    twin = seq_index % twins
    place_in_head = dp_index * twins + twin
    row_count = rows // twins
    three = jnp.concatenate([w_query.T, w_key.T, w_value.T], axis=0)
    three = after(three, in_part)

    def to_rank(which_head, place):
        return (place // twins) * seq_count + which_head * twins + place % twins

    def rounds(turn, back):
        pairs = []
        for which_head in range(HEADS):
            for i in range(per_head):
                owner = which_head * per_head + i
                user = to_rank(which_head, (i + turn) % per_head)
                pairs.append((user, owner) if back else (owner, user))
        return pairs

    pieces = jnp.stack([lax.ppermute(three, both, rounds(turn, False)) for turn in range(per_head)])
    pieces = pieces.reshape(per_head, 3, cols, d_model)
    ordered = [
        lax.dynamic_index_in_dim(pieces, (place_in_head - i) % per_head, 0, keepdims=False)
        for i in range(per_head)
    ]
    w_head = jnp.stack(ordered, axis=1).reshape(3 * HEAD_DIM, d_model)

    team = [team_bit, core]
    ff_high = [step for step in seq_high if step != team_bit]
    ff_order = ff_high + [near] + dp_bits
    ff_other = ff_high + dp_bits + [near]
    units = w_gate.shape[1]
    full_gate = gather(w_gate.T, ff_order, False, {0: in_low})[-1]
    full_up = gather(w_up.T, ff_order, False, {0: in_low})[-1]
    down_out = jnp.transpose(w_down.reshape(dev_count, units, cols), (0, 2, 1))
    down_in = lax.all_to_all(after(down_out, in_low), both, 0, 0, tiled=True)
    full_down = gather(down_in.reshape(d_model, units).T, ff_other, False)[-1]

    features = patch_features.reshape(rows * patch_dev, vit)
    ones = jnp.zeros((rows * patch_dev, 128), BF16).at[:, 0].set(1)
    features_more = jnp.concatenate([features, ones], axis=1)
    patch_rows = dot_nt(features_more[:, :half_in], in_low) + dot_nt(
        features_more[:, half_in:], in_high
    )
    units_eye = jnp.eye(8, 128, dtype=BF16)
    small = dot_nt(units_eye, in_high[:, wide - half_in - 128 :])
    gain_one, gain_two = small[1], small[2]
    table = small[3].reshape(dev_count, cols)[:, :bias_count].reshape(BUCKETS, HEADS)
    my_table = lax.dynamic_slice_in_dim(table, head, 1, 1).reshape(1, BUCKETS)
    resid = jnp.concatenate(
        [patch_rows.reshape(rows, patch_dev, d_model), text_embeds.astype(F32)], axis=1
    ).reshape(mine, d_model)
    normed_one = rms_norm(resid, gain_one).astype(BF16)
    half = d_model // 2
    order_low = seq_high + [near]
    order_high = [near] + seq_high
    low_stages = gather(normed_one[:, :half], order_low, False)
    high_stages = gather(normed_one[:, half:], order_high, False)
    chips = seq_count // 2

    def my_rows(array):
        if twins == 1:
            return array
        view = array.reshape(chips, rows, tok, array.shape[1])
        view = lax.dynamic_slice_in_dim(view, twin * row_count, row_count, 1)
        return view.reshape(chips * row_count * tok, array.shape[1])

    own_low, own_high = low_stages[-1], high_stages[-1]
    normed_pairs = [
        (my_rows(own_low), my_rows(own_high)),
        (my_rows(swap(own_low, core)), my_rows(swap(own_high, core))),
    ]
    qkv = [
        (dot_nt(low, w_head[:, :half]) + dot_nt(high, w_head[:, half:]))
        .astype(BF16)
        .reshape(chips, row_count, tok, 3 * HEAD_DIM)
        for low, high in normed_pairs
    ]
    full_out = gather(
        w_out.T, seq_high + [near] + dp_bits + [core], True, {0: low_stages[len(seq_high) - 1]}
    )[-1]
    lengths = lax.dynamic_slice_in_dim(text_lengths, twin * row_count, row_count, 0)
    me = seq_index.reshape(1).astype(jnp.int32)
    dims = (row_count, images, patch_dev, text_dev, slots)
    bias = call(
        bias_kernel, jax.ShapeDtypeStruct((SEG_Q, SEG_K), F32), [SMEM], (), 1 << 24, 1 << 20, 8
    )(my_table)
    text_rows = seq_count * TEXT_PITCH
    patches = seq_count * patch_dev
    packed_shape = jax.ShapeDtypeStruct((seq_count, tok, row_count * HEAD_DIM), BF16)
    mixed = call(
        lambda *refs: forward_kernel(dims, *refs),
        packed_shape,
        [SMEM, SMEM, VMEM, VMEM, VMEM],
        (
            pltpu.VMEM((row_count, patches, 3 * HEAD_DIM), BF16),
            pltpu.VMEM((row_count, text_rows, 3 * HEAD_DIM), BF16),
            pltpu.VMEM((row_count, patches, HEAD_DIM), BF16),
            pltpu.VMEM((row_count, text_rows, HEAD_DIM), F32),
        ),
        1 << 30,
        4 << 20,
        20,
    )(me, lengths, bias, *qkv)
    mixed = lax.all_to_all(mixed, "seq", 0, 0, tiled=True)
    mixed = mixed.reshape(HEADS, twins, tok, row_count, HEAD_DIM)
    attn_out = jnp.transpose(mixed, (1, 3, 2, 0, 4)).reshape(mine, d_model)
    resid_one = resid + dot_nt(attn_out, full_out)
    normed_two = rms_norm(resid_one, gain_two).astype(BF16)
    upstream = jnp.concatenate([d_patch, d_text], axis=1).reshape(mine, d_model)
    team_up = gather(upstream, team, False, {0: own_low})[-1]
    team_normed = gather(normed_two, team, False)[-1]
    gate_pre = dot_nt(team_normed, full_gate)
    up_pre = dot_nt(team_normed, full_up)
    hidden, gated_back = jax.vjp(gated_unit, gate_pre, up_pre)
    hidden = hidden.astype(BF16)

    d_hidden = dot_nt(team_up, full_down)
    d_gate, d_up = gated_back(d_hidden)
    d_gate, d_up = d_gate.astype(BF16), d_up.astype(BF16)
    d_normed_part = dot_nn(d_gate, full_gate) + dot_nn(d_up, full_up)
    d_normed_two = scatter_add(d_normed_part, [core, team_bit], team, False, (core,))[-1]
    _, norm_back_two = jax.vjp(rms_norm, resid_one, gain_two)
    d_resid_one, grad_gain_two = norm_back_two(d_normed_two)
    d_resid_one = d_resid_one + upstream.astype(F32)
    d_mix = d_resid_one.astype(BF16)
    d_attn = dot_nn(d_mix, full_out).astype(BF16)
    d_attn = d_attn.reshape(twins, row_count, tok, HEADS, HEAD_DIM)
    d_attn = jnp.transpose(d_attn, (3, 0, 2, 1, 4)).reshape(packed_shape.shape)
    d_attn = lax.all_to_all(d_attn, "seq", 0, 0, tiled=True)
    half_shape = jax.ShapeDtypeStruct(qkv[0].shape, BF16)
    d_own, d_other, d_bias = call(
        lambda *refs: backward_kernel(dims, *refs),
        (half_shape, half_shape, jax.ShapeDtypeStruct((SEG_Q, SEG_K), F32)),
        [SMEM, SMEM, VMEM, VMEM, VMEM, VMEM],
        (
            pltpu.VMEM((row_count, patches, 3 * HEAD_DIM), BF16),
            pltpu.VMEM((row_count, text_rows, 3 * HEAD_DIM), BF16),
            pltpu.VMEM((row_count, patches, HEAD_DIM), BF16),
            pltpu.VMEM((row_count, text_rows, HEAD_DIM), BF16),
            pltpu.VMEM((row_count, patches, 3 * HEAD_DIM), BF16),
            pltpu.VMEM((row_count, text_rows, 3 * HEAD_DIM), F32),
        ),
        3 << 30,
        8 << 20,
        28,
    )(me, lengths, bias, *qkv, d_attn)
    d_qkv = [
        array.reshape(chips * row_count * tok, 3 * HEAD_DIM) for array in (d_own, d_other)
    ]

    ff_hold = {1: d_own}
    grad_gate = scatter_add(
        dot_tn(after(d_gate, d_normed_part), team_normed).astype(BF16),
        ff_order[::-1], ff_order, False, (), ff_hold,
    )[-1]
    grad_up = scatter_add(
        dot_tn(after(d_up, d_normed_part), team_normed).astype(BF16),
        ff_order[::-1], ff_order, False, (), ff_hold,
    )[-1]
    grad_down = scatter_add(
        dot_tn(after(hidden, d_normed_part), team_up).astype(BF16),
        ff_other[::-1], ff_order, False, (), ff_hold,
    )[-1]
    down_back = grad_down.T.reshape(dev_count, cols, units)
    down_back = lax.all_to_all(down_back, both, 0, 0, tiled=True)
    grad_down = jnp.transpose(down_back, (0, 2, 1)).reshape(dev_count * units, cols)
    out_part = dot_nn(after(hidden, d_normed_part), full_down)
    result = scatter_add(
        out_part, [core, team_bit], team, False, (core,), {0: d_normed_two, 1: d_own}
    )[-1]
    result = (resid_one + result).astype(BF16).reshape(rows, tok, d_model)

    d_table = call(
        bucket_kernel, jax.ShapeDtypeStruct((BUCKETS, 128), F32), [VMEM], (), 1 << 25, 1 << 20, 8
    )(d_bias)[:, 0]

    def all_rows(array):
        if twins == 1:
            return array
        view = array.reshape(chips, row_count, tok, array.shape[1])
        zero = jnp.zeros((chips, rows, tok, array.shape[1]), array.dtype)
        view = lax.dynamic_update_slice_in_dim(zero, view, twin * row_count, 1)
        return view.reshape(chips * mine, array.shape[1])

    chip_bits = seq_high + [near]

    def d_normed(weights, order):
        other = all_rows(dot_nn(d_qkv[1], weights).astype(BF16))
        own = all_rows(dot_nn(d_qkv[0], weights))
        return scatter_add(
            own + swap(other, core).astype(F32), order, chip_bits, False
        )

    low_sums = d_normed(w_head[:, :half], order_low[::-1])
    high_sums = d_normed(w_head[:, half:], order_high[::-1])
    d_normed_one = jnp.concatenate([low_sums[-1], high_sums[-1]], axis=1)
    out_order = [core] + dp_bits[::-1] + [near] + seq_high[::-1]
    grad_out = scatter_add(
        dot_tn(after(d_mix, d_attn), attn_out).astype(BF16), out_order, every, True, (), {1: d_own}
    )[-1]

    d_head = jnp.concatenate(
        [
            sum(dot_tn(grads, pair[which]) for grads, pair in zip(d_qkv, normed_pairs))
            for which in range(2)
        ],
        axis=1,
    )
    d_head = d_head.reshape(3, per_head, cols, d_model).astype(BF16)
    d_head = after(d_head, low_sums[-1])
    d_three = 0.0
    for turn in range(per_head):
        piece = lax.dynamic_index_in_dim(
            d_head, (place_in_head - turn) % per_head, 1, keepdims=False
        )
        got = lax.ppermute(piece.reshape(3 * cols, d_model), both, rounds(turn, True))
        d_three = d_three + got.astype(F32)

    _, norm_back_one = jax.vjp(rms_norm, resid, gain_one)
    d_resid, grad_gain_one = norm_back_one(d_normed_one)
    d_resid = (d_resid + d_resid_one).reshape(rows, tok, d_model)
    text_grad = d_resid[:, patch_dev:]
    d_patch_rows = d_resid[:, :patch_dev].reshape(rows * patch_dev, d_model)
    d_low = d_patch_rows.astype(BF16)
    feature_grad = jnp.concatenate(
        [dot_nn(d_low, in_low), dot_nn(d_low, in_high[:, : vit - half_in])], axis=1
    ).reshape(rows, patch_dev, vit)
    pos_grads = d_table[:, None] * (jnp.arange(HEADS)[None, :] == head).astype(F32)
    pos_grads = jnp.pad(
        pos_grads.reshape(dev_count, bias_count), ((0, 0), (0, cols - bias_count))
    ).reshape(1, d_model)
    small_grads = jnp.concatenate(
        [
            jnp.sum(d_patch_rows, axis=0)[None],
            grad_gain_one[None],
            grad_gain_two[None],
            pos_grads,
            jnp.zeros((12, d_model), F32),
        ],
        axis=0,
    ).astype(BF16)
    left = jnp.concatenate([d_low, small_grads], axis=0)
    right = jnp.concatenate(
        [
            jnp.pad(features, ((0, 0), (0, 128))),
            jnp.pad(jnp.eye(16, 128, dtype=BF16), ((0, 0), (vit, 0))),
        ],
        axis=0,
    )
    in_grads = jnp.concatenate(
        [
            scatter_add(
                dot_tn(left, right[:, :half_in]).astype(BF16),
                [core, near] + dp_bits[::-1] + seq_high[::-1],
                every,
                True,
            )[-1],
            scatter_add(
                dot_tn(left, right[:, half_in:]).astype(BF16),
                [core] + dp_bits[::-1] + [near] + seq_high[::-1],
                every,
                True,
            )[-1],
        ],
        axis=1,
    )
    small_out = in_grads[:, vit:]
    d_three = d_three.reshape(3, cols, d_model)
    return (
        result[:, :patch_dev],
        result[:, patch_dev:],
        feature_grad,
        text_grad,
        in_grads[:, :vit].T,
        small_out[:, 0],
        small_out[:, 1],
        d_three[0].T,
        d_three[1].T,
        d_three[2].T,
        grad_out.T,
        small_out[:, 2],
        grad_gate.T,
        grad_up.T,
        grad_down,
        small_out[:bias_count, 3],
    )


def solution(mesh):
    token = P("dp", "seq", None)
    matrix = P(None, ("dp", "seq"))
    vector = P(("dp", "seq"))
    return jax.shard_map(
        local,
        mesh=mesh,
        in_specs=(
            token, token, P("dp", None), matrix, vector, vector, matrix, matrix, matrix, matrix,
            vector, matrix, matrix, matrix, vector, token, token,
        ),
        out_specs=(
            token, token, token, token, matrix, vector, vector, matrix, matrix, matrix, matrix,
            vector, matrix, matrix, matrix, vector,
        ),
        check_vma=False,
    )
```

```python
import jax
import jax.numpy as jnp
from jax import lax
from jax.experimental import pallas as pl
from jax.experimental.pallas import tpu as pltpu
from jax.sharding import PartitionSpec as P

HEADS = 16
HEAD_DIM = 64
BUCKETS = 32
PATCHES_IMG = 256
TEXT_MOST = 192

EPSILON = 1e-06
MASKED = -1e30
STARTS = (0, 1, 2, 3, 4, 5, 6, 7, 8, 12, 16, 23, 32, 46, 64, 91)
BF16 = jnp.bfloat16
F32 = jnp.float32
INTERPRET = False

SEG_Q = PATCHES_IMG + TEXT_MOST
SEG_K = 2 * PATCHES_IMG
TEXT_K = SEG_K - PATCHES_IMG
TEXT_PITCH = 32


def dot_nt(left, right):
    return lax.dot_general(left, right, (((1,), (1,)), ((), ())), preferred_element_type=F32)


def dot_nn(left, right):
    return lax.dot_general(left, right, (((1,), (0,)), ((), ())), preferred_element_type=F32)


def dot_tn(left, right):
    return lax.dot_general(left, right, (((0,), (0,)), ((), ())), preferred_element_type=F32)


def rms_norm(values, gain):
    return values * lax.rsqrt(jnp.mean(values * values, axis=-1, keepdims=True) + EPSILON) * gain


def gelu_tanh(values):
    return (
        0.5
        * values
        * (1.0 + jnp.tanh(0.7978845608 * (values + 0.044715 * values * values * values)))
    )


def gated_unit(gate_pre, up_pre):
    return gelu_tanh(gate_pre) * up_pre


SEQ = "seq"
BOTH = ("dp", "seq")


def swap(array, step):
    axis, bit = step
    count = lax.axis_size(axis)
    return lax.ppermute(array, axis, [(i, i ^ (1 << bit)) for i in range(count)])


def my_bit(step):
    return (lax.axis_index(step[0]) >> step[1]) & 1


def rank(step):
    return (1000 if step[0] == "dp" else 0) + step[1]


def together(*arrays):
    return lax.optimization_barrier(arrays)


def joined(mine, other, step, have, absolute):
    at = sum(1 for done in have if rank(done) > rank(step))
    if absolute:
        bit = my_bit(step) == 1
        mine, other = jnp.where(bit, other, mine), jnp.where(bit, mine, other)
    shape = (2**at, 1, mine.shape[0] >> at, mine.shape[1])
    return jnp.concatenate([mine.reshape(shape), other.reshape(shape)], axis=1).reshape(
        -1, mine.shape[1]
    )


def halves(grads, step, every, absolute):
    at = sum(1 for other in every if rank(other) > rank(step))
    rows, width = grads.shape[0] // 2, grads.shape[1]
    view = grads.reshape(2**at, 2, rows >> at, width)
    if absolute:
        bit = my_bit(step)
        keep = lax.dynamic_slice_in_dim(view, bit, 1, 1)
        send = lax.dynamic_slice_in_dim(view, 1 - bit, 1, 1)
    else:
        keep, send = view[:, 0], view[:, 1]
    return keep.reshape(rows, width), send.reshape(rows, width)


def gather(block, order, absolute, hooks=None):
    for number, step in enumerate(order):
        other = swap(block, step)
        if hooks and number in hooks:
            block = hooks[number](block)
        block = joined(block, other, step, order[:number], absolute)
    return block


def scatter_add(grads, order, every, absolute, hooks=None):
    for number, step in enumerate(order):
        left = [other for other in every if other not in order[:number]]
        keep, send = halves(grads, step, left, absolute)
        other = swap(send.astype(BF16), step)
        if hooks and number in hooks:
            keep = hooks[number](keep)
        grads = keep.astype(F32) + other.astype(F32)
    return grads


def bias_kernel(table_ref, out_ref):
    delta = lax.broadcasted_iota(jnp.int32, out_ref.shape, 0) - lax.broadcasted_iota(
        jnp.int32, out_ref.shape, 1
    )
    value = jnp.full(out_ref.shape, table_ref[0, BUCKETS - 1], F32)
    for which in range(14, 0, -1):
        value = jnp.where(delta > -STARTS[which + 1], table_ref[0, 16 + which], value)
    for which in range(16):
        value = jnp.where(delta >= STARTS[which], table_ref[0, which], value)
    out_ref[...] = value


def bucket_kernel(d_ref, out_ref):
    shape = d_ref.shape
    delta = lax.broadcasted_iota(jnp.int32, shape, 0) - lax.broadcasted_iota(jnp.int32, shape, 1)
    values = d_ref[...]
    rows = []
    for which in range(BUCKETS):
        low = STARTS[which % 16]
        high = STARTS[which % 16 + 1] if which % 16 < 15 else 1 << 20
        if which < 16:
            inside = (delta >= low) & (delta < high)
        else:
            inside = (delta <= -max(low, 1)) & (delta > -high)
        rows.append(jnp.sum(jnp.where(inside, values, 0.0), axis=0, keepdims=True))
    sums = jnp.sum(jnp.concatenate(rows, axis=0), axis=1, keepdims=True)
    out_ref[...] = jnp.broadcast_to(sums, out_ref.shape)


def unpack(seq_count, where, row, pat_ref, txt_ref, patch_dev, text_dev, lanes):
    tail = TEXT_PITCH - text_dev
    for place in range(seq_count):
        block = where(place)
        patches = block[0:patch_dev, lanes]
        text = block[patch_dev : patch_dev + text_dev, lanes]
        pat_ref[row, place * patch_dev : (place + 1) * patch_dev, :] = patches
        txt_ref[row, place * TEXT_PITCH : place * TEXT_PITCH + text_dev, :] = text
        if tail:
            txt_ref[row, place * TEXT_PITCH + text_dev : (place + 1) * TEXT_PITCH, :] = jnp.zeros(
                (tail, text.shape[1]), text.dtype
            )


def picker(count, text_rows, text_dev, slot_count, first, length):
    shape = (count, text_rows)
    column = lax.broadcasted_iota(jnp.int32, shape, 1)
    inner = column & (TEXT_PITCH - 1)
    slot = (column // TEXT_PITCH) * text_dev + inner
    fill = jnp.where(slot >= slot_count // 2, slot - slot_count // 2, slot + slot_count // 2)
    line = lax.broadcasted_iota(jnp.int32, shape, 0)
    hit = (fill == first + line) & (line < length) & (inner < text_dev)
    return hit.astype(F32).astype(BF16)


def softmax(scores):
    top = jnp.max(scores, axis=-1, keepdims=True)
    expd = jnp.exp(scores - top)
    return expd / jnp.sum(expd, axis=-1, keepdims=True)


def segment_start(len_ref, row, which):
    return lax.fori_loop(0, which, lambda at, total: total + len_ref[row, at], jnp.int32(0))


class Halves:
    def __init__(self, me, own_ref, other_ref, row):
        self.me, self.own, self.other, self.row = me, own_ref, other_ref, row

    def at(self, place):
        apart = place ^ self.me
        return apart & 1, apart >> 1

    def __call__(self, place):
        odd, index = self.at(place)
        return jnp.where(odd == 1, self.other[index, self.row], self.own[index, self.row])


def forward_kernel(dims, me_ref, len_ref, bias_ref, own_ref, other_ref, o_ref, pat, txt, opat, otxt):
    rows, images, patch_dev, text_dev, slots = dims
    seq_count = 2 * own_ref.shape[0]
    text_rows = seq_count * TEXT_PITCH
    for row in range(rows):
        unpack(
            seq_count, Halves(me_ref[0], own_ref, other_ref, row),
            row, pat, txt, patch_dev, text_dev, slice(None),
        )
    otxt[...] = jnp.zeros_like(otxt)

    def attend(compact, queries, keys, length):
        q = compact[:queries, :HEAD_DIM]
        k = compact[:keys, HEAD_DIM : 2 * HEAD_DIM]
        v = compact[:keys, 2 * HEAD_DIM :]
        scores = dot_nt(q, k) + bias_ref[:queries, :keys]
        column = lax.broadcasted_iota(jnp.int32, scores.shape, 1)
        probs = softmax(jnp.where(column < length, scores, MASKED)).astype(BF16)
        return dot_nn(probs, v).astype(BF16)

    def one_segment(step, carry):
        row, image = step // images, step % images
        length = len_ref[row, image]
        first = segment_start(len_ref, row, image)
        pick = picker(TEXT_K, text_rows, text_dev, slots, first, length)
        text = dot_nn(pick, txt[row]).astype(BF16)
        at = pl.multiple_of(image * PATCHES_IMG, PATCHES_IMG)
        compact = jnp.concatenate([pat[row, pl.ds(at, PATCHES_IMG), :], text], axis=0)
        out = attend(compact, SEG_Q, SEG_K, PATCHES_IMG + length)
        opat[row, pl.ds(at, PATCHES_IMG), :] = out[:PATCHES_IMG]
        otxt[row] = otxt[row] + dot_tn(pick[:TEXT_MOST], out[PATCHES_IMG:])
        return carry

    lax.fori_loop(0, rows * images, one_segment, 0)
    pad_q = slots // 4
    pad_k = -(-pad_q // 128) * 128
    for row in range(rows):
        first = segment_start(len_ref, row, images)
        pick = picker(pad_k, text_rows, text_dev, slots, first, pad_q)
        compact = dot_nn(pick, txt[row]).astype(BF16)
        out = attend(compact, pad_q, pad_k, pad_q)
        otxt[row] = otxt[row] + dot_tn(pick[:pad_q], out)
    for place in range(seq_count):
        o_ref[place, 0:patch_dev, :] = jnp.concatenate(
            [opat[row, place * patch_dev : (place + 1) * patch_dev, :] for row in range(rows)],
            axis=1,
        )
        low = place * TEXT_PITCH
        o_ref[place, patch_dev : patch_dev + text_dev, :] = jnp.concatenate(
            [otxt[row, low : low + text_dev, :].astype(BF16) for row in range(rows)], axis=1
        )


def backward_kernel(
    dims, me_ref, len_ref, bias_ref, own_ref, other_ref, do_ref, down_ref, dother_ref, dbias_ref,
    pat, txt, dpat, dtxt, gpat, gtxt,
):
    rows, images, patch_dev, text_dev, slots = dims
    seq_count = 2 * own_ref.shape[0]
    text_rows = seq_count * TEXT_PITCH
    for row in range(rows):
        unpack(
            seq_count, Halves(me_ref[0], own_ref, other_ref, row),
            row, pat, txt, patch_dev, text_dev, slice(None),
        )
        unpack(
            seq_count, lambda place: do_ref.at[place],
            row, dpat, dtxt, patch_dev, text_dev,
            slice(row * HEAD_DIM, (row + 1) * HEAD_DIM),
        )
    gtxt[...] = jnp.zeros_like(gtxt)
    dbias_ref[...] = jnp.zeros_like(dbias_ref)

    def attend_back(compact, d_out, queries, keys, length):
        q = compact[:queries, :HEAD_DIM]
        k = compact[:keys, HEAD_DIM : 2 * HEAD_DIM]
        v = compact[:keys, 2 * HEAD_DIM :]
        scores = dot_nt(q, k) + bias_ref[:queries, :keys]
        column = lax.broadcasted_iota(jnp.int32, scores.shape, 1)
        probs = softmax(jnp.where(column < length, scores, MASKED))
        d_probs = dot_nt(d_out, v)
        centre = jnp.sum(d_probs * probs, axis=-1, keepdims=True)
        d_scores = probs * (d_probs - centre)
        d_low = d_scores.astype(BF16)
        d_q = dot_nn(d_low, k).astype(BF16)
        d_k = dot_tn(d_low, q).astype(BF16)
        d_v = dot_tn(probs.astype(BF16), d_out).astype(BF16)
        return d_scores, jnp.concatenate([d_q, d_k[:queries], d_v[:queries]], axis=1)

    def one_segment(step, carry):
        row, image = step // images, step % images
        length = len_ref[row, image]
        first = segment_start(len_ref, row, image)
        pick = picker(TEXT_K, text_rows, text_dev, slots, first, length)
        at = pl.multiple_of(image * PATCHES_IMG, PATCHES_IMG)
        text = dot_nn(pick, txt[row]).astype(BF16)
        compact = jnp.concatenate([pat[row, pl.ds(at, PATCHES_IMG), :], text], axis=0)
        text_do = dot_nn(pick[:TEXT_MOST], dtxt[row]).astype(BF16)
        d_out = jnp.concatenate([dpat[row, pl.ds(at, PATCHES_IMG), :], text_do], axis=0)
        d_scores, grads = attend_back(compact, d_out, SEG_Q, SEG_K, PATCHES_IMG + length)
        dbias_ref[...] = dbias_ref[...] + d_scores
        gpat[row, pl.ds(at, PATCHES_IMG), :] = grads[:PATCHES_IMG]
        gtxt[row] = gtxt[row] + dot_tn(pick[:TEXT_MOST], grads[PATCHES_IMG:])
        return carry

    lax.fori_loop(0, rows * images, one_segment, 0)
    pad_q = slots // 4
    pad_k = -(-pad_q // 128) * 128
    for row in range(rows):
        first = segment_start(len_ref, row, images)
        pick = picker(pad_k, text_rows, text_dev, slots, first, pad_q)
        compact = dot_nn(pick, txt[row]).astype(BF16)
        d_out = dot_nn(pick[:pad_q], dtxt[row]).astype(BF16)
        d_scores, grads = attend_back(compact, d_out, pad_q, pad_k, pad_q)
        dbias_ref[:pad_q, :pad_k] = dbias_ref[:pad_q, :pad_k] + d_scores
        gtxt[row] = gtxt[row] + dot_tn(pick[:pad_q], grads)
    for row in range(rows):
        for place in range(seq_count):
            odd, index = Halves(me_ref[0], own_ref, other_ref, row).at(place)
            low = place * TEXT_PITCH
            patches = gpat[row, place * patch_dev : (place + 1) * patch_dev, :]
            text = gtxt[row, low : low + text_dev, :].astype(BF16)

            def put(target):
                target[index, row, 0:patch_dev, :] = patches
                target[index, row, patch_dev : patch_dev + text_dev, :] = text

            pl.when(odd == 0)(lambda: put(down_ref))
            pl.when(odd == 1)(lambda: put(dother_ref))


SMEM = pl.BlockSpec(memory_space=pltpu.SMEM)
VMEM = pl.BlockSpec(memory_space=pltpu.VMEM)


def call(kernel, out_shape, in_specs, scratch=(), flops=0, bytes_accessed=0, vmem=16):
    single = not isinstance(out_shape, (tuple, list))
    return pl.pallas_call(
        kernel,
        out_shape=out_shape,
        in_specs=in_specs,
        out_specs=VMEM if single else [VMEM] * len(out_shape),
        scratch_shapes=list(scratch),
        cost_estimate=pl.CostEstimate(
            flops=flops, bytes_accessed=bytes_accessed, transcendentals=0
        ),
        compiler_params=pltpu.CompilerParams(vmem_limit_bytes=vmem << 20),
        interpret=INTERPRET,
    )


def local(
    patch_features, text_embeds, text_lengths, w_in, b_in, gain_attn, w_query, w_key, w_value,
    w_out, gain_ffn, w_gate, w_up, w_down, position_bias, d_patch, d_text,
):
    seq_count, dp_count = lax.axis_size(SEQ), lax.axis_size("dp")
    dev_count = seq_count * dp_count
    seq_index, dp_index = lax.axis_index(SEQ), lax.axis_index("dp")
    rows, patch_dev, vit = patch_features.shape
    text_dev = text_embeds.shape[1]
    tok = patch_dev + text_dev
    mine = rows * tok
    d_model = text_embeds.shape[2]
    cols = w_in.shape[1]
    images = text_lengths.shape[1]
    slots = text_dev * seq_count
    core, near, team_bit = ("seq", 0), ("seq", 1), ("seq", 3)
    seq_high = [("seq", bit) for bit in range(seq_count.bit_length() - 2, 1, -1)]
    dp_bits = [("dp", bit) for bit in range(dp_count.bit_length() - 1)]
    every = dp_bits + seq_high + [near, core]

    bias_count = position_bias.shape[0]
    pack = jnp.concatenate(
        [
            w_in,
            b_in[None],
            gain_attn[None],
            gain_ffn[None],
            jnp.pad(position_bias, (0, cols - bias_count))[None],
            jnp.zeros((124, cols), BF16),
            w_out,
        ],
        axis=0,
    ).T
    wide = vit + 128
    half_in = (wide + d_model) // 256 * 128
    per_head = dev_count // HEADS
    twins = seq_count // HEADS
    head = seq_index // twins
    twin = seq_index % twins
    place_in_head = dp_index * twins + twin
    row_count = rows // twins
    three = jnp.concatenate([w_query.T, w_key.T, w_value.T], axis=0)

    def to_rank(which_head, place):
        return (place // twins) * seq_count + which_head * twins + place % twins

    def rounds(turn, back):
        pairs = []
        for which_head in range(HEADS):
            for i in range(per_head):
                owner = which_head * per_head + i
                user = to_rank(which_head, (i + turn) % per_head)
                pairs.append((user, owner) if back else (owner, user))
        return pairs

    team = [team_bit, core]
    ff_far = [step for step in seq_high if step != team_bit]
    units = w_gate.shape[1]
    down_out = jnp.transpose(w_down.reshape(dev_count, units, cols), (0, 2, 1))
    upstream = jnp.concatenate([d_patch, d_text], axis=1).reshape(mine, d_model)
    late = {}

    down_in = lax.all_to_all(down_out, BOTH, 0, 0, tiled=True)
    ff_order = ff_far + [near] + dp_bits

    def while_split(block):
        block, down = together(block, down_in)
        late["ff"] = jnp.concatenate(
            [w_gate.T, w_up.T, down.reshape(d_model, units).T], axis=1
        )
        for step in ff_far[:-1]:
            late["ff"] = jnp.concatenate([late["ff"], swap(late["ff"], step)], axis=0)
        late["ff_got"] = swap(late["ff"], ff_far[-1])
        return block

    def while_core(block):
        block, send = together(block, three)
        late["pieces"] = [lax.ppermute(send, BOTH, rounds(turn, False)) for turn in range(per_head)]
        return block

    in_low = gather(
        pack[:, :half_in],
        seq_high + dp_bits + [near, core],
        True,
        {len(seq_high): while_split, len(every) - 1: while_core},
    )
    in_high = gather(pack[:, half_in:], seq_high + [near] + dp_bits + [core], True)
    full_out = in_high[:, wide - half_in :]

    features = patch_features.reshape(rows * patch_dev, vit)
    ones = jnp.zeros((rows * patch_dev, 128), BF16).at[:, 0].set(1)
    features_more = jnp.concatenate([features, ones], axis=1)
    patch_rows = dot_nt(features_more[:, :half_in], in_low) + dot_nt(
        features_more[:, half_in:], in_high[:, : wide - half_in]
    )
    units_eye = jnp.eye(8, 128, dtype=BF16)
    small = dot_nt(units_eye, in_high[:, wide - half_in - 128 : wide - half_in])
    gain_one, gain_two = small[1], small[2]
    table = small[3].reshape(dev_count, cols)[:, :bias_count].reshape(BUCKETS, HEADS)
    my_table = lax.dynamic_slice_in_dim(table, head, 1, 1).reshape(1, BUCKETS)
    resid = jnp.concatenate(
        [patch_rows.reshape(rows, patch_dev, d_model), text_embeds.astype(F32)], axis=1
    ).reshape(mine, d_model)
    normed_one = rms_norm(resid, gain_one).astype(BF16)
    half = d_model // 2
    order_low = seq_high + [near]
    order_high = [near] + seq_high
    chips = seq_count // 2
    normed_one, *pieces = together(normed_one, *late["pieces"])

    def while_last(block):
        block, late["up"] = together(block, upstream)
        late["up_got"] = swap(late["up"], team_bit)
        return block

    own_low = gather(normed_one[:, :half], order_low, False, {len(seq_high): while_last})
    own_high = gather(normed_one[:, half:], order_high, False)
    own_low, own_high, ff_got, up_got = together(
        own_low, own_high, late["ff_got"], late["up_got"]
    )
    other_low, other_high = swap(own_low, core), swap(own_high, core)
    ff_block = jnp.concatenate([late["ff"], ff_got], axis=0)
    ff_got = swap(ff_block, near)
    team_up = jnp.concatenate([late["up"], up_got], axis=0)
    team_up = jnp.concatenate([team_up, swap(team_up, core)], axis=0)

    def my_rows(array):
        if twins == 1:
            return array
        view = array.reshape(chips, rows, tok, array.shape[1])
        view = lax.dynamic_slice_in_dim(view, twin * row_count, row_count, 1)
        return view.reshape(chips * row_count * tok, array.shape[1])

    pieces = jnp.stack(pieces).reshape(per_head, 3, cols, d_model)
    ordered = [
        lax.dynamic_index_in_dim(pieces, (place_in_head - i) % per_head, 0, keepdims=False)
        for i in range(per_head)
    ]
    w_head = jnp.stack(ordered, axis=1).reshape(3 * HEAD_DIM, d_model)
    normed_pairs = [
        (my_rows(own_low), my_rows(own_high)),
        (my_rows(other_low), my_rows(other_high)),
    ]
    qkv = [
        (dot_nt(low, w_head[:, :half]) + dot_nt(high, w_head[:, half:]))
        .astype(BF16)
        .reshape(chips, row_count, tok, 3 * HEAD_DIM)
        for low, high in normed_pairs
    ]
    *qkv, ff_got = together(*qkv, ff_got)
    ff_mine = []
    for which in range(3):
        part = slice(which * d_model, (which + 1) * d_model)
        block = jnp.concatenate([ff_block[:, part], ff_got[:, part]], axis=0)
        for step in dp_bits[:-1]:
            block = jnp.concatenate([block, swap(block, step)], axis=0)
        ff_mine.append(block)
    ff_theirs = [swap(block, dp_bits[-1]) for block in ff_mine]
    lengths = lax.dynamic_slice_in_dim(text_lengths, twin * row_count, row_count, 0)
    me = seq_index.reshape(1).astype(jnp.int32)
    dims = (row_count, images, patch_dev, text_dev, slots)
    bias = call(
        bias_kernel, jax.ShapeDtypeStruct((SEG_Q, SEG_K), F32), [SMEM], (), 1 << 24, 1 << 20, 8
    )(my_table)
    text_rows = seq_count * TEXT_PITCH
    patches = seq_count * patch_dev
    packed_shape = jax.ShapeDtypeStruct((seq_count, tok, row_count * HEAD_DIM), BF16)
    mixed = call(
        lambda *refs: forward_kernel(dims, *refs),
        packed_shape,
        [SMEM, SMEM, VMEM, VMEM, VMEM],
        (
            pltpu.VMEM((row_count, patches, 3 * HEAD_DIM), BF16),
            pltpu.VMEM((row_count, text_rows, 3 * HEAD_DIM), BF16),
            pltpu.VMEM((row_count, patches, HEAD_DIM), BF16),
            pltpu.VMEM((row_count, text_rows, HEAD_DIM), F32),
        ),
        1 << 24,
        1 << 20,
        20,
    )(me, lengths, bias, *qkv)
    mixed, ff_theirs[0] = together(mixed, ff_theirs[0])
    mixed_got = lax.all_to_all(mixed, SEQ, 0, 0, tiled=True)
    mixed_got, ff_theirs[1] = together(mixed_got, ff_theirs[1])
    mixed_got = mixed_got.reshape(HEADS, twins, tok, row_count, HEAD_DIM)
    attn_out = jnp.transpose(mixed_got, (1, 3, 2, 0, 4)).reshape(mine, d_model)
    resid_one = resid + dot_nt(attn_out, full_out)
    normed_two = rms_norm(resid_one, gain_two).astype(BF16)
    team_normed = normed_two
    for step in team:
        team_normed = jnp.concatenate([team_normed, swap(team_normed, step)], axis=0)
    weights_at = [ff_mine, ff_theirs]
    d_normed_part, unit_grads = 0.0, []
    for full_gate, full_up, full_down in weights_at:
        gate_pre = dot_nt(team_normed, full_gate)
        up_pre = dot_nt(team_normed, full_up)
        hidden, gated_back = jax.vjp(gated_unit, gate_pre, up_pre)
        d_gate, d_up = gated_back(dot_nt(team_up, full_down))
        unit_grads.append([d_gate.astype(BF16), d_up.astype(BF16), hidden.astype(BF16)])
        for grad, full in zip(unit_grads[-1], (full_gate, full_up)):
            d_normed_part = d_normed_part + dot_nn(grad, full)

    def unit_weight_grads(d_gate, d_up, hidden):
        return jnp.concatenate(
            [
                dot_tn(d_gate, team_normed).astype(BF16),
                dot_tn(d_up, team_normed).astype(BF16),
                dot_tn(hidden, team_up).astype(BF16),
            ],
            axis=1,
        )

    def ff_grads_start(keep):
        keep, *grads = together(keep, *unit_grads[1])
        keep, send = together(keep, unit_weight_grads(*grads))
        late["ff_got"] = swap(send, dp_bits[-1])
        return keep

    keep, send = halves(d_normed_part, core, [core], False)
    d_normed_two = keep + swap(send.astype(BF16), core).astype(F32)
    keep, send = halves(d_normed_two, team_bit, [team_bit], False)
    got = swap(send.astype(BF16), team_bit)
    d_normed_two = ff_grads_start(keep) + got.astype(F32)
    _, norm_back_two = jax.vjp(rms_norm, resid_one, gain_two)
    d_resid_one, grad_gain_two = norm_back_two(d_normed_two)
    d_resid_one = d_resid_one + upstream.astype(F32)
    d_mix = d_resid_one.astype(BF16)
    d_attn = dot_nn(d_mix, full_out).astype(BF16)
    d_attn = d_attn.reshape(twins, row_count, tok, HEADS, HEAD_DIM)
    d_attn = jnp.transpose(d_attn, (3, 0, 2, 1, 4)).reshape(packed_shape.shape)
    d_attn_got = lax.all_to_all(d_attn, SEQ, 0, 0, tiled=True)

    d_mix, *grads = together(d_mix, *unit_grads[0])
    ff_keep = unit_weight_grads(*grads)
    out_part = dot_nn(grads[2], weights_at[0][2]) + dot_nn(unit_grads[1][2], weights_at[1][2])
    out_keep, send = halves(out_part, core, [core], False)
    out_grad = dot_tn(d_mix, attn_out).astype(BF16)
    d_attn_got, send, ff_keep, out_grad = together(
        d_attn_got, send.astype(BF16), ff_keep, out_grad
    )
    out_got = swap(send, core)
    half_shape = jax.ShapeDtypeStruct(qkv[0].shape, BF16)
    d_own, d_other, d_bias = call(
        lambda *refs: backward_kernel(dims, *refs),
        (half_shape, half_shape, jax.ShapeDtypeStruct((SEG_Q, SEG_K), F32)),
        [SMEM, SMEM, VMEM, VMEM, VMEM, VMEM],
        (
            pltpu.VMEM((row_count, patches, 3 * HEAD_DIM), BF16),
            pltpu.VMEM((row_count, text_rows, 3 * HEAD_DIM), BF16),
            pltpu.VMEM((row_count, patches, HEAD_DIM), BF16),
            pltpu.VMEM((row_count, text_rows, HEAD_DIM), BF16),
            pltpu.VMEM((row_count, patches, 3 * HEAD_DIM), BF16),
            pltpu.VMEM((row_count, text_rows, 3 * HEAD_DIM), F32),
        ),
        1 << 24,
        1 << 20,
        28,
    )(me, lengths, bias, *qkv, d_attn_got)
    d_qkv = [array.reshape(chips * row_count * tok, 3 * HEAD_DIM) for array in (d_own, d_other)]

    def all_rows(array):
        if twins == 1:
            return array
        view = array.reshape(chips, row_count, tok, array.shape[1])
        zero = jnp.zeros((chips, rows, tok, array.shape[1]), array.dtype)
        view = lax.dynamic_update_slice_in_dim(zero, view, twin * row_count, 1)
        return view.reshape(chips * mine, array.shape[1])

    chip_bits = seq_high + [near]
    weights = (w_head[:, :half], w_head[:, half:])
    sends = together(*[all_rows(dot_nn(d_qkv[1], part).astype(BF16)) for part in weights], d_own)
    others = [swap(send, core) for send in sends[:2]]
    d_qkv[0] = sends[2].reshape(d_qkv[0].shape)
    owns = [
        all_rows(dot_nn(d_qkv[0], part)) + other.astype(F32) for part, other in zip(weights, others)
    ]
    state = {}

    def ff_take(keep, step):
        keep, got = together(keep, state["ff_got"])
        state["ff"] = state["ff_keep"].astype(F32) + got.astype(F32)
        return keep

    def ff_start(keep, step):
        count = state["ff"].shape[0] // 2
        state["ff_keep"] = state["ff"][:count]
        keep, send = together(keep, state["ff"][count:].astype(BF16))
        state["ff_got"] = swap(send, step)
        return keep

    ff_back = ff_order[::-1]
    state.update(ff_keep=ff_keep, ff_got=late["ff_got"])

    def while_first(keep):
        keep = ff_take(keep, ff_back[0])
        for step in ff_back[1 : len(dp_bits)]:
            keep = ff_take(ff_start(keep, step), step)
        return ff_start(keep, near)

    def while_last_again(keep):
        keep = ff_take(keep, near)
        for step in ff_far[:0:-1]:
            keep = ff_take(ff_start(keep, step), step)
        return ff_start(keep, ff_far[0])

    def while_middle(keep):
        keep, grads_own, grads_other = together(keep, *d_qkv)
        d_head = jnp.concatenate(
            [
                dot_tn(grads_own, normed_pairs[0][which])
                + dot_tn(grads_other, normed_pairs[1][which])
                for which in range(2)
            ],
            axis=1,
        )
        d_head = d_head.reshape(3, per_head, cols, d_model).astype(BF16)
        sends = [
            lax.dynamic_index_in_dim(
                d_head, (place_in_head - turn) % per_head, 1, keepdims=False
            ).reshape(3 * cols, d_model)
            for turn in range(per_head)
        ]
        keep, *state["sends"] = together(keep, *sends)
        return keep

    low_sums = scatter_add(owns[0], order_low[::-1], chip_bits, False, {0: while_first, 1: while_middle, len(order_low) - 1: while_last_again})
    high_sums = scatter_add(owns[1], order_high[::-1], chip_bits, False)
    d_normed_one = jnp.concatenate([low_sums, high_sums], axis=1)
    d_table = call(
        bucket_kernel, jax.ShapeDtypeStruct((BUCKETS, 128), F32), [VMEM], (), 1 << 20, 1 << 20, 8
    )(d_bias)[:, 0]
    _, norm_back_one = jax.vjp(rms_norm, resid, gain_one)
    d_resid, grad_gain_one = norm_back_one(d_normed_one)
    d_resid = (d_resid + d_resid_one).reshape(rows, tok, d_model)
    text_grad = d_resid[:, patch_dev:]
    d_patch_rows = d_resid[:, :patch_dev].reshape(rows * patch_dev, d_model)
    d_low = d_patch_rows.astype(BF16)
    pos_grads = d_table[:, None] * (jnp.arange(HEADS)[None, :] == head).astype(F32)
    pos_grads = jnp.pad(
        pos_grads.reshape(dev_count, bias_count), ((0, 0), (0, cols - bias_count))
    ).reshape(1, d_model)
    small_grads = jnp.concatenate(
        [
            jnp.sum(d_patch_rows, axis=0)[None],
            grad_gain_one[None],
            grad_gain_two[None],
            pos_grads,
            jnp.zeros((12, d_model), F32),
        ],
        axis=0,
    ).astype(BF16)
    left = jnp.concatenate([d_low, small_grads], axis=0)
    right = jnp.concatenate(
        [
            jnp.pad(features, ((0, 0), (0, 128))),
            jnp.pad(jnp.eye(16, 128, dtype=BF16), ((0, 0), (vit, 0))),
        ],
        axis=0,
    )

    def while_core_again(keep):
        keep, got, *sends = together(keep, out_got, *state["sends"])
        part = out_keep + got.astype(F32)
        state["out_keep"], send = halves(part, team_bit, [team_bit], False)
        keep, send, state["d_low"] = together(keep, send.astype(BF16), d_low)
        state["three"] = [
            lax.ppermute(send, BOTH, rounds(turn, True)) for turn, send in enumerate(sends)
        ]
        state["out_got"] = swap(send, team_bit)
        return keep

    def while_end(keep):
        keep, *state["three"] = together(keep, *state["three"])
        return keep

    def while_split_again(keep):
        keep = ff_take(keep, ff_far[0])
        down = state["ff"][:, 2 * d_model :]
        down_back = down.T.reshape(dev_count, cols, units)
        keep, down_back = together(keep, down_back)
        state["down_back"] = lax.all_to_all(down_back, BOTH, 0, 0, tiled=True)
        return keep

    out_grad = dot_tn(d_mix, attn_out).astype(BF16)
    in_low_sums = scatter_add(
        dot_tn(left, right[:, :half_in]).astype(BF16),
        [core, near] + dp_bits[::-1] + seq_high[::-1],
        every,
        True,
        {0: while_core_again, 2: while_split_again, len(every) - 1: while_end},
    )
    in_high_sums = scatter_add(
        jnp.concatenate([dot_tn(left, right[:, half_in:]).astype(BF16), out_grad], axis=1),
        [core] + dp_bits[::-1] + [near] + seq_high[::-1],
        every,
        True,
    )
    in_grads = jnp.concatenate([in_low_sums, in_high_sums], axis=1)
    small_out, grad_w_out = in_grads[:, vit:wide], in_grads[:, wide:]
    d_low = state["d_low"]
    feature_grad = jnp.concatenate(
        [dot_nn(d_low, in_low), dot_nn(d_low, in_high[:, : vit - half_in])], axis=1
    ).reshape(rows, patch_dev, vit)
    result = resid_one + state["out_keep"] + state["out_got"].astype(F32)
    result = result.astype(BF16).reshape(rows, tok, d_model)
    grad_gate = state["ff"][:, :d_model]
    grad_up = state["ff"][:, d_model : 2 * d_model]
    grad_down = jnp.transpose(state["down_back"], (0, 2, 1)).reshape(dev_count * units, cols)
    grad_down = grad_down.astype(F32)
    d_three = sum(got.astype(F32) for got in state["three"]).reshape(3, cols, d_model)
    return (
        result[:, :patch_dev],
        result[:, patch_dev:],
        feature_grad,
        text_grad,
        in_grads[:, :vit].T,
        small_out[:, 0],
        small_out[:, 1],
        d_three[0].T,
        d_three[1].T,
        d_three[2].T,
        grad_w_out.T,
        small_out[:, 2],
        grad_gate.T,
        grad_up.T,
        grad_down,
        small_out[:bias_count, 3],
    )


def solution(mesh):
    token = P("dp", SEQ, None)
    matrix = P(None, BOTH)
    vector = P(BOTH)
    return jax.shard_map(
        local,
        mesh=mesh,
        in_specs=(
            token, token, P("dp", None), matrix, vector, vector, matrix, matrix, matrix, matrix,
            vector, matrix, matrix, matrix, vector, token, token,
        ),
        out_specs=(
            token, token, token, token, matrix, vector, vector, matrix, matrix, matrix, matrix,
            vector, matrix, matrix, matrix, vector,
        ),
        check_vma=False,
    )
```

```python
import jax
import jax.numpy as jnp
from jax import lax
from jax.experimental import pallas as pl
from jax.experimental.pallas import tpu as pltpu
from jax.sharding import PartitionSpec as P

HEADS = 16
HEAD_DIM = 64
BUCKETS = 32
PATCHES_IMG = 256
TEXT_MOST = 192

EPSILON = 1e-06
MASKED = -1e30
STARTS = (0, 1, 2, 3, 4, 5, 6, 7, 8, 12, 16, 23, 32, 46, 64, 91)
BF16 = jnp.bfloat16
F32 = jnp.float32
INTERPRET = False

SEG_Q = PATCHES_IMG + TEXT_MOST
SEG_K = 2 * PATCHES_IMG
TEXT_K = SEG_K - PATCHES_IMG
TEXT_PITCH = 32


def dot_nt(left, right):
    return lax.dot_general(left, right, (((1,), (1,)), ((), ())), preferred_element_type=F32)


def dot_nn(left, right):
    return lax.dot_general(left, right, (((1,), (0,)), ((), ())), preferred_element_type=F32)


def dot_tn(left, right):
    return lax.dot_general(left, right, (((0,), (0,)), ((), ())), preferred_element_type=F32)


def rms_norm(values, gain):
    return values * lax.rsqrt(jnp.mean(values * values, axis=-1, keepdims=True) + EPSILON) * gain


def gelu_tanh(values):
    return (
        0.5
        * values
        * (1.0 + jnp.tanh(0.7978845608 * (values + 0.044715 * values * values * values)))
    )


def gated_unit(gate_pre, up_pre):
    return gelu_tanh(gate_pre) * up_pre


SEQ = "seq"
BOTH = ("dp", "seq")


def swap(array, step):
    axis, bit = step
    count = lax.axis_size(axis)
    return lax.ppermute(array, axis, [(i, i ^ (1 << bit)) for i in range(count)])


def my_bit(step):
    return (lax.axis_index(step[0]) >> step[1]) & 1


def rank(step):
    return (1000 if step[0] == "dp" else 0) + step[1]


def after(value, signal):
    return value + (signal[(0,) * signal.ndim] * 0).astype(value.dtype)


def together(*arrays):
    return lax.optimization_barrier(arrays)


def joined(mine, other, step, have, absolute):
    at = sum(1 for done in have if rank(done) > rank(step))
    if absolute:
        bit = my_bit(step) == 1
        mine, other = jnp.where(bit, other, mine), jnp.where(bit, mine, other)
    shape = (2**at, 1, mine.shape[0] >> at, mine.shape[1])
    return jnp.concatenate([mine.reshape(shape), other.reshape(shape)], axis=1).reshape(
        -1, mine.shape[1]
    )


def halves(grads, step, every, absolute):
    at = sum(1 for other in every if rank(other) > rank(step))
    rows, width = grads.shape[0] // 2, grads.shape[1]
    view = grads.reshape(2**at, 2, rows >> at, width)
    if absolute:
        bit = my_bit(step)
        keep = lax.dynamic_slice_in_dim(view, bit, 1, 1)
        send = lax.dynamic_slice_in_dim(view, 1 - bit, 1, 1)
    else:
        keep, send = view[:, 0], view[:, 1]
    return keep.reshape(rows, width), send.reshape(rows, width)


def gather(block, order, absolute, hooks=None, have=()):
    for number, step in enumerate(order):
        other = swap(block, step)
        if hooks and number in hooks:
            block = hooks[number](block)
        block = joined(block, other, step, list(have) + order[:number], absolute)
    return block


def scatter_add(grads, order, every, absolute, hooks=None):
    for number, step in enumerate(order):
        left = [other for other in every if other not in order[:number]]
        keep, send = halves(grads, step, left, absolute)
        other = swap(send.astype(BF16), step)
        if hooks and number in hooks:
            keep = hooks[number](keep)
        grads = keep.astype(F32) + other.astype(F32)
    return grads


def bias_kernel(table_ref, out_ref):
    delta = lax.broadcasted_iota(jnp.int32, out_ref.shape, 0) - lax.broadcasted_iota(
        jnp.int32, out_ref.shape, 1
    )
    value = jnp.full(out_ref.shape, table_ref[0, BUCKETS - 1], F32)
    for which in range(14, 0, -1):
        value = jnp.where(delta > -STARTS[which + 1], table_ref[0, 16 + which], value)
    for which in range(16):
        value = jnp.where(delta >= STARTS[which], table_ref[0, which], value)
    out_ref[...] = value


def bucket_kernel(d_ref, out_ref):
    shape = d_ref.shape
    delta = lax.broadcasted_iota(jnp.int32, shape, 0) - lax.broadcasted_iota(jnp.int32, shape, 1)
    values = d_ref[...]
    rows = []
    for which in range(BUCKETS):
        low = STARTS[which % 16]
        high = STARTS[which % 16 + 1] if which % 16 < 15 else 1 << 20
        if which < 16:
            inside = (delta >= low) & (delta < high)
        else:
            inside = (delta <= -max(low, 1)) & (delta > -high)
        rows.append(jnp.sum(jnp.where(inside, values, 0.0), axis=0, keepdims=True))
    sums = jnp.sum(jnp.concatenate(rows, axis=0), axis=1, keepdims=True)
    out_ref[...] = jnp.broadcast_to(sums, out_ref.shape)


def unpack(seq_count, where, row, pat_ref, txt_ref, patch_dev, text_dev, lanes):
    tail = TEXT_PITCH - text_dev
    for place in range(seq_count):
        block = where(place)
        patches = block[0:patch_dev, lanes]
        text = block[patch_dev : patch_dev + text_dev, lanes]
        pat_ref[row, place * patch_dev : (place + 1) * patch_dev, :] = patches
        txt_ref[row, place * TEXT_PITCH : place * TEXT_PITCH + text_dev, :] = text
        if tail:
            txt_ref[row, place * TEXT_PITCH + text_dev : (place + 1) * TEXT_PITCH, :] = jnp.zeros(
                (tail, text.shape[1]), text.dtype
            )


def picker(count, text_rows, text_dev, slot_count, first, length):
    shape = (count, text_rows)
    column = lax.broadcasted_iota(jnp.int32, shape, 1)
    inner = column & (TEXT_PITCH - 1)
    slot = (column // TEXT_PITCH) * text_dev + inner
    fill = jnp.where(slot >= slot_count // 2, slot - slot_count // 2, slot + slot_count // 2)
    line = lax.broadcasted_iota(jnp.int32, shape, 0)
    hit = (fill == first + line) & (line < length) & (inner < text_dev)
    return hit.astype(F32).astype(BF16)


def softmax(scores):
    top = jnp.max(scores, axis=-1, keepdims=True)
    expd = jnp.exp(scores - top)
    return expd / jnp.sum(expd, axis=-1, keepdims=True)


def segment_start(len_ref, row, which):
    return lax.fori_loop(0, which, lambda at, total: total + len_ref[row, at], jnp.int32(0))


class Halves:
    def __init__(self, me, own_ref, other_ref, row):
        self.me, self.own, self.other, self.row = me, own_ref, other_ref, row

    def at(self, place):
        apart = place ^ self.me
        return apart & 1, apart >> 1

    def __call__(self, place):
        odd, index = self.at(place)
        return jnp.where(odd == 1, self.other[index, self.row], self.own[index, self.row])


def forward_kernel(dims, me_ref, len_ref, bias_ref, own_ref, other_ref, o_ref, pat, txt, opat, otxt):
    rows, images, patch_dev, text_dev, slots = dims
    seq_count = 2 * own_ref.shape[0]
    text_rows = seq_count * TEXT_PITCH
    for row in range(rows):
        unpack(
            seq_count, Halves(me_ref[0], own_ref, other_ref, row),
            row, pat, txt, patch_dev, text_dev, slice(None),
        )
    otxt[...] = jnp.zeros_like(otxt)

    def attend(compact, queries, keys, length):
        q = compact[:queries, :HEAD_DIM]
        k = compact[:keys, HEAD_DIM : 2 * HEAD_DIM]
        v = compact[:keys, 2 * HEAD_DIM :]
        scores = dot_nt(q, k) + bias_ref[:queries, :keys]
        column = lax.broadcasted_iota(jnp.int32, scores.shape, 1)
        probs = softmax(jnp.where(column < length, scores, MASKED)).astype(BF16)
        return dot_nn(probs, v).astype(BF16)

    def one_segment(step, carry):
        row, image = step // images, step % images
        length = len_ref[row, image]
        first = segment_start(len_ref, row, image)
        pick = picker(TEXT_K, text_rows, text_dev, slots, first, length)
        text = dot_nn(pick, txt[row]).astype(BF16)
        at = pl.multiple_of(image * PATCHES_IMG, PATCHES_IMG)
        compact = jnp.concatenate([pat[row, pl.ds(at, PATCHES_IMG), :], text], axis=0)
        out = attend(compact, SEG_Q, SEG_K, PATCHES_IMG + length)
        opat[row, pl.ds(at, PATCHES_IMG), :] = out[:PATCHES_IMG]
        otxt[row] = otxt[row] + dot_tn(pick[:TEXT_MOST], out[PATCHES_IMG:])
        return carry

    lax.fori_loop(0, rows * images, one_segment, 0)
    pad_q = slots // 4
    pad_k = -(-pad_q // 128) * 128
    for row in range(rows):
        first = segment_start(len_ref, row, images)
        pick = picker(pad_k, text_rows, text_dev, slots, first, pad_q)
        compact = dot_nn(pick, txt[row]).astype(BF16)
        out = attend(compact, pad_q, pad_k, pad_q)
        otxt[row] = otxt[row] + dot_tn(pick[:pad_q], out)
    for place in range(seq_count):
        o_ref[place, 0:patch_dev, :] = jnp.concatenate(
            [opat[row, place * patch_dev : (place + 1) * patch_dev, :] for row in range(rows)],
            axis=1,
        )
        low = place * TEXT_PITCH
        o_ref[place, patch_dev : patch_dev + text_dev, :] = jnp.concatenate(
            [otxt[row, low : low + text_dev, :].astype(BF16) for row in range(rows)], axis=1
        )


def backward_kernel(
    dims, me_ref, len_ref, bias_ref, own_ref, other_ref, do_ref, down_ref, dother_ref, dbias_ref,
    pat, txt, dpat, dtxt, gpat, gtxt,
):
    rows, images, patch_dev, text_dev, slots = dims
    seq_count = 2 * own_ref.shape[0]
    text_rows = seq_count * TEXT_PITCH
    for row in range(rows):
        unpack(
            seq_count, Halves(me_ref[0], own_ref, other_ref, row),
            row, pat, txt, patch_dev, text_dev, slice(None),
        )
        unpack(
            seq_count, lambda place: do_ref.at[place],
            row, dpat, dtxt, patch_dev, text_dev,
            slice(row * HEAD_DIM, (row + 1) * HEAD_DIM),
        )
    gtxt[...] = jnp.zeros_like(gtxt)
    dbias_ref[...] = jnp.zeros_like(dbias_ref)

    def attend_back(compact, d_out, queries, keys, length):
        q = compact[:queries, :HEAD_DIM]
        k = compact[:keys, HEAD_DIM : 2 * HEAD_DIM]
        v = compact[:keys, 2 * HEAD_DIM :]
        scores = dot_nt(q, k) + bias_ref[:queries, :keys]
        column = lax.broadcasted_iota(jnp.int32, scores.shape, 1)
        probs = softmax(jnp.where(column < length, scores, MASKED))
        d_probs = dot_nt(d_out, v)
        centre = jnp.sum(d_probs * probs, axis=-1, keepdims=True)
        d_scores = probs * (d_probs - centre)
        d_low = d_scores.astype(BF16)
        d_q = dot_nn(d_low, k).astype(BF16)
        d_k = dot_tn(d_low, q).astype(BF16)
        d_v = dot_tn(probs.astype(BF16), d_out).astype(BF16)
        return d_scores, jnp.concatenate([d_q, d_k[:queries], d_v[:queries]], axis=1)

    def one_segment(step, carry):
        row, image = step // images, step % images
        length = len_ref[row, image]
        first = segment_start(len_ref, row, image)
        pick = picker(TEXT_K, text_rows, text_dev, slots, first, length)
        at = pl.multiple_of(image * PATCHES_IMG, PATCHES_IMG)
        text = dot_nn(pick, txt[row]).astype(BF16)
        compact = jnp.concatenate([pat[row, pl.ds(at, PATCHES_IMG), :], text], axis=0)
        text_do = dot_nn(pick[:TEXT_MOST], dtxt[row]).astype(BF16)
        d_out = jnp.concatenate([dpat[row, pl.ds(at, PATCHES_IMG), :], text_do], axis=0)
        d_scores, grads = attend_back(compact, d_out, SEG_Q, SEG_K, PATCHES_IMG + length)
        dbias_ref[...] = dbias_ref[...] + d_scores
        gpat[row, pl.ds(at, PATCHES_IMG), :] = grads[:PATCHES_IMG]
        gtxt[row] = gtxt[row] + dot_tn(pick[:TEXT_MOST], grads[PATCHES_IMG:])
        return carry

    lax.fori_loop(0, rows * images, one_segment, 0)
    pad_q = slots // 4
    pad_k = -(-pad_q // 128) * 128
    for row in range(rows):
        first = segment_start(len_ref, row, images)
        pick = picker(pad_k, text_rows, text_dev, slots, first, pad_q)
        compact = dot_nn(pick, txt[row]).astype(BF16)
        d_out = dot_nn(pick[:pad_q], dtxt[row]).astype(BF16)
        d_scores, grads = attend_back(compact, d_out, pad_q, pad_k, pad_q)
        dbias_ref[:pad_q, :pad_k] = dbias_ref[:pad_q, :pad_k] + d_scores
        gtxt[row] = gtxt[row] + dot_tn(pick[:pad_q], grads)
    for row in range(rows):
        for place in range(seq_count):
            odd, index = Halves(me_ref[0], own_ref, other_ref, row).at(place)
            low = place * TEXT_PITCH
            patches = gpat[row, place * patch_dev : (place + 1) * patch_dev, :]
            text = gtxt[row, low : low + text_dev, :].astype(BF16)

            def put(target):
                target[index, row, 0:patch_dev, :] = patches
                target[index, row, patch_dev : patch_dev + text_dev, :] = text

            pl.when(odd == 0)(lambda: put(down_ref))
            pl.when(odd == 1)(lambda: put(dother_ref))


SMEM = pl.BlockSpec(memory_space=pltpu.SMEM)
VMEM = pl.BlockSpec(memory_space=pltpu.VMEM)


def call(kernel, out_shape, in_specs, scratch=(), flops=0, bytes_accessed=0, vmem=16):
    single = not isinstance(out_shape, (tuple, list))
    return pl.pallas_call(
        kernel,
        out_shape=out_shape,
        in_specs=in_specs,
        out_specs=VMEM if single else [VMEM] * len(out_shape),
        scratch_shapes=list(scratch),
        cost_estimate=pl.CostEstimate(
            flops=flops, bytes_accessed=bytes_accessed, transcendentals=0
        ),
        compiler_params=pltpu.CompilerParams(vmem_limit_bytes=vmem << 20),
        interpret=INTERPRET,
    )


def local(
    patch_features, text_embeds, text_lengths, w_in, b_in, gain_attn, w_query, w_key, w_value,
    w_out, gain_ffn, w_gate, w_up, w_down, position_bias, d_patch, d_text,
):
    seq_count, dp_count = lax.axis_size(SEQ), lax.axis_size("dp")
    dev_count = seq_count * dp_count
    seq_index, dp_index = lax.axis_index(SEQ), lax.axis_index("dp")
    rows, patch_dev, vit = patch_features.shape
    text_dev = text_embeds.shape[1]
    tok = patch_dev + text_dev
    mine = rows * tok
    d_model = text_embeds.shape[2]
    cols = w_in.shape[1]
    images = text_lengths.shape[1]
    slots = text_dev * seq_count
    core, near = ("seq", 0), ("seq", 1)
    seq_high = [("seq", bit) for bit in range(seq_count.bit_length() - 2, 1, -1)]
    dp_bits = [("dp", bit) for bit in range(dp_count.bit_length() - 1)]
    every = dp_bits + seq_high + [near, core]

    bias_count = position_bias.shape[0]
    pack = jnp.concatenate(
        [
            w_in,
            b_in[None],
            gain_attn[None],
            gain_ffn[None],
            jnp.pad(position_bias, (0, cols - bias_count))[None],
            jnp.zeros((124, cols), BF16),
            w_out,
        ],
        axis=0,
    ).T
    wide = vit + 128
    half_in = (wide + d_model) // 256 * 128
    per_head = dev_count // HEADS
    twins = seq_count // HEADS
    chips = seq_count // 2
    head_slot = (seq_index % 2) * chips + seq_index // 2
    head = head_slot // twins
    twin = head_slot % twins
    place_in_head = dp_index * twins + twin
    row_count = rows // twins
    three = jnp.concatenate([w_query.T, w_key.T, w_value.T], axis=0)

    def to_rank(which_head, place):
        slot = which_head * twins + place % twins
        return (place // twins) * seq_count + 2 * (slot % chips) + slot // chips

    def rounds(turn, back):
        pairs = []
        for which_head in range(HEADS):
            for i in range(per_head):
                owner = which_head * per_head + i
                user = to_rank(which_head, (i + turn) % per_head)
                pairs.append((user, owner) if back else (owner, user))
        return pairs

    team = [("seq", 2), near, core]
    ff_far = [step for step in seq_high if step not in team]
    ff_order = ff_far + dp_bits
    units = w_gate.shape[1]
    down_out = jnp.transpose(w_down.reshape(dev_count, units, cols), (0, 2, 1))
    down_in = lax.all_to_all(down_out, BOTH, 0, 0, tiled=True)
    upstream = jnp.concatenate([d_patch, d_text], axis=1).reshape(mine, d_model)
    up_got = swap(upstream, team[0])
    late = {}

    def while_split(block):
        block, late["down"] = together(block, down_in)
        return block

    def while_core(block):
        block, send, gate, up, got = together(block, three, w_gate, w_up, up_got)
        late["ff"] = jnp.concatenate(
            [gate.T, up.T, late["down"].reshape(d_model, units).T], axis=1
        )
        for step in ff_far[:-1]:
            late["ff"] = jnp.concatenate([late["ff"], swap(late["ff"], step)], axis=0)
        late["ff_got"] = swap(late["ff"], ff_far[-1])
        late["up"] = jnp.concatenate([upstream, got], axis=0)
        late["up_got"] = swap(late["up"], team[1])
        late["pieces"] = [lax.ppermute(send, BOTH, rounds(turn, False)) for turn in range(per_head)]
        return block

    pack = gather(pack, seq_high, True)
    in_low = gather(
        pack[:, :half_in],
        dp_bits + [near, core],
        True,
        {0: while_split, len(dp_bits) + 1: while_core},
        seq_high,
    )
    in_high = gather(pack[:, half_in:], [near] + dp_bits + [core], True, None, seq_high)
    full_out = in_high[:, wide - half_in :]

    features = patch_features.reshape(rows * patch_dev, vit)
    ones = jnp.zeros((rows * patch_dev, 128), BF16).at[:, 0].set(1)
    features_more = jnp.concatenate([features, ones], axis=1)
    patch_rows = dot_nt(features_more[:, :half_in], in_low) + dot_nt(
        features_more[:, half_in:], in_high[:, : wide - half_in]
    )
    units_eye = jnp.eye(8, 128, dtype=BF16)
    small = dot_nt(units_eye, in_high[:, wide - half_in - 128 : wide - half_in])
    gain_one, gain_two = small[1], small[2]
    table = small[3].reshape(dev_count, cols)[:, :bias_count].reshape(BUCKETS, HEADS)
    my_table = lax.dynamic_slice_in_dim(table, head, 1, 1).reshape(1, BUCKETS)
    resid = jnp.concatenate(
        [patch_rows.reshape(rows, patch_dev, d_model), text_embeds.astype(F32)], axis=1
    ).reshape(mine, d_model)
    normed_one = rms_norm(resid, gain_one).astype(BF16)
    half = d_model // 2
    order_low = seq_high + [near]
    order_high = [near] + seq_high
    for piece in late["pieces"]:
        normed_one = after(normed_one, piece)

    def while_start(block):
        block, late["ff_got"], late["up_got"] = together(block, late["ff_got"], late["up_got"])
        return block

    own_low = gather(normed_one[:, :half], order_low, False, {0: while_start})
    ff_block = jnp.concatenate([late["ff"], late["ff_got"]], axis=0)
    for step in dp_bits[:-1]:
        ff_block = jnp.concatenate([ff_block, swap(ff_block, step)], axis=0)
    ff_got = swap(ff_block, dp_bits[-1])
    team_up = jnp.concatenate([late["up"], late["up_got"]], axis=0)
    team_up = jnp.concatenate([team_up, swap(team_up, core)], axis=0)
    own_high = gather(normed_one[:, half:], order_high, False)
    own_low, own_high, ff_got = together(own_low, own_high, ff_got)
    full_gate, full_up, full_down = [
        jnp.concatenate([array[:, which * d_model : (which + 1) * d_model] for array in (ff_block, ff_got)], axis=0)
        for which in range(3)
    ]
    other_low, other_high = swap(own_low, core), swap(own_high, core)

    def my_rows(array):
        if twins == 1:
            return array
        view = array.reshape(chips, rows, tok, array.shape[1])
        view = lax.dynamic_slice_in_dim(view, twin * row_count, row_count, 1)
        return view.reshape(chips * row_count * tok, array.shape[1])

    pieces = jnp.stack(late["pieces"]).reshape(per_head, 3, cols, d_model)
    ordered = [
        lax.dynamic_index_in_dim(pieces, (place_in_head - i) % per_head, 0, keepdims=False)
        for i in range(per_head)
    ]
    w_head = jnp.stack(ordered, axis=1).reshape(3 * HEAD_DIM, d_model)
    normed_pairs = [
        (my_rows(own_low), my_rows(own_high)),
        (my_rows(other_low), my_rows(other_high)),
    ]
    qkv = [
        (dot_nt(low, w_head[:, :half]) + dot_nt(high, w_head[:, half:]))
        .astype(BF16)
        .reshape(chips, row_count, tok, 3 * HEAD_DIM)
        for low, high in normed_pairs
    ]
    lengths = lax.dynamic_slice_in_dim(text_lengths, twin * row_count, row_count, 0)
    me = seq_index.reshape(1).astype(jnp.int32)
    dims = (row_count, images, patch_dev, text_dev, slots)
    bias = call(
        bias_kernel, jax.ShapeDtypeStruct((SEG_Q, SEG_K), F32), [SMEM], (), 1 << 24, 1 << 20, 8
    )(my_table)
    text_rows = seq_count * TEXT_PITCH
    patches = seq_count * patch_dev
    packed_shape = jax.ShapeDtypeStruct((seq_count, tok, row_count * HEAD_DIM), BF16)
    mixed = call(
        lambda *refs: forward_kernel(dims, *refs),
        packed_shape,
        [SMEM, SMEM, VMEM, VMEM, VMEM],
        (
            pltpu.VMEM((row_count, patches, 3 * HEAD_DIM), BF16),
            pltpu.VMEM((row_count, text_rows, 3 * HEAD_DIM), BF16),
            pltpu.VMEM((row_count, patches, HEAD_DIM), BF16),
            pltpu.VMEM((row_count, text_rows, HEAD_DIM), F32),
        ),
        1 << 24,
        1 << 20,
        20,
    )(me, lengths, bias, *qkv)
    mixed_got = lax.all_to_all(mixed, SEQ, 0, 0, tiled=True)
    mixed_got = mixed_got.reshape(chips, 2, tok, row_count, HEAD_DIM).swapaxes(0, 1)
    mixed_got = mixed_got.reshape(HEADS, twins, tok, row_count, HEAD_DIM)
    attn_out = jnp.transpose(mixed_got, (1, 3, 2, 0, 4)).reshape(mine, d_model)
    resid_one = resid + dot_nt(attn_out, full_out)
    normed_two = rms_norm(resid_one, gain_two).astype(BF16)
    team_normed = normed_two
    for step in team:
        team_normed = jnp.concatenate([team_normed, swap(team_normed, step)], axis=0)
    gate_pre = dot_nt(team_normed, full_gate)
    up_pre = dot_nt(team_normed, full_up)
    hidden, gated_back = jax.vjp(gated_unit, gate_pre, up_pre)
    hidden = hidden.astype(BF16)

    d_gate, d_up = gated_back(dot_nt(team_up, full_down))
    d_gate, d_up = d_gate.astype(BF16), d_up.astype(BF16)
    d_normed_two = dot_nn(d_gate, full_gate) + dot_nn(d_up, full_up)
    state = {}

    def ff_take(keep):
        keep, got = together(keep, state["ff_got"])
        state["ff"] = state["ff_keep"].astype(F32) + got.astype(F32)
        return keep

    def ff_start(keep, step):
        count = state["ff"].shape[0] // 2
        state["ff_keep"] = state["ff"][:count]
        keep, send = together(keep, state["ff"][count:].astype(BF16))
        state["ff_got"] = swap(send, step)
        return keep

    def while_team(keep):
        keep, *grads = together(keep, d_gate, d_up, hidden)
        state["ff"] = jnp.concatenate(
            [
                dot_tn(grad, of).astype(BF16)
                for grad, of in zip(grads, (team_normed, team_normed, team_up))
            ],
            axis=1,
        )
        return ff_start(keep, dp_bits[-1])

    def team_sum(part, step, hook=None):
        keep, send = halves(part, step, [step], False)
        got = swap(send.astype(BF16), step)
        return (hook(keep) if hook else keep) + got.astype(F32)

    d_normed_two = team_sum(d_normed_two, team[2])
    d_normed_two = team_sum(d_normed_two, team[1], while_team)
    d_normed_two = team_sum(d_normed_two, team[0])
    _, norm_back_two = jax.vjp(rms_norm, resid_one, gain_two)
    d_resid_one, grad_gain_two = norm_back_two(d_normed_two)
    d_resid_one = d_resid_one + upstream.astype(F32)
    d_mix = d_resid_one.astype(BF16)
    d_attn = dot_nn(d_mix, full_out).astype(BF16)
    d_attn = d_attn.reshape(twins, row_count, tok, HEADS, HEAD_DIM)
    d_attn = jnp.transpose(d_attn, (3, 0, 2, 1, 4)).reshape(2, chips, tok, row_count * HEAD_DIM)
    d_attn = d_attn.swapaxes(0, 1).reshape(packed_shape.shape)
    d_attn_got = lax.all_to_all(d_attn, SEQ, 0, 0, tiled=True)

    out_grad = dot_tn(d_mix, attn_out).astype(BF16)
    out_part = team_sum(dot_nn(hidden, full_down), core)
    out_keep, send = halves(out_part, team[1], [team[1]], False)
    d_attn_got, out_grad, send = together(d_attn_got, out_grad, send.astype(BF16))
    out_got = swap(send, team[1])
    half_shape = jax.ShapeDtypeStruct(qkv[0].shape, BF16)
    d_own, d_other, d_bias = call(
        lambda *refs: backward_kernel(dims, *refs),
        (half_shape, half_shape, jax.ShapeDtypeStruct((SEG_Q, SEG_K), F32)),
        [SMEM, SMEM, VMEM, VMEM, VMEM, VMEM],
        (
            pltpu.VMEM((row_count, patches, 3 * HEAD_DIM), BF16),
            pltpu.VMEM((row_count, text_rows, 3 * HEAD_DIM), BF16),
            pltpu.VMEM((row_count, patches, HEAD_DIM), BF16),
            pltpu.VMEM((row_count, text_rows, HEAD_DIM), BF16),
            pltpu.VMEM((row_count, patches, 3 * HEAD_DIM), BF16),
            pltpu.VMEM((row_count, text_rows, 3 * HEAD_DIM), F32),
        ),
        1 << 24,
        1 << 20,
        28,
    )(me, lengths, bias, *qkv, d_attn_got)
    d_other, out_got = together(d_other, out_got)
    out_part = out_keep + out_got.astype(F32)
    d_qkv = [array.reshape(chips * row_count * tok, 3 * HEAD_DIM) for array in (d_own, d_other)]

    def all_rows(array):
        if twins == 1:
            return array
        view = array.reshape(chips, row_count, tok, array.shape[1])
        zero = jnp.zeros((chips, rows, tok, array.shape[1]), array.dtype)
        view = lax.dynamic_update_slice_in_dim(zero, view, twin * row_count, 1)
        return view.reshape(chips * mine, array.shape[1])

    chip_bits = seq_high + [near]
    weights = (w_head[:, :half], w_head[:, half:])
    sends = together(*[all_rows(dot_nn(d_qkv[1], part).astype(BF16)) for part in weights], d_own)
    others = [swap(send, core) for send in sends[:2]]
    d_qkv[0] = sends[2].reshape(d_qkv[0].shape)
    owns = [
        all_rows(dot_nn(d_qkv[0], part)) + other.astype(F32) for part, other in zip(weights, others)
    ]
    def while_first(keep):
        keep = ff_take(keep)
        for step in dp_bits[-2::-1]:
            keep = ff_take(ff_start(keep, step))
        for step in ff_far[:0:-1]:
            keep = ff_take(ff_start(keep, step))
        return keep

    def while_middle(keep):
        keep, grads_own, grads_other = together(keep, *d_qkv)
        d_head = jnp.concatenate(
            [
                dot_tn(grads_own, normed_pairs[0][which])
                + dot_tn(grads_other, normed_pairs[1][which])
                for which in range(2)
            ],
            axis=1,
        )
        d_head = d_head.reshape(3, per_head, cols, d_model).astype(BF16)
        sends = [
            lax.dynamic_index_in_dim(
                d_head, (place_in_head - turn) % per_head, 1, keepdims=False
            ).reshape(3 * cols, d_model)
            for turn in range(per_head)
        ]
        keep, *sends = together(keep, *sends)
        state["three"] = [
            lax.ppermute(send, BOTH, rounds(turn, True)) for turn, send in enumerate(sends)
        ]
        return keep

    def while_late(keep):
        keep, *state["three"] = together(keep, *state["three"])
        return keep

    low_sums = scatter_add(owns[0], order_low[::-1], chip_bits, False, {0: while_middle, 1: while_first, len(order_low) - 1: while_late})
    high_sums = scatter_add(owns[1], order_high[::-1], chip_bits, False)
    d_normed_one = jnp.concatenate([low_sums, high_sums], axis=1)
    d_table = call(
        bucket_kernel, jax.ShapeDtypeStruct((BUCKETS, 128), F32), [VMEM], (), 1 << 20, 1 << 20, 8
    )(d_bias)[:, 0]
    _, norm_back_one = jax.vjp(rms_norm, resid, gain_one)
    d_resid, grad_gain_one = norm_back_one(d_normed_one)
    d_resid = (d_resid + d_resid_one).reshape(rows, tok, d_model)
    text_grad = d_resid[:, patch_dev:]
    d_patch_rows = d_resid[:, :patch_dev].reshape(rows * patch_dev, d_model)
    d_low = d_patch_rows.astype(BF16)
    pos_grads = d_table[:, None] * (jnp.arange(HEADS)[None, :] == head).astype(F32)
    pos_grads = jnp.pad(
        pos_grads.reshape(dev_count, bias_count), ((0, 0), (0, cols - bias_count))
    ).reshape(1, d_model)
    small_grads = jnp.concatenate(
        [
            jnp.sum(d_patch_rows, axis=0)[None],
            grad_gain_one[None],
            grad_gain_two[None],
            pos_grads,
            jnp.zeros((12, d_model), F32),
        ],
        axis=0,
    ).astype(BF16)
    left = jnp.concatenate([d_low, small_grads], axis=0)
    right = jnp.concatenate(
        [
            jnp.pad(features, ((0, 0), (0, 128))),
            jnp.pad(jnp.eye(16, 128, dtype=BF16), ((0, 0), (vit, 0))),
        ],
        axis=0,
    )

    def while_core_again(keep):
        keep = ff_start(keep, ff_far[0])
        keep, part = together(keep, out_part)
        state["out_keep"], send = halves(part, team[0], [team[0]], False)
        state["out_got"] = swap(send.astype(BF16), team[0])
        keep, state["d_low"] = together(keep, d_low)
        return keep

    def while_half_again(keep):
        keep = ff_take(keep)
        down = state["ff"][:, 2 * d_model :]
        down_back = down.T.reshape(dev_count, cols, units)
        keep, down_back, state["out_got"] = together(keep, down_back, state["out_got"])
        state["down_back"] = lax.all_to_all(down_back, BOTH, 0, 0, tiled=True)
        return keep

    def while_end(keep):
        keep, state["down_back"] = together(keep, state["down_back"])
        return keep

    in_low_sums = scatter_add(
        dot_tn(left, right[:, :half_in]).astype(BF16),
        [core, near] + dp_bits[::-1],
        every,
        True,
        {0: while_core_again, 2: while_half_again},
    )
    in_high_sums = scatter_add(
        jnp.concatenate([dot_tn(left, right[:, half_in:]).astype(BF16), out_grad], axis=1),
        [core] + dp_bits[::-1] + [near],
        every,
        True,
    )
    in_grads = scatter_add(
        jnp.concatenate([in_low_sums, in_high_sums], axis=1),
        seq_high[::-1],
        seq_high,
        True,
        {len(seq_high) - 1: while_end},
    )
    small_out, grad_w_out = in_grads[:, vit:wide], in_grads[:, wide:]
    d_low = state["d_low"]
    feature_grad = jnp.concatenate(
        [dot_nn(d_low, in_low), dot_nn(d_low, in_high[:, : vit - half_in])], axis=1
    ).reshape(rows, patch_dev, vit)
    result = resid_one + state["out_keep"] + state["out_got"].astype(F32)
    result = result.astype(BF16).reshape(rows, tok, d_model)
    grad_gate = state["ff"][:, :d_model]
    grad_up = state["ff"][:, d_model : 2 * d_model]
    grad_down = jnp.transpose(state["down_back"], (0, 2, 1)).reshape(dev_count * units, cols)
    grad_down = grad_down.astype(F32)
    d_three = sum(got.astype(F32) for got in state["three"]).reshape(3, cols, d_model)
    return (
        result[:, :patch_dev],
        result[:, patch_dev:],
        feature_grad,
        text_grad,
        in_grads[:, :vit].T,
        small_out[:, 0],
        small_out[:, 1],
        d_three[0].T,
        d_three[1].T,
        d_three[2].T,
        grad_w_out.T,
        small_out[:, 2],
        grad_gate.T,
        grad_up.T,
        grad_down,
        small_out[:bias_count, 3],
    )


def solution(mesh):
    token = P("dp", SEQ, None)
    matrix = P(None, BOTH)
    vector = P(BOTH)
    return jax.shard_map(
        local,
        mesh=mesh,
        in_specs=(
            token, token, P("dp", None), matrix, vector, vector, matrix, matrix, matrix, matrix,
            vector, matrix, matrix, matrix, vector, token, token,
        ),
        out_specs=(
            token, token, token, token, matrix, vector, vector, matrix, matrix, matrix, matrix,
            vector, matrix, matrix, matrix, vector,
        ),
        check_vma=False,
    )
```

```python
import jax
import jax.numpy as jnp
from jax import lax
from jax.experimental import pallas as pl
from jax.experimental.pallas import tpu as pltpu
from jax.sharding import PartitionSpec as P

HEADS = 16
HEAD_DIM = 64
BUCKETS = 32
PATCHES_IMG = 256
TEXT_MOST = 192

EPSILON = 1e-06
MASKED = -1e30
STARTS = (0, 1, 2, 3, 4, 5, 6, 7, 8, 12, 16, 23, 32, 46, 64, 91)
BF16 = jnp.bfloat16
F32 = jnp.float32
INTERPRET = False

SEG_Q = PATCHES_IMG + TEXT_MOST
SEG_K = 2 * PATCHES_IMG
TEXT_K = SEG_K - PATCHES_IMG
TEXT_PITCH = 32


def dot_nt(left, right):
    return lax.dot_general(left, right, (((1,), (1,)), ((), ())), preferred_element_type=F32)


def dot_nn(left, right):
    return lax.dot_general(left, right, (((1,), (0,)), ((), ())), preferred_element_type=F32)


def dot_tn(left, right):
    return lax.dot_general(left, right, (((0,), (0,)), ((), ())), preferred_element_type=F32)


def rms_norm(values, gain):
    return values * lax.rsqrt(jnp.mean(values * values, axis=-1, keepdims=True) + EPSILON) * gain


def gelu_tanh(values):
    return (
        0.5
        * values
        * (1.0 + jnp.tanh(0.7978845608 * (values + 0.044715 * values * values * values)))
    )


def gated_unit(gate_pre, up_pre):
    return gelu_tanh(gate_pre) * up_pre


SEQ = "seq"
BOTH = ("dp", "seq")


def swap(array, step):
    axis, bit = step
    count = lax.axis_size(axis)
    return lax.ppermute(array, axis, [(i, i ^ (1 << bit)) for i in range(count)])


def my_bit(step):
    return (lax.axis_index(step[0]) >> step[1]) & 1


def rank(step):
    return (1000 if step[0] == "dp" else 0) + step[1]


def after(value, signal):
    return value + (signal[(0,) * signal.ndim] * 0).astype(value.dtype)


def together(*arrays):
    return lax.optimization_barrier(arrays)


def joined(mine, other, step, have, absolute):
    at = sum(1 for done in have if rank(done) > rank(step))
    if absolute:
        bit = my_bit(step) == 1
        mine, other = jnp.where(bit, other, mine), jnp.where(bit, mine, other)
    shape = (2**at, 1, mine.shape[0] >> at, mine.shape[1])
    return jnp.concatenate([mine.reshape(shape), other.reshape(shape)], axis=1).reshape(
        -1, mine.shape[1]
    )


def halves(grads, step, every, absolute):
    at = sum(1 for other in every if rank(other) > rank(step))
    rows, width = grads.shape[0] // 2, grads.shape[1]
    view = grads.reshape(2**at, 2, rows >> at, width)
    if absolute:
        bit = my_bit(step)
        keep = lax.dynamic_slice_in_dim(view, bit, 1, 1)
        send = lax.dynamic_slice_in_dim(view, 1 - bit, 1, 1)
    else:
        keep, send = view[:, 0], view[:, 1]
    return keep.reshape(rows, width), send.reshape(rows, width)


def gather(block, order, absolute, hooks=None, have=()):
    for number, step in enumerate(order):
        other = swap(block, step)
        if hooks and number in hooks:
            block = hooks[number](block)
        block = joined(block, other, step, list(have) + order[:number], absolute)
    return block


def scatter_add(grads, order, every, absolute, hooks=None):
    for number, step in enumerate(order):
        left = [other for other in every if other not in order[:number]]
        keep, send = halves(grads, step, left, absolute)
        other = swap(send.astype(BF16), step)
        if hooks and number in hooks:
            keep = hooks[number](keep)
        grads = keep.astype(F32) + other.astype(F32)
    return grads


def bias_kernel(table_ref, out_ref):
    delta = lax.broadcasted_iota(jnp.int32, out_ref.shape, 0) - lax.broadcasted_iota(
        jnp.int32, out_ref.shape, 1
    )
    value = jnp.full(out_ref.shape, table_ref[0, BUCKETS - 1], F32)
    for which in range(14, 0, -1):
        value = jnp.where(delta > -STARTS[which + 1], table_ref[0, 16 + which], value)
    for which in range(16):
        value = jnp.where(delta >= STARTS[which], table_ref[0, which], value)
    out_ref[...] = value


def bucket_kernel(d_ref, out_ref):
    shape = d_ref.shape
    delta = lax.broadcasted_iota(jnp.int32, shape, 0) - lax.broadcasted_iota(jnp.int32, shape, 1)
    values = d_ref[...]
    rows = []
    for which in range(BUCKETS):
        low = STARTS[which % 16]
        high = STARTS[which % 16 + 1] if which % 16 < 15 else 1 << 20
        if which < 16:
            inside = (delta >= low) & (delta < high)
        else:
            inside = (delta <= -max(low, 1)) & (delta > -high)
        rows.append(jnp.sum(jnp.where(inside, values, 0.0), axis=0, keepdims=True))
    sums = jnp.sum(jnp.concatenate(rows, axis=0), axis=1, keepdims=True)
    out_ref[...] = jnp.broadcast_to(sums, out_ref.shape)


def unpack(seq_count, where, row, pat_ref, txt_ref, patch_dev, text_dev, lanes):
    tail = TEXT_PITCH - text_dev
    for place in range(seq_count):
        block = where(place)
        patches = block[0:patch_dev, lanes]
        text = block[patch_dev : patch_dev + text_dev, lanes]
        pat_ref[row, place * patch_dev : (place + 1) * patch_dev, :] = patches
        txt_ref[row, place * TEXT_PITCH : place * TEXT_PITCH + text_dev, :] = text
        if tail:
            txt_ref[row, place * TEXT_PITCH + text_dev : (place + 1) * TEXT_PITCH, :] = jnp.zeros(
                (tail, text.shape[1]), text.dtype
            )


def picker(count, text_rows, text_dev, slot_count, first, length):
    shape = (count, text_rows)
    column = lax.broadcasted_iota(jnp.int32, shape, 1)
    inner = column & (TEXT_PITCH - 1)
    slot = (column // TEXT_PITCH) * text_dev + inner
    fill = jnp.where(slot >= slot_count // 2, slot - slot_count // 2, slot + slot_count // 2)
    line = lax.broadcasted_iota(jnp.int32, shape, 0)
    hit = (fill == first + line) & (line < length) & (inner < text_dev)
    return hit.astype(F32).astype(BF16)


def softmax(scores):
    top = jnp.max(scores, axis=-1, keepdims=True)
    expd = jnp.exp(scores - top)
    return expd / jnp.sum(expd, axis=-1, keepdims=True)


def segment_start(len_ref, row, which):
    return lax.fori_loop(0, which, lambda at, total: total + len_ref[row, at], jnp.int32(0))


class Halves:
    def __init__(self, me, own_ref, other_ref, row):
        self.me, self.own, self.other, self.row = me, own_ref, other_ref, row

    def at(self, place):
        apart = place ^ self.me
        return apart & 1, apart >> 1

    def __call__(self, place):
        odd, index = self.at(place)
        return jnp.where(odd == 1, self.other[index, self.row], self.own[index, self.row])


def forward_kernel(dims, me_ref, len_ref, bias_ref, own_ref, other_ref, o_ref, pat, txt, opat, otxt):
    rows, images, patch_dev, text_dev, slots = dims
    seq_count = 2 * own_ref.shape[0]
    text_rows = seq_count * TEXT_PITCH
    for row in range(rows):
        unpack(
            seq_count, Halves(me_ref[0], own_ref, other_ref, row),
            row, pat, txt, patch_dev, text_dev, slice(None),
        )
    otxt[...] = jnp.zeros_like(otxt)

    def attend(compact, queries, keys, length):
        q = compact[:queries, :HEAD_DIM]
        k = compact[:keys, HEAD_DIM : 2 * HEAD_DIM]
        v = compact[:keys, 2 * HEAD_DIM :]
        scores = dot_nt(q, k) + bias_ref[:queries, :keys]
        column = lax.broadcasted_iota(jnp.int32, scores.shape, 1)
        probs = softmax(jnp.where(column < length, scores, MASKED)).astype(BF16)
        return dot_nn(probs, v).astype(BF16)

    def one_segment(step, carry):
        row, image = step // images, step % images
        length = len_ref[row, image]
        first = segment_start(len_ref, row, image)
        pick = picker(TEXT_K, text_rows, text_dev, slots, first, length)
        text = dot_nn(pick, txt[row]).astype(BF16)
        at = pl.multiple_of(image * PATCHES_IMG, PATCHES_IMG)
        compact = jnp.concatenate([pat[row, pl.ds(at, PATCHES_IMG), :], text], axis=0)
        out = attend(compact, SEG_Q, SEG_K, PATCHES_IMG + length)
        opat[row, pl.ds(at, PATCHES_IMG), :] = out[:PATCHES_IMG]
        otxt[row] = otxt[row] + dot_tn(pick[:TEXT_MOST], out[PATCHES_IMG:])
        return carry

    lax.fori_loop(0, rows * images, one_segment, 0)
    pad_q = slots // 4
    pad_k = -(-pad_q // 128) * 128
    for row in range(rows):
        first = segment_start(len_ref, row, images)
        pick = picker(pad_k, text_rows, text_dev, slots, first, pad_q)
        compact = dot_nn(pick, txt[row]).astype(BF16)
        out = attend(compact, pad_q, pad_k, pad_q)
        otxt[row] = otxt[row] + dot_tn(pick[:pad_q], out)
    for place in range(seq_count):
        o_ref[place, 0:patch_dev, :] = jnp.concatenate(
            [opat[row, place * patch_dev : (place + 1) * patch_dev, :] for row in range(rows)],
            axis=1,
        )
        low = place * TEXT_PITCH
        o_ref[place, patch_dev : patch_dev + text_dev, :] = jnp.concatenate(
            [otxt[row, low : low + text_dev, :].astype(BF16) for row in range(rows)], axis=1
        )


def backward_kernel(
    dims, me_ref, len_ref, bias_ref, own_ref, other_ref, do_ref, down_ref, dother_ref, dbias_ref,
    pat, txt, dpat, dtxt, gpat, gtxt,
):
    rows, images, patch_dev, text_dev, slots = dims
    seq_count = 2 * own_ref.shape[0]
    text_rows = seq_count * TEXT_PITCH
    for row in range(rows):
        unpack(
            seq_count, Halves(me_ref[0], own_ref, other_ref, row),
            row, pat, txt, patch_dev, text_dev, slice(None),
        )
        unpack(
            seq_count, lambda place: do_ref.at[place],
            row, dpat, dtxt, patch_dev, text_dev,
            slice(row * HEAD_DIM, (row + 1) * HEAD_DIM),
        )
    gtxt[...] = jnp.zeros_like(gtxt)
    dbias_ref[...] = jnp.zeros_like(dbias_ref)

    def attend_back(compact, d_out, queries, keys, length):
        q = compact[:queries, :HEAD_DIM]
        k = compact[:keys, HEAD_DIM : 2 * HEAD_DIM]
        v = compact[:keys, 2 * HEAD_DIM :]
        scores = dot_nt(q, k) + bias_ref[:queries, :keys]
        column = lax.broadcasted_iota(jnp.int32, scores.shape, 1)
        probs = softmax(jnp.where(column < length, scores, MASKED))
        d_probs = dot_nt(d_out, v)
        centre = jnp.sum(d_probs * probs, axis=-1, keepdims=True)
        d_scores = probs * (d_probs - centre)
        d_low = d_scores.astype(BF16)
        d_q = dot_nn(d_low, k).astype(BF16)
        d_k = dot_tn(d_low, q).astype(BF16)
        d_v = dot_tn(probs.astype(BF16), d_out).astype(BF16)
        return d_scores, jnp.concatenate([d_q, d_k[:queries], d_v[:queries]], axis=1)

    def one_segment(step, carry):
        row, image = step // images, step % images
        length = len_ref[row, image]
        first = segment_start(len_ref, row, image)
        pick = picker(TEXT_K, text_rows, text_dev, slots, first, length)
        at = pl.multiple_of(image * PATCHES_IMG, PATCHES_IMG)
        text = dot_nn(pick, txt[row]).astype(BF16)
        compact = jnp.concatenate([pat[row, pl.ds(at, PATCHES_IMG), :], text], axis=0)
        text_do = dot_nn(pick[:TEXT_MOST], dtxt[row]).astype(BF16)
        d_out = jnp.concatenate([dpat[row, pl.ds(at, PATCHES_IMG), :], text_do], axis=0)
        d_scores, grads = attend_back(compact, d_out, SEG_Q, SEG_K, PATCHES_IMG + length)
        dbias_ref[...] = dbias_ref[...] + d_scores
        gpat[row, pl.ds(at, PATCHES_IMG), :] = grads[:PATCHES_IMG]
        gtxt[row] = gtxt[row] + dot_tn(pick[:TEXT_MOST], grads[PATCHES_IMG:])
        return carry

    lax.fori_loop(0, rows * images, one_segment, 0)
    pad_q = slots // 4
    pad_k = -(-pad_q // 128) * 128
    for row in range(rows):
        first = segment_start(len_ref, row, images)
        pick = picker(pad_k, text_rows, text_dev, slots, first, pad_q)
        compact = dot_nn(pick, txt[row]).astype(BF16)
        d_out = dot_nn(pick[:pad_q], dtxt[row]).astype(BF16)
        d_scores, grads = attend_back(compact, d_out, pad_q, pad_k, pad_q)
        dbias_ref[:pad_q, :pad_k] = dbias_ref[:pad_q, :pad_k] + d_scores
        gtxt[row] = gtxt[row] + dot_tn(pick[:pad_q], grads)
    for row in range(rows):
        for place in range(seq_count):
            odd, index = Halves(me_ref[0], own_ref, other_ref, row).at(place)
            low = place * TEXT_PITCH
            patches = gpat[row, place * patch_dev : (place + 1) * patch_dev, :]
            text = gtxt[row, low : low + text_dev, :].astype(BF16)

            def put(target):
                target[index, row, 0:patch_dev, :] = patches
                target[index, row, patch_dev : patch_dev + text_dev, :] = text

            pl.when(odd == 0)(lambda: put(down_ref))
            pl.when(odd == 1)(lambda: put(dother_ref))


def mix_kernel(chips, twins, got_ref, weight_ref, resid_ref, gain_ref, mixed_ref, sum_ref, norm_ref):
    tok, packed = got_ref.shape[1:]
    for twin in range(twins):
        for row in range(packed // HEAD_DIM):
            lanes = slice(row * HEAD_DIM, (row + 1) * HEAD_DIM)
            slots = [which * twins + twin for which in range(HEADS)]
            heads = [got_ref[2 * (slot % chips) + slot // chips, :, lanes] for slot in slots]
            low = (twin * (packed // HEAD_DIM) + row) * tok
            mixed_ref[low : low + tok, :] = jnp.concatenate(heads, axis=1)
    total = resid_ref[...] + dot_nt(mixed_ref[...], weight_ref[...])
    sum_ref[...] = total
    norm_ref[...] = rms_norm(total, gain_ref[...]).astype(BF16)


SMEM = pl.BlockSpec(memory_space=pltpu.SMEM)
VMEM = pl.BlockSpec(memory_space=pltpu.VMEM)


def call(kernel, out_shape, in_specs, scratch=(), flops=0, bytes_accessed=0, vmem=16):
    single = not isinstance(out_shape, (tuple, list))
    return pl.pallas_call(
        kernel,
        out_shape=out_shape,
        in_specs=in_specs,
        out_specs=VMEM if single else [VMEM] * len(out_shape),
        scratch_shapes=list(scratch),
        cost_estimate=pl.CostEstimate(
            flops=flops, bytes_accessed=bytes_accessed, transcendentals=0
        ),
        compiler_params=pltpu.CompilerParams(vmem_limit_bytes=vmem << 20),
        interpret=INTERPRET,
    )


def local(
    patch_features, text_embeds, text_lengths, w_in, b_in, gain_attn, w_query, w_key, w_value,
    w_out, gain_ffn, w_gate, w_up, w_down, position_bias, d_patch, d_text,
):
    seq_count, dp_count = lax.axis_size(SEQ), lax.axis_size("dp")
    dev_count = seq_count * dp_count
    seq_index, dp_index = lax.axis_index(SEQ), lax.axis_index("dp")
    rows, patch_dev, vit = patch_features.shape
    text_dev = text_embeds.shape[1]
    tok = patch_dev + text_dev
    mine = rows * tok
    d_model = text_embeds.shape[2]
    cols = w_in.shape[1]
    images = text_lengths.shape[1]
    slots = text_dev * seq_count
    core, near = ("seq", 0), ("seq", 1)
    seq_high = [("seq", bit) for bit in range(seq_count.bit_length() - 2, 1, -1)]
    dp_bits = [("dp", bit) for bit in range(dp_count.bit_length() - 1)]
    every = dp_bits + seq_high + [near, core]

    bias_count = position_bias.shape[0]
    pack = jnp.concatenate(
        [
            w_in,
            b_in[None],
            gain_attn[None],
            gain_ffn[None],
            jnp.pad(position_bias, (0, cols - bias_count))[None],
            jnp.zeros((124, cols), BF16),
            w_out,
        ],
        axis=0,
    ).T
    wide = vit + 128
    half_in = (wide + d_model) // 256 * 128
    half_back = wide // 256 * 128
    per_head = dev_count // HEADS
    twins = seq_count // HEADS
    chips = seq_count // 2
    head_slot = (seq_index % 2) * chips + seq_index // 2
    head = head_slot // twins
    twin = head_slot % twins
    place_in_head = dp_index * twins + twin
    row_count = rows // twins
    three = jnp.concatenate([w_query.T, w_key.T, w_value.T], axis=0)

    def to_rank(which_head, place):
        slot = which_head * twins + place % twins
        return (place // twins) * seq_count + 2 * (slot % chips) + slot // chips

    def rounds(turn, back):
        pairs = []
        for which_head in range(HEADS):
            for i in range(per_head):
                owner = which_head * per_head + i
                user = to_rank(which_head, (i + turn) % per_head)
                pairs.append((user, owner) if back else (owner, user))
        return pairs

    team = [("seq", 2), near, core]
    ff_far = [step for step in seq_high if step not in team]
    ff_order = ff_far + dp_bits
    units = w_gate.shape[1]
    down_out = jnp.transpose(w_down.reshape(dev_count, units, cols), (0, 2, 1))
    down_in = lax.all_to_all(down_out, BOTH, 0, 0, tiled=True)
    upstream = jnp.concatenate([d_patch, d_text], axis=1).reshape(mine, d_model)
    up_got = swap(upstream, team[0])
    late = {}

    def far_gather(block):
        for step in ff_far[:-1]:
            block = jnp.concatenate([block, swap(block, step)], axis=0)
        return block, swap(block, ff_far[-1])

    gate_up, gate_up_got = far_gather(jnp.concatenate([w_gate.T, w_up.T], axis=1))

    def while_near(block):
        block, got = together(block, up_got)
        late["up"] = jnp.concatenate([upstream, got], axis=0)
        return block

    def while_core(block):
        block, late["gate_up"] = together(block, gate_up_got)
        late["up_got"] = swap(late["up"], team[1])
        late["pieces"] = [lax.ppermute(three, BOTH, rounds(turn, False)) for turn in range(per_head)]
        return block

    pack = gather(pack, seq_high, True)
    in_low = gather(
        pack[:, :half_in],
        dp_bits + [near, core],
        True,
        {len(dp_bits): while_near, len(dp_bits) + 1: while_core},
        seq_high,
    )
    in_high = gather(pack[:, half_in:], [near] + dp_bits + [core], True, None, seq_high)
    full_out = in_high[:, wide - half_in :]

    features = patch_features.reshape(rows * patch_dev, vit)
    ones = jnp.zeros((rows * patch_dev, 128), BF16).at[:, 0].set(1)
    features_more = jnp.concatenate([features, ones], axis=1)
    patch_rows = dot_nt(features_more[:, :half_in], in_low) + dot_nt(
        features_more[:, half_in:], in_high[:, : wide - half_in]
    )
    units_eye = jnp.eye(8, 128, dtype=BF16)
    small = dot_nt(units_eye, in_high[:, wide - half_in - 128 : wide - half_in])
    gain_one, gain_two = small[1], small[2]
    table = small[3].reshape(dev_count, cols)[:, :bias_count].reshape(BUCKETS, HEADS)
    my_table = lax.dynamic_slice_in_dim(table, head, 1, 1).reshape(1, BUCKETS)
    resid = jnp.concatenate(
        [patch_rows.reshape(rows, patch_dev, d_model), text_embeds.astype(F32)], axis=1
    ).reshape(mine, d_model)
    normed_one = rms_norm(resid, gain_one).astype(BF16)
    half = d_model // 2
    order_low = seq_high + [near]
    order_high = [near] + seq_high
    normed_one, *late["pieces"] = together(normed_one, *late["pieces"])

    def while_start(block):
        block, late["up_got"] = together(block, late["up_got"])
        return block

    own_low = gather(normed_one[:, :half], order_low, False, {0: while_start})
    gate_up = jnp.concatenate([gate_up, late["gate_up"]], axis=0)
    for step in dp_bits[:-1]:
        gate_up = jnp.concatenate([gate_up, swap(gate_up, step)], axis=0)
    gate_up_got = swap(gate_up, dp_bits[-1])
    team_up = jnp.concatenate([late["up"], late["up_got"]], axis=0)
    team_up = jnp.concatenate([team_up, swap(team_up, core)], axis=0)
    own_high = gather(normed_one[:, half:], order_high, False)
    own_low, own_high = together(own_low, own_high)
    other_low, other_high = swap(own_low, core), swap(own_high, core)

    def my_rows(array):
        if twins == 1:
            return array
        view = array.reshape(chips, rows, tok, array.shape[1])
        view = lax.dynamic_slice_in_dim(view, twin * row_count, row_count, 1)
        return view.reshape(chips * row_count * tok, array.shape[1])

    pieces = jnp.stack(late["pieces"]).reshape(per_head, 3, cols, d_model)
    ordered = [
        lax.dynamic_index_in_dim(pieces, (place_in_head - i) % per_head, 0, keepdims=False)
        for i in range(per_head)
    ]
    w_head = jnp.stack(ordered, axis=1).reshape(3 * HEAD_DIM, d_model)
    normed_pairs = [
        (my_rows(own_low), my_rows(own_high)),
        (my_rows(other_low), my_rows(other_high)),
    ]
    qkv = [
        (dot_nt(low, w_head[:, :half]) + dot_nt(high, w_head[:, half:]))
        .astype(BF16)
        .reshape(chips, row_count, tok, 3 * HEAD_DIM)
        for low, high in normed_pairs
    ]
    *qkv, down = together(*qkv, down_in)
    full_down, down_got = far_gather(down.reshape(d_model, units).T)
    lengths = lax.dynamic_slice_in_dim(text_lengths, twin * row_count, row_count, 0)
    me = seq_index.reshape(1).astype(jnp.int32)
    dims = (row_count, images, patch_dev, text_dev, slots)
    bias = call(
        bias_kernel, jax.ShapeDtypeStruct((SEG_Q, SEG_K), F32), [SMEM], (), 1 << 24, 1 << 20, 8
    )(my_table)
    text_rows = seq_count * TEXT_PITCH
    patches = seq_count * patch_dev
    packed_shape = jax.ShapeDtypeStruct((seq_count, tok, row_count * HEAD_DIM), BF16)
    mixed = call(
        lambda *refs: forward_kernel(dims, *refs),
        packed_shape,
        [SMEM, SMEM, VMEM, VMEM, VMEM],
        (
            pltpu.VMEM((row_count, patches, 3 * HEAD_DIM), BF16),
            pltpu.VMEM((row_count, text_rows, 3 * HEAD_DIM), BF16),
            pltpu.VMEM((row_count, patches, HEAD_DIM), BF16),
            pltpu.VMEM((row_count, text_rows, HEAD_DIM), F32),
        ),
        1 << 24,
        1 << 20,
        20,
    )(me, lengths, bias, *qkv)
    mixed, gate_up_got, down_got = together(mixed, gate_up_got, down_got)
    full_gate, full_up = [
        jnp.concatenate([array[:, part] for array in (gate_up, gate_up_got)], axis=0)
        for part in (slice(0, d_model), slice(d_model, 2 * d_model))
    ]
    mixed_got = lax.all_to_all(mixed, SEQ, 0, 0, tiled=True)
    full_down = jnp.concatenate([full_down, down_got], axis=0)
    for step in dp_bits[:-1]:
        full_down = jnp.concatenate([full_down, swap(full_down, step)], axis=0)
    full_down = jnp.concatenate([full_down, swap(full_down, dp_bits[-1])], axis=0)
    attn_out, resid_one, normed_two = call(
        lambda *refs: mix_kernel(chips, twins, *refs),
        (
            jax.ShapeDtypeStruct((mine, d_model), BF16),
            jax.ShapeDtypeStruct((mine, d_model), F32),
            jax.ShapeDtypeStruct((mine, d_model), BF16),
        ),
        [VMEM, VMEM, VMEM, VMEM],
        (),
        1 << 24,
        1 << 20,
        12,
    )(mixed_got, full_out, resid, gain_two[None])
    team_normed = normed_two
    for step in team:
        got = swap(team_normed, step)
        if step == near:
            team_normed, full_gate, full_up, full_down = together(
                team_normed, full_gate, full_up, full_down
            )
        team_normed = jnp.concatenate([team_normed, got], axis=0)
    gate_pre = dot_nt(team_normed, full_gate)
    up_pre = dot_nt(team_normed, full_up)
    hidden, gated_back = jax.vjp(gated_unit, gate_pre, up_pre)
    hidden = hidden.astype(BF16)

    state = {}
    grad_down = dot_tn(hidden, team_up).astype(BF16)

    def down_start(step):
        count = grad_down_of["sum"].shape[0] // 2
        grad_down_of["keep"] = grad_down_of["sum"][:count]
        grad_down_of["got"] = swap(grad_down_of["sum"][count:].astype(BF16), step)

    def down_take(keep):
        keep, got = together(keep, grad_down_of["got"])
        grad_down_of["sum"] = grad_down_of["keep"].astype(F32) + got.astype(F32)
        return keep

    grad_down_of = {"sum": grad_down}
    down_start(dp_bits[-1])
    d_gate, d_up = gated_back(dot_nt(team_up, full_down))
    d_gate, d_up = d_gate.astype(BF16), d_up.astype(BF16)
    d_normed_two = dot_nn(d_gate, full_gate) + dot_nn(d_up, full_up)

    def ff_take(keep):
        keep, got = together(keep, state["ff_got"])
        state["ff"] = state["ff_keep"].astype(F32) + got.astype(F32)
        return keep

    def ff_start(keep, step):
        count = state["ff"].shape[0] // 2
        state["ff_keep"] = state["ff"][:count]
        keep, send = together(keep, state["ff"][count:].astype(BF16))
        state["ff_got"] = swap(send, step)
        return keep

    def while_team(keep):
        keep = down_take(keep)
        for step in dp_bits[-2::-1] + ff_far[:0:-1]:
            down_start(step)
            keep = down_take(keep)
        down_start(ff_far[0])
        keep, *grads = together(keep, d_gate, d_up)
        state["ff"] = jnp.concatenate(
            [dot_tn(grad, team_normed).astype(BF16) for grad in grads], axis=1
        )
        return ff_start(keep, dp_bits[-1])

    def team_sum(part, step, hook=None):
        keep, send = halves(part, step, [step], False)
        got = swap(send.astype(BF16), step)
        return (hook(keep) if hook else keep) + got.astype(F32)

    d_normed_two = team_sum(d_normed_two, team[2])
    d_normed_two = team_sum(d_normed_two, team[1], while_team)
    d_normed_two = team_sum(d_normed_two, team[0])
    _, norm_back_two = jax.vjp(rms_norm, resid_one, gain_two)
    d_resid_one, grad_gain_two = norm_back_two(d_normed_two)
    d_resid_one = d_resid_one + upstream.astype(F32)
    d_mix = d_resid_one.astype(BF16)
    d_attn = dot_nn(d_mix, full_out).astype(BF16)
    d_attn = d_attn.reshape(twins, row_count, tok, HEADS, HEAD_DIM)
    d_attn = jnp.transpose(d_attn, (3, 0, 2, 1, 4)).reshape(2, chips, tok, row_count * HEAD_DIM)
    d_attn = d_attn.swapaxes(0, 1).reshape(packed_shape.shape)
    d_attn_got = lax.all_to_all(d_attn, SEQ, 0, 0, tiled=True)

    out_grad = {"sum": dot_tn(d_mix, attn_out).astype(BF16), "left": list(every)}

    def out_grad_start(keep, step):
        out_grad["keep"], send = halves(out_grad["sum"], step, out_grad["left"], True)
        keep, send = together(keep, send.astype(BF16))
        out_grad["got"] = swap(send, step)
        return keep

    def out_grad_take(keep, step):
        keep, got = together(keep, out_grad["got"])
        out_grad["sum"] = out_grad["keep"].astype(F32) + got.astype(F32)
        out_grad["left"].remove(step)
        return keep

    out_part = team_sum(dot_nn(hidden, full_down), core)
    out_keep, send = halves(out_part, team[1], [team[1]], False)
    d_attn_got, send = together(out_grad_start(d_attn_got, core), send.astype(BF16))
    out_got = swap(send, team[1])
    half_shape = jax.ShapeDtypeStruct(qkv[0].shape, BF16)
    d_own, d_other, d_bias = call(
        lambda *refs: backward_kernel(dims, *refs),
        (half_shape, half_shape, jax.ShapeDtypeStruct((SEG_Q, SEG_K), F32)),
        [SMEM, SMEM, VMEM, VMEM, VMEM, VMEM],
        (
            pltpu.VMEM((row_count, patches, 3 * HEAD_DIM), BF16),
            pltpu.VMEM((row_count, text_rows, 3 * HEAD_DIM), BF16),
            pltpu.VMEM((row_count, patches, HEAD_DIM), BF16),
            pltpu.VMEM((row_count, text_rows, HEAD_DIM), BF16),
            pltpu.VMEM((row_count, patches, 3 * HEAD_DIM), BF16),
            pltpu.VMEM((row_count, text_rows, 3 * HEAD_DIM), F32),
        ),
        1 << 24,
        1 << 20,
        28,
    )(me, lengths, bias, *qkv, d_attn_got)
    d_other, out_got = together(down_take(d_other), out_got)
    out_part = out_keep + out_got.astype(F32)
    down_back = grad_down_of["sum"].T.reshape(dev_count, cols, units)
    state["down_back"] = lax.all_to_all(down_back, BOTH, 0, 0, tiled=True)
    d_qkv = [array.reshape(chips * row_count * tok, 3 * HEAD_DIM) for array in (d_own, d_other)]

    def all_rows(array):
        if twins == 1:
            return array
        view = array.reshape(chips, row_count, tok, array.shape[1])
        zero = jnp.zeros((chips, rows, tok, array.shape[1]), array.dtype)
        view = lax.dynamic_update_slice_in_dim(zero, view, twin * row_count, 1)
        return view.reshape(chips * mine, array.shape[1])

    chip_bits = seq_high + [near]
    weights = (w_head[:, :half], w_head[:, half:])
    sends = together(*[all_rows(dot_nn(d_qkv[1], part).astype(BF16)) for part in weights], d_own)
    others = [swap(send, core) for send in sends[:2]]
    d_qkv[0] = sends[2].reshape(d_qkv[0].shape)
    owns = [
        all_rows(dot_nn(d_qkv[0], part)) + other.astype(F32) for part, other in zip(weights, others)
    ]
    def while_first(keep):
        keep = ff_take(keep)
        for step in dp_bits[-2::-1]:
            keep = ff_take(ff_start(keep, step))
        for step in ff_far[:0:-1]:
            keep = ff_take(ff_start(keep, step))
        keep = out_grad_take(keep, dp_bits[-1])
        for step in dp_bits[-2::-1]:
            keep = out_grad_take(out_grad_start(keep, step), step)
        return out_grad_start(keep, near)

    def while_middle(keep):
        keep = out_grad_start(out_grad_take(keep, core), dp_bits[-1])
        keep, grads_own, grads_other = together(keep, *d_qkv)
        d_head = jnp.concatenate(
            [
                dot_tn(grads_own, normed_pairs[0][which])
                + dot_tn(grads_other, normed_pairs[1][which])
                for which in range(2)
            ],
            axis=1,
        )
        d_head = d_head.reshape(3, per_head, cols, d_model).astype(BF16)
        sends = [
            lax.dynamic_index_in_dim(
                d_head, (place_in_head - turn) % per_head, 1, keepdims=False
            ).reshape(3 * cols, d_model)
            for turn in range(per_head)
        ]
        keep, *sends = together(keep, *sends)
        state["three"] = [
            lax.ppermute(send, BOTH, rounds(turn, True)) for turn, send in enumerate(sends)
        ]
        return keep

    def while_late(keep):
        keep, *state["three"] = together(keep, *state["three"])
        return out_grad_take(keep, near)

    low_sums = scatter_add(owns[0], order_low[::-1], chip_bits, False, {0: while_middle, 1: while_first, len(order_low) - 1: while_late})
    high_sums = scatter_add(owns[1], order_high[::-1], chip_bits, False)
    d_normed_one = jnp.concatenate([low_sums, high_sums], axis=1)
    d_table = call(
        bucket_kernel, jax.ShapeDtypeStruct((BUCKETS, 128), F32), [VMEM], (), 1 << 20, 1 << 20, 8
    )(d_bias)[:, 0]
    _, norm_back_one = jax.vjp(rms_norm, resid, gain_one)
    d_resid, grad_gain_one = norm_back_one(d_normed_one)
    d_resid = (d_resid + d_resid_one).reshape(rows, tok, d_model)
    text_grad = d_resid[:, patch_dev:]
    d_patch_rows = d_resid[:, :patch_dev].reshape(rows * patch_dev, d_model)
    d_low = d_patch_rows.astype(BF16)
    pos_grads = d_table[:, None] * (jnp.arange(HEADS)[None, :] == head).astype(F32)
    pos_grads = jnp.pad(
        pos_grads.reshape(dev_count, bias_count), ((0, 0), (0, cols - bias_count))
    ).reshape(1, d_model)
    small_grads = jnp.concatenate(
        [
            jnp.sum(d_patch_rows, axis=0)[None],
            grad_gain_one[None],
            grad_gain_two[None],
            pos_grads,
            jnp.zeros((12, d_model), F32),
        ],
        axis=0,
    ).astype(BF16)
    left = jnp.concatenate([d_low, small_grads], axis=0)
    right = jnp.concatenate(
        [
            jnp.pad(features, ((0, 0), (0, 128))),
            jnp.pad(jnp.eye(16, 128, dtype=BF16), ((0, 0), (vit, 0))),
        ],
        axis=0,
    )

    def while_core_again(keep):
        keep = ff_start(keep, ff_far[0])
        keep, part = together(keep, out_part)
        state["out_keep"], send = halves(part, team[0], [team[0]], False)
        state["out_got"] = swap(send.astype(BF16), team[0])
        keep, state["d_low"] = together(keep, d_low)
        return keep

    def while_half_again(keep):
        keep, state["out_got"] = together(ff_take(keep), state["out_got"])
        return keep

    def while_end(keep):
        keep, state["down_back"] = together(keep, state["down_back"])
        return keep

    in_low_sums = scatter_add(
        dot_tn(left, right[:, :half_back]).astype(BF16),
        [core, near] + dp_bits[::-1],
        every,
        True,
        {0: while_core_again, 2: while_half_again},
    )
    in_high_sums = scatter_add(
        dot_tn(left, right[:, half_back:]).astype(BF16),
        [core] + dp_bits[::-1] + [near],
        every,
        True,
    )
    in_grads = scatter_add(
        jnp.concatenate([in_low_sums, in_high_sums, out_grad["sum"]], axis=1),
        seq_high[::-1],
        seq_high,
        True,
        {0: while_end},
    )
    small_out, grad_w_out = in_grads[:, vit:wide], in_grads[:, wide:]
    d_low = state["d_low"]
    feature_grad = jnp.concatenate(
        [dot_nn(d_low, in_low), dot_nn(d_low, in_high[:, : vit - half_in])], axis=1
    ).reshape(rows, patch_dev, vit)
    result = resid_one + state["out_keep"] + state["out_got"].astype(F32)
    result = result.astype(BF16).reshape(rows, tok, d_model)
    grad_gate, grad_up = state["ff"][:, :d_model], state["ff"][:, d_model:]
    grad_down = jnp.transpose(state["down_back"], (0, 2, 1)).reshape(dev_count * units, cols)
    grad_down = grad_down.astype(F32)
    d_three = sum(got.astype(F32) for got in state["three"]).reshape(3, cols, d_model)
    return (
        result[:, :patch_dev],
        result[:, patch_dev:],
        feature_grad,
        text_grad,
        in_grads[:, :vit].T,
        small_out[:, 0],
        small_out[:, 1],
        d_three[0].T,
        d_three[1].T,
        d_three[2].T,
        grad_w_out.T,
        small_out[:, 2],
        grad_gate.T,
        grad_up.T,
        grad_down,
        small_out[:bias_count, 3],
    )


def solution(mesh):
    token = P("dp", SEQ, None)
    matrix = P(None, BOTH)
    vector = P(BOTH)
    return jax.shard_map(
        local,
        mesh=mesh,
        in_specs=(
            token, token, P("dp", None), matrix, vector, vector, matrix, matrix, matrix, matrix,
            vector, matrix, matrix, matrix, vector, token, token,
        ),
        out_specs=(
            token, token, token, token, matrix, vector, vector, matrix, matrix, matrix, matrix,
            vector, matrix, matrix, matrix, vector,
        ),
        check_vma=False,
    )
```

```python
import jax
import jax.numpy as jnp
from jax import lax
from jax.experimental import pallas as pl
from jax.experimental.pallas import tpu as pltpu
from jax.sharding import PartitionSpec as P

HEADS = 16
HEAD_DIM = 64
BUCKETS = 32
PATCHES_IMG = 256
TEXT_MOST = 192

EPSILON = 1e-06
MASKED = -1e30
STARTS = (0, 1, 2, 3, 4, 5, 6, 7, 8, 12, 16, 23, 32, 46, 64, 91)
BF16 = jnp.bfloat16
F32 = jnp.float32
INTERPRET = False

SEG_Q = PATCHES_IMG + TEXT_MOST
SEG_K = 2 * PATCHES_IMG
TEXT_K = SEG_K - PATCHES_IMG
TEXT_PITCH = 32


def dot_nt(left, right):
    return lax.dot_general(left, right, (((1,), (1,)), ((), ())), preferred_element_type=F32)


def dot_nn(left, right):
    return lax.dot_general(left, right, (((1,), (0,)), ((), ())), preferred_element_type=F32)


def dot_tn(left, right):
    return lax.dot_general(left, right, (((0,), (0,)), ((), ())), preferred_element_type=F32)


def rms_norm(values, gain):
    return values * lax.rsqrt(jnp.mean(values * values, axis=-1, keepdims=True) + EPSILON) * gain


def gelu_tanh(values):
    return (
        0.5
        * values
        * (1.0 + jnp.tanh(0.7978845608 * (values + 0.044715 * values * values * values)))
    )


def gated_unit(gate_pre, up_pre):
    return gelu_tanh(gate_pre) * up_pre


SEQ = "seq"
BOTH = ("dp", "seq")


def swap(array, step):
    axis, bit = step
    count = lax.axis_size(axis)
    return lax.ppermute(array, axis, [(i, i ^ (1 << bit)) for i in range(count)])


def my_bit(step):
    return (lax.axis_index(step[0]) >> step[1]) & 1


def rank(step):
    return (1000 if step[0] == "dp" else 0) + step[1]


def after(value, signal):
    return value + (signal[(0,) * signal.ndim] * 0).astype(value.dtype)


def together(*arrays):
    return lax.optimization_barrier(arrays)


def joined(mine, other, step, have, absolute):
    at = sum(1 for done in have if rank(done) > rank(step))
    if absolute:
        bit = my_bit(step) == 1
        mine, other = jnp.where(bit, other, mine), jnp.where(bit, mine, other)
    shape = (2**at, 1, mine.shape[0] >> at, mine.shape[1])
    return jnp.concatenate([mine.reshape(shape), other.reshape(shape)], axis=1).reshape(
        -1, mine.shape[1]
    )


def halves(grads, step, every, absolute):
    at = sum(1 for other in every if rank(other) > rank(step))
    rows, width = grads.shape[0] // 2, grads.shape[1]
    view = grads.reshape(2**at, 2, rows >> at, width)
    if absolute:
        bit = my_bit(step)
        keep = lax.dynamic_slice_in_dim(view, bit, 1, 1)
        send = lax.dynamic_slice_in_dim(view, 1 - bit, 1, 1)
    else:
        keep, send = view[:, 0], view[:, 1]
    return keep.reshape(rows, width), send.reshape(rows, width)


def gather(block, order, absolute, hooks=None, have=()):
    for number, step in enumerate(order):
        other = swap(block, step)
        if hooks and number in hooks:
            block = hooks[number](block)
        block = joined(block, other, step, list(have) + order[:number], absolute)
    return block


def scatter_add(grads, order, every, absolute, hooks=None):
    for number, step in enumerate(order):
        left = [other for other in every if other not in order[:number]]
        keep, send = halves(grads, step, left, absolute)
        other = swap(send.astype(BF16), step)
        if hooks and number in hooks:
            keep = hooks[number](keep)
        grads = keep.astype(F32) + other.astype(F32)
    return grads


def scatter_add_pair(low, high, order_low, order_high, every, absolute, hooks):
    for number, (step_low, step_high) in enumerate(zip(order_low, order_high)):
        left_low = [other for other in every if other not in order_low[:number]]
        left_high = [other for other in every if other not in order_high[:number]]
        keep_low, send_low = halves(low, step_low, left_low, absolute)
        keep_high, send_high = halves(high, step_high, left_high, absolute)
        send_low, send_high = together(send_low.astype(BF16), send_high.astype(BF16))
        got_low, got_high = swap(send_low, step_low), swap(send_high, step_high)
        if number in hooks:
            keep_low = hooks[number](keep_low)
        low = keep_low.astype(F32) + got_low.astype(F32)
        high = keep_high.astype(F32) + got_high.astype(F32)
    return low, high


def bias_kernel(table_ref, out_ref):
    delta = lax.broadcasted_iota(jnp.int32, out_ref.shape, 0) - lax.broadcasted_iota(
        jnp.int32, out_ref.shape, 1
    )
    value = jnp.full(out_ref.shape, table_ref[0, BUCKETS - 1], F32)
    for which in range(14, 0, -1):
        value = jnp.where(delta > -STARTS[which + 1], table_ref[0, 16 + which], value)
    for which in range(16):
        value = jnp.where(delta >= STARTS[which], table_ref[0, which], value)
    out_ref[...] = value


def bucket_kernel(d_ref, out_ref):
    shape = d_ref.shape
    delta = lax.broadcasted_iota(jnp.int32, shape, 0) - lax.broadcasted_iota(jnp.int32, shape, 1)
    values = d_ref[...]
    rows = []
    for which in range(BUCKETS):
        low = STARTS[which % 16]
        high = STARTS[which % 16 + 1] if which % 16 < 15 else 1 << 20
        if which < 16:
            inside = (delta >= low) & (delta < high)
        else:
            inside = (delta <= -max(low, 1)) & (delta > -high)
        rows.append(jnp.sum(jnp.where(inside, values, 0.0), axis=0, keepdims=True))
    sums = jnp.sum(jnp.concatenate(rows, axis=0), axis=1, keepdims=True)
    out_ref[...] = jnp.broadcast_to(sums, out_ref.shape)


def unpack(seq_count, where, row, pat_ref, txt_ref, patch_dev, text_dev, lanes):
    tail = TEXT_PITCH - text_dev
    for place in range(seq_count):
        block = where(place)
        patches = block[0:patch_dev, lanes]
        text = block[patch_dev : patch_dev + text_dev, lanes]
        pat_ref[row, place * patch_dev : (place + 1) * patch_dev, :] = patches
        txt_ref[row, place * TEXT_PITCH : place * TEXT_PITCH + text_dev, :] = text
        if tail:
            txt_ref[row, place * TEXT_PITCH + text_dev : (place + 1) * TEXT_PITCH, :] = jnp.zeros(
                (tail, text.shape[1]), text.dtype
            )


def picker(count, text_rows, text_dev, slot_count, first, length):
    column = lax.broadcasted_iota(jnp.int32, (1, text_rows), 1)
    inner = column & (TEXT_PITCH - 1)
    slot = (column // TEXT_PITCH) * text_dev + inner
    fill = jnp.where(slot >= slot_count // 2, slot - slot_count // 2, slot + slot_count // 2)
    fill = jnp.where(inner < text_dev, fill, -1)
    line = lax.broadcasted_iota(jnp.int32, (count, 1), 0)
    wanted = jnp.where(line < length, first + line, -2)
    return (fill == wanted).astype(F32).astype(BF16)


def masked_keys(keys, length):
    column = lax.broadcasted_iota(jnp.int32, (1, keys), 1)
    return jnp.where(column < length, 0.0, MASKED)


def softmax(scores):
    top = jnp.max(scores, axis=-1, keepdims=True)
    expd = jnp.exp(scores - top)
    return expd * (1.0 / jnp.sum(expd, axis=-1, keepdims=True))


def segment_start(len_ref, row, which):
    return lax.fori_loop(0, which, lambda at, total: total + len_ref[row, at], jnp.int32(0))


class Halves:
    def __init__(self, me, own_ref, other_ref, row):
        self.me, self.own, self.other, self.row = me, own_ref, other_ref, row

    def at(self, place):
        apart = place ^ self.me
        return apart & 1, apart >> 1

    def __call__(self, place):
        odd, index = self.at(place)
        return jnp.where(odd == 1, self.other[index, self.row], self.own[index, self.row])


def forward_kernel(dims, me_ref, len_ref, bias_ref, own_ref, other_ref, o_ref, pat, txt, opat, otxt):
    rows, images, patch_dev, text_dev, slots = dims
    seq_count = 2 * own_ref.shape[0]
    text_rows = seq_count * TEXT_PITCH
    for row in range(rows):
        unpack(
            seq_count, Halves(me_ref[0], own_ref, other_ref, row),
            row, pat, txt, patch_dev, text_dev, slice(None),
        )
    otxt[...] = jnp.zeros_like(otxt)

    def attend(compact, queries, keys, length):
        q = compact[:queries, :HEAD_DIM]
        k = compact[:keys, HEAD_DIM : 2 * HEAD_DIM]
        v = compact[:keys, 2 * HEAD_DIM :]
        scores = dot_nt(q, k) + bias_ref[:queries, :keys] + masked_keys(keys, length)
        probs = softmax(scores).astype(BF16)
        return dot_nn(probs, v).astype(BF16)

    def one_segment(step, carry):
        row, image = step // images, step % images
        length = len_ref[row, image]
        first = segment_start(len_ref, row, image)
        pick = picker(TEXT_K, text_rows, text_dev, slots, first, length)
        text = dot_nn(pick, txt[row]).astype(BF16)
        at = pl.multiple_of(image * PATCHES_IMG, PATCHES_IMG)
        compact = jnp.concatenate([pat[row, pl.ds(at, PATCHES_IMG), :], text], axis=0)
        out = attend(compact, SEG_Q, SEG_K, PATCHES_IMG + length)
        opat[row, pl.ds(at, PATCHES_IMG), :] = out[:PATCHES_IMG]
        otxt[row] = otxt[row] + dot_tn(pick[:TEXT_MOST], out[PATCHES_IMG:])
        return carry

    lax.fori_loop(0, rows * images, one_segment, 0)
    pad_q = slots // 4
    pad_k = -(-pad_q // 128) * 128
    for row in range(rows):
        first = segment_start(len_ref, row, images)
        pick = picker(pad_k, text_rows, text_dev, slots, first, pad_q)
        compact = dot_nn(pick, txt[row]).astype(BF16)
        out = attend(compact, pad_q, pad_k, pad_q)
        otxt[row] = otxt[row] + dot_tn(pick[:pad_q], out)
    for place in range(seq_count):
        o_ref[place, 0:patch_dev, :] = jnp.concatenate(
            [opat[row, place * patch_dev : (place + 1) * patch_dev, :] for row in range(rows)],
            axis=1,
        )
        low = place * TEXT_PITCH
        o_ref[place, patch_dev : patch_dev + text_dev, :] = jnp.concatenate(
            [otxt[row, low : low + text_dev, :].astype(BF16) for row in range(rows)], axis=1
        )


def backward_kernel(
    dims, me_ref, len_ref, bias_ref, own_ref, other_ref, do_ref, down_ref, dother_ref, dbias_ref,
    pat, txt, dpat, dtxt, gpat, gtxt,
):
    rows, images, patch_dev, text_dev, slots = dims
    seq_count = 2 * own_ref.shape[0]
    text_rows = seq_count * TEXT_PITCH
    for row in range(rows):
        unpack(
            seq_count, Halves(me_ref[0], own_ref, other_ref, row),
            row, pat, txt, patch_dev, text_dev, slice(None),
        )
        unpack(
            seq_count, lambda place: do_ref.at[place],
            row, dpat, dtxt, patch_dev, text_dev,
            slice(row * HEAD_DIM, (row + 1) * HEAD_DIM),
        )
    gtxt[...] = jnp.zeros_like(gtxt)
    dbias_ref[...] = jnp.zeros_like(dbias_ref)

    def attend_back(compact, d_out, queries, keys, length):
        q = compact[:queries, :HEAD_DIM]
        k = compact[:keys, HEAD_DIM : 2 * HEAD_DIM]
        v = compact[:keys, 2 * HEAD_DIM :]
        scores = dot_nt(q, k) + bias_ref[:queries, :keys] + masked_keys(keys, length)
        probs = softmax(scores)
        d_probs = dot_nt(d_out, v)
        centre = jnp.sum(d_probs * probs, axis=-1, keepdims=True)
        d_scores = probs * (d_probs - centre)
        d_low = d_scores.astype(BF16)
        d_q = dot_nn(d_low, k).astype(BF16)
        d_k = dot_tn(d_low, q).astype(BF16)
        d_v = dot_tn(probs.astype(BF16), d_out).astype(BF16)
        return d_scores, jnp.concatenate([d_q, d_k[:queries], d_v[:queries]], axis=1)

    def one_segment(step, carry):
        row, image = step // images, step % images
        length = len_ref[row, image]
        first = segment_start(len_ref, row, image)
        pick = picker(TEXT_K, text_rows, text_dev, slots, first, length)
        at = pl.multiple_of(image * PATCHES_IMG, PATCHES_IMG)
        text = dot_nn(pick, txt[row]).astype(BF16)
        compact = jnp.concatenate([pat[row, pl.ds(at, PATCHES_IMG), :], text], axis=0)
        text_do = dot_nn(pick[:TEXT_MOST], dtxt[row]).astype(BF16)
        d_out = jnp.concatenate([dpat[row, pl.ds(at, PATCHES_IMG), :], text_do], axis=0)
        d_scores, grads = attend_back(compact, d_out, SEG_Q, SEG_K, PATCHES_IMG + length)
        dbias_ref[...] = dbias_ref[...] + d_scores
        gpat[row, pl.ds(at, PATCHES_IMG), :] = grads[:PATCHES_IMG]
        gtxt[row] = gtxt[row] + dot_tn(pick[:TEXT_MOST], grads[PATCHES_IMG:])
        return carry

    lax.fori_loop(0, rows * images, one_segment, 0)
    pad_q = slots // 4
    pad_k = -(-pad_q // 128) * 128
    for row in range(rows):
        first = segment_start(len_ref, row, images)
        pick = picker(pad_k, text_rows, text_dev, slots, first, pad_q)
        compact = dot_nn(pick, txt[row]).astype(BF16)
        d_out = dot_nn(pick[:pad_q], dtxt[row]).astype(BF16)
        d_scores, grads = attend_back(compact, d_out, pad_q, pad_k, pad_q)
        dbias_ref[:pad_q, :pad_k] = dbias_ref[:pad_q, :pad_k] + d_scores
        gtxt[row] = gtxt[row] + dot_tn(pick[:pad_q], grads)
    for row in range(rows):
        for place in range(seq_count):
            odd, index = Halves(me_ref[0], own_ref, other_ref, row).at(place)
            low = place * TEXT_PITCH
            patches = gpat[row, place * patch_dev : (place + 1) * patch_dev, :]
            text = gtxt[row, low : low + text_dev, :].astype(BF16)

            def put(target):
                target[index, row, 0:patch_dev, :] = patches
                target[index, row, patch_dev : patch_dev + text_dev, :] = text

            pl.when(odd == 0)(lambda: put(down_ref))
            pl.when(odd == 1)(lambda: put(dother_ref))


def mix_kernel(chips, twins, got_ref, weight_ref, resid_ref, gain_ref, mixed_ref, sum_ref, norm_ref):
    tok, packed = got_ref.shape[1:]
    for twin in range(twins):
        for row in range(packed // HEAD_DIM):
            lanes = slice(row * HEAD_DIM, (row + 1) * HEAD_DIM)
            slots = [which * twins + twin for which in range(HEADS)]
            heads = [got_ref[2 * (slot % chips) + slot // chips, :, lanes] for slot in slots]
            low = (twin * (packed // HEAD_DIM) + row) * tok
            mixed_ref[low : low + tok, :] = jnp.concatenate(heads, axis=1)
    total = resid_ref[...] + dot_nt(mixed_ref[...], weight_ref[...])
    sum_ref[...] = total
    norm_ref[...] = rms_norm(total, gain_ref[...]).astype(BF16)


SMEM = pl.BlockSpec(memory_space=pltpu.SMEM)
VMEM = pl.BlockSpec(memory_space=pltpu.VMEM)


def call(kernel, out_shape, in_specs, scratch=(), flops=0, bytes_accessed=0, vmem=16):
    single = not isinstance(out_shape, (tuple, list))
    return pl.pallas_call(
        kernel,
        out_shape=out_shape,
        in_specs=in_specs,
        out_specs=VMEM if single else [VMEM] * len(out_shape),
        scratch_shapes=list(scratch),
        cost_estimate=pl.CostEstimate(
            flops=flops, bytes_accessed=bytes_accessed, transcendentals=0
        ),
        compiler_params=pltpu.CompilerParams(vmem_limit_bytes=vmem << 20),
        interpret=INTERPRET,
    )


def local(
    patch_features, text_embeds, text_lengths, w_in, b_in, gain_attn, w_query, w_key, w_value,
    w_out, gain_ffn, w_gate, w_up, w_down, position_bias, d_patch, d_text,
):
    seq_count, dp_count = lax.axis_size(SEQ), lax.axis_size("dp")
    dev_count = seq_count * dp_count
    seq_index, dp_index = lax.axis_index(SEQ), lax.axis_index("dp")
    rows, patch_dev, vit = patch_features.shape
    text_dev = text_embeds.shape[1]
    tok = patch_dev + text_dev
    mine = rows * tok
    d_model = text_embeds.shape[2]
    cols = w_in.shape[1]
    images = text_lengths.shape[1]
    slots = text_dev * seq_count
    core, near = ("seq", 0), ("seq", 1)
    seq_high = [("seq", bit) for bit in range(seq_count.bit_length() - 2, 1, -1)]
    dp_bits = [("dp", bit) for bit in range(dp_count.bit_length() - 1)]
    every = dp_bits + seq_high + [near, core]

    bias_count = position_bias.shape[0]
    pack = jnp.concatenate(
        [
            w_in,
            b_in[None],
            gain_attn[None],
            gain_ffn[None],
            jnp.pad(position_bias, (0, cols - bias_count))[None],
            jnp.zeros((124, cols), BF16),
            w_out,
        ],
        axis=0,
    ).T
    wide = vit + 128
    half_in = wide // 256 * 128
    per_head = dev_count // HEADS
    twins = seq_count // HEADS
    chips = seq_count // 2
    head_slot = (seq_index % 2) * chips + seq_index // 2
    head = head_slot // twins
    twin = head_slot % twins
    place_in_head = dp_index * twins + twin
    row_count = rows // twins
    three = jnp.concatenate([w_query.T, w_key.T, w_value.T], axis=0)

    def to_rank(which_head, place):
        slot = which_head * twins + place % twins
        return (place // twins) * seq_count + 2 * (slot % chips) + slot // chips

    def rounds(turn, back):
        pairs = []
        for which_head in range(HEADS):
            for i in range(per_head):
                owner = which_head * per_head + i
                user = to_rank(which_head, (i + turn) % per_head)
                pairs.append((user, owner) if back else (owner, user))
        return pairs

    team = [("seq", 2), near, core]
    ff_far = [step for step in seq_high if step not in team]
    ff_order = ff_far + dp_bits
    units = w_gate.shape[1]
    down_out = jnp.transpose(w_down.reshape(dev_count, units, cols), (0, 2, 1))
    down_in = lax.all_to_all(down_out, BOTH, 0, 0, tiled=True)
    upstream = jnp.concatenate([d_patch, d_text], axis=1).reshape(mine, d_model)
    up_got = swap(upstream, team[0])
    late = {}

    def far_gather(block):
        for step in ff_far[:-1]:
            block = jnp.concatenate([block, swap(block, step)], axis=0)
        return block, swap(block, ff_far[-1])

    gate_up, gate_up_got = far_gather(jnp.concatenate([w_gate.T, w_up.T], axis=1))

    def while_near(block):
        block, late["gate_up"] = together(block, gate_up_got)
        return block

    def while_core(block):
        block, got = together(block, up_got)
        late["up"] = jnp.concatenate([upstream, got], axis=0)
        late["up_got"] = swap(late["up"], team[1])
        late["pieces"] = [lax.ppermute(three, BOTH, rounds(turn, False)) for turn in range(per_head)]
        return block

    pack = gather(pack, seq_high, True)
    in_low = gather(
        pack[:, :half_in],
        dp_bits + [near, core],
        True,
        {len(dp_bits): while_near, len(dp_bits) + 1: while_core},
        seq_high,
    )
    in_high = gather(pack[:, half_in:wide], [near] + dp_bits + [core], True, None, seq_high)
    out_block = {"mine": pack[:, wide:], "have": list(seq_high)}

    def out_start(block, step):
        block, send = together(block, out_block["mine"])
        out_block["mine"], out_block["got"] = send, swap(send, step)
        return block

    def out_take(block, step):
        block, got = together(block, out_block["got"])
        out_block["mine"] = joined(out_block["mine"], got, step, out_block["have"], True)
        out_block["have"].append(step)
        return block

    features = patch_features.reshape(rows * patch_dev, vit)
    ones = jnp.zeros((rows * patch_dev, 128), BF16).at[:, 0].set(1)
    features_more = jnp.concatenate([features, ones], axis=1)
    patch_rows = dot_nt(features_more[:, :half_in], in_low) + dot_nt(
        features_more[:, half_in:], in_high
    )
    units_eye = jnp.eye(8, 128, dtype=BF16)
    small = dot_nt(units_eye, in_high[:, wide - half_in - 128 :])
    gain_one, gain_two = small[1], small[2]
    table = small[3].reshape(dev_count, cols)[:, :bias_count].reshape(BUCKETS, HEADS)
    my_table = lax.dynamic_slice_in_dim(table, head, 1, 1).reshape(1, BUCKETS)
    resid = jnp.concatenate(
        [patch_rows.reshape(rows, patch_dev, d_model), text_embeds.astype(F32)], axis=1
    ).reshape(mine, d_model)
    normed_one = rms_norm(resid, gain_one).astype(BF16)
    half = d_model // 2
    order_low = seq_high + [near]
    order_high = [near] + seq_high
    normed_one, *late["pieces"] = together(normed_one, *late["pieces"])

    def while_start(block):
        block, late["up_got"] = together(block, late["up_got"])
        for step in dp_bits[:-1]:
            block = out_take(out_start(block, step), step)
        return out_start(block, dp_bits[-1])

    def while_second(block):
        return out_start(out_take(block, dp_bits[-1]), near)

    def while_last(block):
        return out_start(out_take(block, near), core)

    own_low = gather(
        normed_one[:, :half],
        order_low,
        False,
        {0: while_start, 1: while_second, len(order_low) - 1: while_last},
    )
    gate_up = jnp.concatenate([gate_up, late["gate_up"]], axis=0)
    for step in dp_bits[:-1]:
        gate_up = jnp.concatenate([gate_up, swap(gate_up, step)], axis=0)
    gate_up_got = swap(gate_up, dp_bits[-1])
    team_up = jnp.concatenate([late["up"], late["up_got"]], axis=0)
    team_up = jnp.concatenate([team_up, swap(team_up, core)], axis=0)
    own_high = gather(normed_one[:, half:], order_high, False)
    other_low, other_high = swap(own_low, core), swap(own_high, core)

    def my_rows(array):
        if twins == 1:
            return array
        view = array.reshape(chips, rows, tok, array.shape[1])
        view = lax.dynamic_slice_in_dim(view, twin * row_count, row_count, 1)
        return view.reshape(chips * row_count * tok, array.shape[1])

    pieces = jnp.stack(late["pieces"]).reshape(per_head, 3, cols, d_model)
    ordered = [
        lax.dynamic_index_in_dim(pieces, (place_in_head - i) % per_head, 0, keepdims=False)
        for i in range(per_head)
    ]
    w_head = jnp.stack(ordered, axis=1).reshape(3 * HEAD_DIM, d_model)
    normed_pairs = [
        (my_rows(own_low), my_rows(own_high)),
        (my_rows(other_low), my_rows(other_high)),
    ]
    qkv = [
        (dot_nt(low, w_head[:, :half]) + dot_nt(high, w_head[:, half:]))
        .astype(BF16)
        .reshape(chips, row_count, tok, 3 * HEAD_DIM)
        for low, high in normed_pairs
    ]
    *qkv, down = together(*qkv, down_in)
    full_down, down_got = far_gather(down.reshape(d_model, units).T)
    lengths = lax.dynamic_slice_in_dim(text_lengths, twin * row_count, row_count, 0)
    me = seq_index.reshape(1).astype(jnp.int32)
    dims = (row_count, images, patch_dev, text_dev, slots)
    bias = call(
        bias_kernel, jax.ShapeDtypeStruct((SEG_Q, SEG_K), F32), [SMEM], (), 1 << 24, 1 << 20, 8
    )(my_table)
    text_rows = seq_count * TEXT_PITCH
    patches = seq_count * patch_dev
    packed_shape = jax.ShapeDtypeStruct((seq_count, tok, row_count * HEAD_DIM), BF16)
    mixed = call(
        lambda *refs: forward_kernel(dims, *refs),
        packed_shape,
        [SMEM, SMEM, VMEM, VMEM, VMEM],
        (
            pltpu.VMEM((row_count, patches, 3 * HEAD_DIM), BF16),
            pltpu.VMEM((row_count, text_rows, 3 * HEAD_DIM), BF16),
            pltpu.VMEM((row_count, patches, HEAD_DIM), BF16),
            pltpu.VMEM((row_count, text_rows, HEAD_DIM), F32),
        ),
        1 << 24,
        1 << 20,
        20,
    )(me, lengths, bias, *qkv)
    mixed, gate_up_got, down_got = together(mixed, gate_up_got, down_got)
    full_gate, full_up = [
        jnp.concatenate([array[:, part] for array in (gate_up, gate_up_got)], axis=0)
        for part in (slice(0, d_model), slice(d_model, 2 * d_model))
    ]
    mixed_got = lax.all_to_all(mixed, SEQ, 0, 0, tiled=True)
    mixed_got = out_take(mixed_got, core)
    full_out = out_block["mine"]
    full_down = jnp.concatenate([full_down, down_got], axis=0)
    for step in dp_bits[:-1]:
        full_down = jnp.concatenate([full_down, swap(full_down, step)], axis=0)
    full_down = jnp.concatenate([full_down, swap(full_down, dp_bits[-1])], axis=0)
    attn_out, resid_one, normed_two = call(
        lambda *refs: mix_kernel(chips, twins, *refs),
        (
            jax.ShapeDtypeStruct((mine, d_model), BF16),
            jax.ShapeDtypeStruct((mine, d_model), F32),
            jax.ShapeDtypeStruct((mine, d_model), BF16),
        ),
        [VMEM, VMEM, VMEM, VMEM],
        (),
        1 << 24,
        1 << 20,
        12,
    )(mixed_got, full_out, resid, gain_two[None])
    team_normed = normed_two
    for step in team:
        got = swap(team_normed, step)
        if step == near:
            team_normed, full_gate, full_up, full_down = together(
                team_normed, full_gate, full_up, full_down
            )
        team_normed = jnp.concatenate([team_normed, got], axis=0)
    gate_pre = dot_nt(team_normed, full_gate)
    up_pre = dot_nt(team_normed, full_up)
    hidden, gated_back = jax.vjp(gated_unit, gate_pre, up_pre)
    hidden = hidden.astype(BF16)

    state = {}
    grad_down = dot_tn(hidden, team_up).astype(BF16)

    def down_start(step):
        count = grad_down_of["sum"].shape[0] // 2
        grad_down_of["keep"] = grad_down_of["sum"][:count]
        grad_down_of["got"] = swap(grad_down_of["sum"][count:].astype(BF16), step)

    def down_take(keep):
        keep, got = together(keep, grad_down_of["got"])
        grad_down_of["sum"] = grad_down_of["keep"].astype(F32) + got.astype(F32)
        return keep

    grad_down_of = {"sum": grad_down}
    down_start(dp_bits[-1])
    d_gate, d_up = gated_back(dot_nt(team_up, full_down))
    d_gate, d_up = d_gate.astype(BF16), d_up.astype(BF16)
    d_normed_two = dot_nn(d_gate, full_gate) + dot_nn(d_up, full_up)

    def ff_take(keep):
        keep, got = together(keep, state["ff_got"])
        state["ff"] = state["ff_keep"].astype(F32) + got.astype(F32)
        return keep

    def ff_start(keep, step):
        count = state["ff"].shape[0] // 2
        state["ff_keep"] = state["ff"][:count]
        keep, send = together(keep, state["ff"][count:].astype(BF16))
        state["ff_got"] = swap(send, step)
        return keep

    def while_team(keep):
        keep, *grads = together(keep, d_gate, d_up)
        state["ff"] = jnp.concatenate(
            [dot_tn(grad, team_normed).astype(BF16) for grad in grads], axis=1
        )
        return ff_start(keep, dp_bits[-1])

    def team_sum(part, step, hook=None):
        keep, send = halves(part, step, [step], False)
        got = swap(send.astype(BF16), step)
        return (hook(keep) if hook else keep) + got.astype(F32)

    d_normed_two = team_sum(d_normed_two, team[2])
    d_normed_two = team_sum(d_normed_two, team[1], while_team)
    d_normed_two = team_sum(d_normed_two, team[0])
    _, norm_back_two = jax.vjp(rms_norm, resid_one, gain_two)
    d_resid_one, grad_gain_two = norm_back_two(d_normed_two)
    d_resid_one = d_resid_one + upstream.astype(F32)
    d_mix = d_resid_one.astype(BF16)
    d_attn = dot_nn(d_mix, full_out).astype(BF16)
    d_attn = d_attn.reshape(twins, row_count, tok, HEADS, HEAD_DIM)
    d_attn = jnp.transpose(d_attn, (3, 0, 2, 1, 4)).reshape(2, chips, tok, row_count * HEAD_DIM)
    d_attn = d_attn.swapaxes(0, 1).reshape(packed_shape.shape)
    d_attn_got = lax.all_to_all(d_attn, SEQ, 0, 0, tiled=True)

    out_grad = {"sum": dot_tn(d_mix, attn_out).astype(BF16), "left": list(every)}

    def out_grad_start(keep, step):
        out_grad["keep"], send = halves(out_grad["sum"], step, out_grad["left"], True)
        keep, send = together(keep, send.astype(BF16))
        out_grad["got"] = swap(send, step)
        return keep

    def out_grad_take(keep, step):
        keep, got = together(keep, out_grad["got"])
        out_grad["sum"] = out_grad["keep"].astype(F32) + got.astype(F32)
        out_grad["left"].remove(step)
        return keep

    d_mix = down_take(d_mix)
    for step in dp_bits[-2::-1] + ff_far[:0:-1]:
        down_start(step)
        d_mix = down_take(d_mix)
    down_start(ff_far[0])
    out_part = team_sum(dot_nn(hidden, full_down), core)
    out_keep, send = halves(out_part, team[1], [team[1]], False)
    d_attn_got, send = together(out_grad_start(d_attn_got, core), send.astype(BF16))
    out_got = swap(send, team[1])
    half_shape = jax.ShapeDtypeStruct(qkv[0].shape, BF16)
    d_own, d_other, d_bias = call(
        lambda *refs: backward_kernel(dims, *refs),
        (half_shape, half_shape, jax.ShapeDtypeStruct((SEG_Q, SEG_K), F32)),
        [SMEM, SMEM, VMEM, VMEM, VMEM, VMEM],
        (
            pltpu.VMEM((row_count, patches, 3 * HEAD_DIM), BF16),
            pltpu.VMEM((row_count, text_rows, 3 * HEAD_DIM), BF16),
            pltpu.VMEM((row_count, patches, HEAD_DIM), BF16),
            pltpu.VMEM((row_count, text_rows, HEAD_DIM), BF16),
            pltpu.VMEM((row_count, patches, 3 * HEAD_DIM), BF16),
            pltpu.VMEM((row_count, text_rows, 3 * HEAD_DIM), F32),
        ),
        1 << 24,
        1 << 20,
        28,
    )(me, lengths, bias, *qkv, d_attn_got)
    d_other, out_got = together(down_take(d_other), out_got)
    out_part = out_keep + out_got.astype(F32)
    down_back = grad_down_of["sum"].T.reshape(dev_count, cols, units)
    state["down_back"] = lax.all_to_all(down_back, BOTH, 0, 0, tiled=True)
    d_qkv = [array.reshape(chips * row_count * tok, 3 * HEAD_DIM) for array in (d_own, d_other)]

    def all_rows(array):
        if twins == 1:
            return array
        view = array.reshape(chips, row_count, tok, array.shape[1])
        zero = jnp.zeros((chips, rows, tok, array.shape[1]), array.dtype)
        view = lax.dynamic_update_slice_in_dim(zero, view, twin * row_count, 1)
        return view.reshape(chips * mine, array.shape[1])

    chip_bits = seq_high + [near]
    weights = (w_head[:, :half], w_head[:, half:])
    sends = together(*[all_rows(dot_nn(d_qkv[1], part).astype(BF16)) for part in weights], d_own)
    others = [swap(send, core) for send in sends[:2]]
    d_qkv[0] = sends[2].reshape(d_qkv[0].shape)
    owns = [
        all_rows(dot_nn(d_qkv[0], part)) + other.astype(F32) for part, other in zip(weights, others)
    ]
    def while_first(keep):
        keep = ff_take(keep)
        for step in dp_bits[-2::-1]:
            keep = ff_take(ff_start(keep, step))
        for step in ff_far[:0:-1]:
            keep = ff_take(ff_start(keep, step))
        keep = out_grad_take(keep, dp_bits[-1])
        for step in dp_bits[-2::-1]:
            keep = out_grad_take(out_grad_start(keep, step), step)
        return out_grad_start(keep, near)

    def while_middle(keep):
        keep = out_grad_start(out_grad_take(keep, core), dp_bits[-1])
        keep, grads_own, grads_other = together(keep, *d_qkv)
        d_head = jnp.concatenate(
            [
                dot_tn(grads_own, normed_pairs[0][which])
                + dot_tn(grads_other, normed_pairs[1][which])
                for which in range(2)
            ],
            axis=1,
        )
        d_head = d_head.reshape(3, per_head, cols, d_model).astype(BF16)
        sends = [
            lax.dynamic_index_in_dim(
                d_head, (place_in_head - turn) % per_head, 1, keepdims=False
            ).reshape(3 * cols, d_model)
            for turn in range(per_head)
        ]
        keep, *sends = together(keep, *sends)
        state["three"] = [
            lax.ppermute(send, BOTH, rounds(turn, True)) for turn, send in enumerate(sends)
        ]
        return keep

    def while_late(keep):
        keep, *state["three"] = together(keep, *state["three"])
        return keep

    low_sums, high_sums = scatter_add_pair(
        *owns,
        order_low[::-1],
        order_high[::-1],
        chip_bits,
        False,
        {0: while_middle, 1: while_first, len(order_low) - 1: while_late},
    )
    d_normed_one = jnp.concatenate([low_sums, high_sums], axis=1)
    d_table = call(
        bucket_kernel, jax.ShapeDtypeStruct((BUCKETS, 128), F32), [VMEM], (), 1 << 20, 1 << 20, 8
    )(d_bias)[:, 0]
    _, norm_back_one = jax.vjp(rms_norm, resid, gain_one)
    d_resid, grad_gain_one = norm_back_one(d_normed_one)
    d_resid = (d_resid + d_resid_one).reshape(rows, tok, d_model)
    text_grad = d_resid[:, patch_dev:]
    d_patch_rows = d_resid[:, :patch_dev].reshape(rows * patch_dev, d_model)
    d_low = d_patch_rows.astype(BF16)
    pos_grads = d_table[:, None] * (jnp.arange(HEADS)[None, :] == head).astype(F32)
    pos_grads = jnp.pad(
        pos_grads.reshape(dev_count, bias_count), ((0, 0), (0, cols - bias_count))
    ).reshape(1, d_model)
    small_grads = jnp.concatenate(
        [
            jnp.sum(d_patch_rows, axis=0)[None],
            grad_gain_one[None],
            grad_gain_two[None],
            pos_grads,
            jnp.zeros((12, d_model), F32),
        ],
        axis=0,
    ).astype(BF16)
    left = jnp.concatenate([d_low, small_grads], axis=0)
    right = jnp.concatenate(
        [
            jnp.pad(features, ((0, 0), (0, 128))),
            jnp.pad(jnp.eye(16, 128, dtype=BF16), ((0, 0), (vit, 0))),
        ],
        axis=0,
    )

    def while_core_again(keep):
        keep = ff_start(keep, ff_far[0])
        keep, part = together(keep, out_part)
        state["out_keep"], send = halves(part, team[0], [team[0]], False)
        state["out_got"] = swap(send.astype(BF16), team[0])
        keep, state["d_low"] = together(keep, d_low)
        return keep

    def while_half_again(keep):
        keep, state["out_got"] = together(ff_take(out_grad_take(keep, near)), state["out_got"])
        return keep

    def while_end(keep):
        keep, state["down_back"] = together(keep, state["down_back"])
        return keep

    in_low_sums, in_high_sums = scatter_add_pair(
        dot_tn(left, right[:, :half_in]).astype(BF16),
        dot_tn(left, right[:, half_in:]).astype(BF16),
        [core, near] + dp_bits[::-1],
        [core] + dp_bits[::-1] + [near],
        every,
        True,
        {0: while_core_again, 2: while_half_again},
    )
    in_grads = scatter_add(
        jnp.concatenate([in_low_sums, in_high_sums, out_grad["sum"]], axis=1),
        seq_high[::-1],
        seq_high,
        True,
        {0: while_end},
    )
    small_out, grad_w_out = in_grads[:, vit:wide], in_grads[:, wide:]
    d_low = state["d_low"]
    feature_grad = jnp.concatenate(
        [dot_nn(d_low, in_low), dot_nn(d_low, in_high[:, : vit - half_in])], axis=1
    ).reshape(rows, patch_dev, vit)
    result = resid_one + state["out_keep"] + state["out_got"].astype(F32)
    result = result.astype(BF16).reshape(rows, tok, d_model)
    grad_gate, grad_up = state["ff"][:, :d_model], state["ff"][:, d_model:]
    grad_down = jnp.transpose(state["down_back"], (0, 2, 1)).reshape(dev_count * units, cols)
    grad_down = grad_down.astype(F32)
    d_three = sum(got.astype(F32) for got in state["three"]).reshape(3, cols, d_model)
    return (
        result[:, :patch_dev],
        result[:, patch_dev:],
        feature_grad,
        text_grad,
        in_grads[:, :vit].T,
        small_out[:, 0],
        small_out[:, 1],
        d_three[0].T,
        d_three[1].T,
        d_three[2].T,
        grad_w_out.T,
        small_out[:, 2],
        grad_gate.T,
        grad_up.T,
        grad_down,
        small_out[:bias_count, 3],
    )


def solution(mesh):
    token = P("dp", SEQ, None)
    matrix = P(None, BOTH)
    vector = P(BOTH)
    return jax.shard_map(
        local,
        mesh=mesh,
        in_specs=(
            token, token, P("dp", None), matrix, vector, vector, matrix, matrix, matrix, matrix,
            vector, matrix, matrix, matrix, vector, token, token,
        ),
        out_specs=(
            token, token, token, token, matrix, vector, vector, matrix, matrix, matrix, matrix,
            vector, matrix, matrix, matrix, vector,
        ),
        check_vma=False,
    )
```

```python
import jax
import jax.numpy as jnp
from jax import lax
from jax.experimental import pallas as pl
from jax.experimental.pallas import tpu as pltpu
from jax.sharding import PartitionSpec as P

HEADS = 16
HEAD_DIM = 64
BUCKETS = 32
PATCHES_IMG = 256
TEXT_MOST = 192

EPSILON = 1e-06
MASKED = -1e30
STARTS = (0, 1, 2, 3, 4, 5, 6, 7, 8, 12, 16, 23, 32, 46, 64, 91)
BF16 = jnp.bfloat16
F32 = jnp.float32
INTERPRET = False

SEG_Q = PATCHES_IMG + TEXT_MOST
SEG_K = 2 * PATCHES_IMG
TEXT_K = SEG_K - PATCHES_IMG
TEXT_PITCH = 32


def dot_nt(left, right):
    return lax.dot_general(left, right, (((1,), (1,)), ((), ())), preferred_element_type=F32)


def dot_nn(left, right):
    return lax.dot_general(left, right, (((1,), (0,)), ((), ())), preferred_element_type=F32)


def dot_tn(left, right):
    return lax.dot_general(left, right, (((0,), (0,)), ((), ())), preferred_element_type=F32)


def rms_norm(values, gain):
    return values * lax.rsqrt(jnp.mean(values * values, axis=-1, keepdims=True) + EPSILON) * gain


def gelu_tanh(values):
    return (
        0.5
        * values
        * (1.0 + jnp.tanh(0.7978845608 * (values + 0.044715 * values * values * values)))
    )


def gated_unit(gate_pre, up_pre):
    return gelu_tanh(gate_pre) * up_pre


SEQ = "seq"
BOTH = ("dp", "seq")


def swap(array, step):
    axis, bit = step
    count = lax.axis_size(axis)
    return lax.ppermute(array, axis, [(i, i ^ (1 << bit)) for i in range(count)])


def my_bit(step):
    return (lax.axis_index(step[0]) >> step[1]) & 1


def rank(step):
    return (1000 if step[0] == "dp" else 0) + step[1]


def after(value, signal):
    return value + (signal[(0,) * signal.ndim] * 0).astype(value.dtype)


def together(*arrays):
    return lax.optimization_barrier(arrays)


def joined(mine, other, step, have, absolute):
    at = sum(1 for done in have if rank(done) > rank(step))
    if absolute:
        bit = my_bit(step) == 1
        mine, other = jnp.where(bit, other, mine), jnp.where(bit, mine, other)
    shape = (2**at, 1, mine.shape[0] >> at, mine.shape[1])
    return jnp.concatenate([mine.reshape(shape), other.reshape(shape)], axis=1).reshape(
        -1, mine.shape[1]
    )


def halves(grads, step, every, absolute):
    at = sum(1 for other in every if rank(other) > rank(step))
    rows, width = grads.shape[0] // 2, grads.shape[1]
    view = grads.reshape(2**at, 2, rows >> at, width)
    if absolute:
        bit = my_bit(step)
        keep = lax.dynamic_slice_in_dim(view, bit, 1, 1)
        send = lax.dynamic_slice_in_dim(view, 1 - bit, 1, 1)
    else:
        keep, send = view[:, 0], view[:, 1]
    return keep.reshape(rows, width), send.reshape(rows, width)


def gather(block, order, absolute, hooks=None, have=()):
    for number, step in enumerate(order):
        other = swap(block, step)
        if hooks and number in hooks:
            block = hooks[number](block)
        block = joined(block, other, step, list(have) + order[:number], absolute)
    return block


def scatter_add(grads, order, every, absolute, hooks=None):
    for number, step in enumerate(order):
        left = [other for other in every if other not in order[:number]]
        keep, send = halves(grads, step, left, absolute)
        other = swap(send.astype(BF16), step)
        if hooks and number in hooks:
            keep = hooks[number](keep)
        grads = keep.astype(F32) + other.astype(F32)
    return grads


def scatter_add_pair(low, high, order_low, order_high, every, absolute, hooks):
    for number, (step_low, step_high) in enumerate(zip(order_low, order_high)):
        left_low = [other for other in every if other not in order_low[:number]]
        left_high = [other for other in every if other not in order_high[:number]]
        keep_low, send_low = halves(low, step_low, left_low, absolute)
        keep_high, send_high = halves(high, step_high, left_high, absolute)
        send_low, send_high = together(send_low.astype(BF16), send_high.astype(BF16))
        got_low, got_high = swap(send_low, step_low), swap(send_high, step_high)
        if number in hooks:
            keep_low = hooks[number](keep_low)
        low = keep_low.astype(F32) + got_low.astype(F32)
        high = keep_high.astype(F32) + got_high.astype(F32)
    return low, high


def bias_kernel(table_ref, out_ref):
    delta = lax.broadcasted_iota(jnp.int32, out_ref.shape, 0) - lax.broadcasted_iota(
        jnp.int32, out_ref.shape, 1
    )
    value = jnp.full(out_ref.shape, table_ref[0, BUCKETS - 1], F32)
    for which in range(14, 0, -1):
        value = jnp.where(delta > -STARTS[which + 1], table_ref[0, 16 + which], value)
    for which in range(16):
        value = jnp.where(delta >= STARTS[which], table_ref[0, which], value)
    out_ref[...] = value


def bucket_kernel(d_ref, out_ref):
    shape = d_ref.shape
    delta = lax.broadcasted_iota(jnp.int32, shape, 0) - lax.broadcasted_iota(jnp.int32, shape, 1)
    values = d_ref[...]
    rows = []
    for which in range(BUCKETS):
        low = STARTS[which % 16]
        high = STARTS[which % 16 + 1] if which % 16 < 15 else 1 << 20
        if which < 16:
            inside = (delta >= low) & (delta < high)
        else:
            inside = (delta <= -max(low, 1)) & (delta > -high)
        rows.append(jnp.sum(jnp.where(inside, values, 0.0), axis=0, keepdims=True))
    sums = jnp.sum(jnp.concatenate(rows, axis=0), axis=1, keepdims=True)
    out_ref[...] = jnp.broadcast_to(sums, out_ref.shape)


def unpack(seq_count, where, row, pat_ref, txt_ref, patch_dev, text_dev, lanes):
    tail = TEXT_PITCH - text_dev
    for place in range(seq_count):
        block = where(place)
        patches = block[0:patch_dev, lanes]
        text = block[patch_dev : patch_dev + text_dev, lanes]
        pat_ref[row, place * patch_dev : (place + 1) * patch_dev, :] = patches
        txt_ref[row, place * TEXT_PITCH : place * TEXT_PITCH + text_dev, :] = text
        if tail:
            txt_ref[row, place * TEXT_PITCH + text_dev : (place + 1) * TEXT_PITCH, :] = jnp.zeros(
                (tail, text.shape[1]), text.dtype
            )


def picker(count, text_rows, text_dev, slot_count, first, length):
    column = lax.broadcasted_iota(jnp.int32, (1, text_rows), 1)
    inner = column & (TEXT_PITCH - 1)
    slot = (column // TEXT_PITCH) * text_dev + inner
    fill = jnp.where(slot >= slot_count // 2, slot - slot_count // 2, slot + slot_count // 2)
    fill = jnp.where(inner < text_dev, fill, -1)
    line = lax.broadcasted_iota(jnp.int32, (count, 1), 0)
    wanted = jnp.where(line < length, first + line, -2)
    return (fill == wanted).astype(F32).astype(BF16)


def masked_keys(keys, length):
    column = lax.broadcasted_iota(jnp.int32, (1, keys), 1)
    return jnp.where(column < length, 0.0, MASKED)


def softmax(scores):
    top = jnp.max(scores, axis=-1, keepdims=True)
    expd = jnp.exp(scores - top)
    return expd * (1.0 / jnp.sum(expd, axis=-1, keepdims=True))


def segment_start(len_ref, row, which):
    return lax.fori_loop(0, which, lambda at, total: total + len_ref[row, at], jnp.int32(0))


class Halves:
    def __init__(self, me, own_ref, other_ref, row):
        self.me, self.own, self.other, self.row = me, own_ref, other_ref, row

    def at(self, place):
        apart = place ^ self.me
        return apart & 1, apart >> 1

    def __call__(self, place):
        odd, index = self.at(place)
        return jnp.where(odd == 1, self.other[index, self.row], self.own[index, self.row])


def forward_kernel(dims, me_ref, len_ref, bias_ref, own_ref, other_ref, o_ref, pat, txt, opat, otxt):
    rows, images, patch_dev, text_dev, slots = dims
    seq_count = 2 * own_ref.shape[0]
    text_rows = seq_count * TEXT_PITCH
    for row in range(rows):
        unpack(
            seq_count, Halves(me_ref[0], own_ref, other_ref, row),
            row, pat, txt, patch_dev, text_dev, slice(None),
        )
    otxt[...] = jnp.zeros_like(otxt)

    def attend(compact, queries, keys, length):
        q = compact[:queries, :HEAD_DIM]
        k = compact[:keys, HEAD_DIM : 2 * HEAD_DIM]
        v = compact[:keys, 2 * HEAD_DIM :]
        scores = dot_nt(q, k) + bias_ref[:queries, :keys] + masked_keys(keys, length)
        probs = softmax(scores).astype(BF16)
        return dot_nn(probs, v).astype(BF16)

    def one_segment(step, carry):
        row, image = step // images, step % images
        length = len_ref[row, image]
        first = segment_start(len_ref, row, image)
        pick = picker(TEXT_K, text_rows, text_dev, slots, first, length)
        text = dot_nn(pick, txt[row]).astype(BF16)
        at = pl.multiple_of(image * PATCHES_IMG, PATCHES_IMG)
        compact = jnp.concatenate([pat[row, pl.ds(at, PATCHES_IMG), :], text], axis=0)
        out = attend(compact, SEG_Q, SEG_K, PATCHES_IMG + length)
        opat[row, pl.ds(at, PATCHES_IMG), :] = out[:PATCHES_IMG]
        otxt[row] = otxt[row] + dot_tn(pick[:TEXT_MOST], out[PATCHES_IMG:])
        return carry

    lax.fori_loop(0, rows * images, one_segment, 0)
    pad_q = slots // 4
    pad_k = -(-pad_q // 128) * 128
    for row in range(rows):
        first = segment_start(len_ref, row, images)
        pick = picker(pad_k, text_rows, text_dev, slots, first, pad_q)
        compact = dot_nn(pick, txt[row]).astype(BF16)
        out = attend(compact, pad_q, pad_k, pad_q)
        otxt[row] = otxt[row] + dot_tn(pick[:pad_q], out)
    for place in range(seq_count):
        o_ref[place, 0:patch_dev, :] = jnp.concatenate(
            [opat[row, place * patch_dev : (place + 1) * patch_dev, :] for row in range(rows)],
            axis=1,
        )
        low = place * TEXT_PITCH
        o_ref[place, patch_dev : patch_dev + text_dev, :] = jnp.concatenate(
            [otxt[row, low : low + text_dev, :].astype(BF16) for row in range(rows)], axis=1
        )


def backward_kernel(
    dims, me_ref, len_ref, bias_ref, own_ref, other_ref, do_ref, down_ref, dother_ref, dbias_ref,
    pat, txt, dpat, dtxt, gpat, gtxt,
):
    rows, images, patch_dev, text_dev, slots = dims
    seq_count = 2 * own_ref.shape[0]
    text_rows = seq_count * TEXT_PITCH
    for row in range(rows):
        unpack(
            seq_count, Halves(me_ref[0], own_ref, other_ref, row),
            row, pat, txt, patch_dev, text_dev, slice(None),
        )
        unpack(
            seq_count, lambda place: do_ref.at[place],
            row, dpat, dtxt, patch_dev, text_dev,
            slice(row * HEAD_DIM, (row + 1) * HEAD_DIM),
        )
    gtxt[...] = jnp.zeros_like(gtxt)
    dbias_ref[...] = jnp.zeros_like(dbias_ref)

    def attend_back(compact, d_out, queries, keys, length):
        q = compact[:queries, :HEAD_DIM]
        k = compact[:keys, HEAD_DIM : 2 * HEAD_DIM]
        v = compact[:keys, 2 * HEAD_DIM :]
        scores = dot_nt(q, k) + bias_ref[:queries, :keys] + masked_keys(keys, length)
        probs = softmax(scores)
        d_probs = dot_nt(d_out, v)
        centre = jnp.sum(d_probs * probs, axis=-1, keepdims=True)
        d_scores = probs * (d_probs - centre)
        d_low = d_scores.astype(BF16)
        d_q = dot_nn(d_low, k).astype(BF16)
        d_k = dot_tn(d_low, q).astype(BF16)
        d_v = dot_tn(probs.astype(BF16), d_out).astype(BF16)
        return d_scores, jnp.concatenate([d_q, d_k[:queries], d_v[:queries]], axis=1)

    def one_segment(step, carry):
        row, image = step // images, step % images
        length = len_ref[row, image]
        first = segment_start(len_ref, row, image)
        pick = picker(TEXT_K, text_rows, text_dev, slots, first, length)
        at = pl.multiple_of(image * PATCHES_IMG, PATCHES_IMG)
        text = dot_nn(pick, txt[row]).astype(BF16)
        compact = jnp.concatenate([pat[row, pl.ds(at, PATCHES_IMG), :], text], axis=0)
        text_do = dot_nn(pick[:TEXT_MOST], dtxt[row]).astype(BF16)
        d_out = jnp.concatenate([dpat[row, pl.ds(at, PATCHES_IMG), :], text_do], axis=0)
        d_scores, grads = attend_back(compact, d_out, SEG_Q, SEG_K, PATCHES_IMG + length)
        dbias_ref[...] = dbias_ref[...] + d_scores
        gpat[row, pl.ds(at, PATCHES_IMG), :] = grads[:PATCHES_IMG]
        gtxt[row] = gtxt[row] + dot_tn(pick[:TEXT_MOST], grads[PATCHES_IMG:])
        return carry

    lax.fori_loop(0, rows * images, one_segment, 0)
    pad_q = slots // 4
    pad_k = -(-pad_q // 128) * 128
    for row in range(rows):
        first = segment_start(len_ref, row, images)
        pick = picker(pad_k, text_rows, text_dev, slots, first, pad_q)
        compact = dot_nn(pick, txt[row]).astype(BF16)
        d_out = dot_nn(pick[:pad_q], dtxt[row]).astype(BF16)
        d_scores, grads = attend_back(compact, d_out, pad_q, pad_k, pad_q)
        dbias_ref[:pad_q, :pad_k] = dbias_ref[:pad_q, :pad_k] + d_scores
        gtxt[row] = gtxt[row] + dot_tn(pick[:pad_q], grads)
    for row in range(rows):
        for place in range(seq_count):
            odd, index = Halves(me_ref[0], own_ref, other_ref, row).at(place)
            low = place * TEXT_PITCH
            patches = gpat[row, place * patch_dev : (place + 1) * patch_dev, :]
            text = gtxt[row, low : low + text_dev, :].astype(BF16)

            def put(target):
                target[index, row, 0:patch_dev, :] = patches
                target[index, row, patch_dev : patch_dev + text_dev, :] = text

            pl.when(odd == 0)(lambda: put(down_ref))
            pl.when(odd == 1)(lambda: put(dother_ref))


def mix_kernel(chips, twins, got_ref, weight_ref, resid_ref, gain_ref, mixed_ref, sum_ref, norm_ref):
    tok, packed = got_ref.shape[1:]
    for twin in range(twins):
        for row in range(packed // HEAD_DIM):
            lanes = slice(row * HEAD_DIM, (row + 1) * HEAD_DIM)
            slots = [which * twins + twin for which in range(HEADS)]
            heads = [got_ref[2 * (slot % chips) + slot // chips, :, lanes] for slot in slots]
            low = (twin * (packed // HEAD_DIM) + row) * tok
            mixed_ref[low : low + tok, :] = jnp.concatenate(heads, axis=1)
    total = resid_ref[...] + dot_nt(mixed_ref[...], weight_ref[...])
    sum_ref[...] = total
    norm_ref[...] = rms_norm(total, gain_ref[...]).astype(BF16)


def project_kernel(low_ref, high_ref, weight_ref, out_ref):
    half = low_ref.shape[1]
    value = dot_nt(low_ref[...], weight_ref[:, :half]) + dot_nt(
        high_ref[...], weight_ref[:, half:]
    )
    out_ref[...] = value.reshape(out_ref.shape).astype(BF16)


def norm_back(values, gain, grad):
    scale = lax.rsqrt(jnp.mean(values * values, axis=-1, keepdims=True) + EPSILON)
    unit = values * scale
    scaled = grad * gain
    d_values = scale * (scaled - unit * jnp.mean(scaled * unit, axis=-1, keepdims=True))
    return d_values, jnp.sum(grad * unit, axis=0, keepdims=True)


def turn_kernel(
    chips, twins, keep_ref, got_ref, sum_ref, gain_ref, up_ref, weight_ref,
    packed_ref, d_sum_ref, low_ref, d_gain_ref, heads,
):
    grad = keep_ref[...] + got_ref[...].astype(F32)
    d_values, d_gain = norm_back(sum_ref[...], gain_ref[...], grad)
    total = d_values + up_ref[...].astype(F32)
    d_sum_ref[...] = total
    low_ref[...] = total.astype(BF16)
    d_gain_ref[...] = jnp.broadcast_to(d_gain, d_gain_ref.shape)
    heads[...] = dot_nn(low_ref[...], weight_ref[...]).astype(BF16)
    tok, packed = packed_ref.shape[1:]
    rows = packed // HEAD_DIM
    for twin in range(twins):
        for which in range(HEADS):
            slot = which * twins + twin
            parts = []
            for row in range(rows):
                low = (twin * rows + row) * tok
                parts.append(heads[low : low + tok, which * HEAD_DIM : (which + 1) * HEAD_DIM])
            packed_ref[2 * (slot % chips) + slot // chips] = jnp.concatenate(parts, axis=1)


SMEM = pl.BlockSpec(memory_space=pltpu.SMEM)
VMEM = pl.BlockSpec(memory_space=pltpu.VMEM)


def call(kernel, out_shape, in_specs, scratch=(), flops=0, bytes_accessed=0, vmem=16):
    single = not isinstance(out_shape, (tuple, list))
    return pl.pallas_call(
        kernel,
        out_shape=out_shape,
        in_specs=in_specs,
        out_specs=VMEM if single else [VMEM] * len(out_shape),
        scratch_shapes=list(scratch),
        cost_estimate=pl.CostEstimate(
            flops=flops, bytes_accessed=bytes_accessed, transcendentals=0
        ),
        compiler_params=pltpu.CompilerParams(vmem_limit_bytes=vmem << 20),
        interpret=INTERPRET,
    )


def local(
    patch_features, text_embeds, text_lengths, w_in, b_in, gain_attn, w_query, w_key, w_value,
    w_out, gain_ffn, w_gate, w_up, w_down, position_bias, d_patch, d_text,
):
    seq_count, dp_count = lax.axis_size(SEQ), lax.axis_size("dp")
    dev_count = seq_count * dp_count
    seq_index, dp_index = lax.axis_index(SEQ), lax.axis_index("dp")
    rows, patch_dev, vit = patch_features.shape
    text_dev = text_embeds.shape[1]
    tok = patch_dev + text_dev
    mine = rows * tok
    d_model = text_embeds.shape[2]
    cols = w_in.shape[1]
    images = text_lengths.shape[1]
    slots = text_dev * seq_count
    core, near = ("seq", 0), ("seq", 1)
    seq_high = [("seq", bit) for bit in range(seq_count.bit_length() - 2, 1, -1)]
    dp_bits = [("dp", bit) for bit in range(dp_count.bit_length() - 1)]
    every = dp_bits + seq_high + [near, core]

    bias_count = position_bias.shape[0]
    pack = jnp.concatenate(
        [
            w_in,
            b_in[None],
            gain_attn[None],
            gain_ffn[None],
            jnp.pad(position_bias, (0, cols - bias_count))[None],
            jnp.zeros((124, cols), BF16),
            w_out,
        ],
        axis=0,
    ).T
    wide = vit + 128
    half_in = wide // 256 * 128
    per_head = dev_count // HEADS
    twins = seq_count // HEADS
    chips = seq_count // 2
    head_slot = (seq_index % 2) * chips + seq_index // 2
    head = head_slot // twins
    twin = head_slot % twins
    place_in_head = dp_index * twins + twin
    row_count = rows // twins
    three = jnp.concatenate([w_query.T, w_key.T, w_value.T], axis=0)

    def to_rank(which_head, place):
        slot = which_head * twins + place % twins
        return (place // twins) * seq_count + 2 * (slot % chips) + slot // chips

    def rounds(turn, back):
        pairs = []
        for which_head in range(HEADS):
            for i in range(per_head):
                owner = which_head * per_head + i
                user = to_rank(which_head, (i + turn) % per_head)
                pairs.append((user, owner) if back else (owner, user))
        return pairs

    team = [("seq", 2), near, core]
    ff_far = [step for step in seq_high if step not in team]
    ff_order = ff_far + dp_bits
    units = w_gate.shape[1]
    down_out = jnp.transpose(w_down.reshape(dev_count, units, cols), (0, 2, 1))
    down_in = lax.all_to_all(down_out, BOTH, 0, 0, tiled=True)
    upstream = jnp.concatenate([d_patch, d_text], axis=1).reshape(mine, d_model)
    up_got = swap(upstream, team[0])
    late = {}

    def far_gather(block):
        for step in ff_far[:-1]:
            block = jnp.concatenate([block, swap(block, step)], axis=0)
        return block, swap(block, ff_far[-1])

    gate_up, gate_up_got = far_gather(jnp.concatenate([w_gate.T, w_up.T], axis=1))

    def while_near(block):
        block, late["gate_up"] = together(block, gate_up_got)
        return block

    def while_core(block):
        block, got = together(block, up_got)
        late["up"] = jnp.concatenate([upstream, got], axis=0)
        late["up_got"] = swap(late["up"], team[1])
        late["pieces"] = [lax.ppermute(three, BOTH, rounds(turn, False)) for turn in range(per_head)]
        return block

    pack = gather(pack, seq_high, True)
    in_low = gather(
        pack[:, :half_in],
        dp_bits + [near, core],
        True,
        {len(dp_bits): while_near, len(dp_bits) + 1: while_core},
        seq_high,
    )
    in_high = gather(pack[:, half_in:wide], [near] + dp_bits + [core], True, None, seq_high)
    out_block = {"mine": pack[:, wide:], "have": list(seq_high)}

    def out_start(block, step):
        block, send = together(block, out_block["mine"])
        out_block["mine"], out_block["got"] = send, swap(send, step)
        return block

    def out_take(block, step):
        block, got = together(block, out_block["got"])
        out_block["mine"] = joined(out_block["mine"], got, step, out_block["have"], True)
        out_block["have"].append(step)
        return block

    features = patch_features.reshape(rows * patch_dev, vit)
    ones = jnp.zeros((rows * patch_dev, 128), BF16).at[:, 0].set(1)
    features_more = jnp.concatenate([features, ones], axis=1)
    patch_rows = dot_nt(features_more[:, :half_in], in_low) + dot_nt(
        features_more[:, half_in:], in_high
    )
    units_eye = jnp.eye(8, 128, dtype=BF16)
    small = dot_nt(units_eye, in_high[:, wide - half_in - 128 :])
    gain_one, gain_two = small[1], small[2]
    table = small[3].reshape(dev_count, cols)[:, :bias_count].reshape(BUCKETS, HEADS)
    my_table = lax.dynamic_slice_in_dim(table, head, 1, 1).reshape(1, BUCKETS)
    resid = jnp.concatenate(
        [patch_rows.reshape(rows, patch_dev, d_model), text_embeds.astype(F32)], axis=1
    ).reshape(mine, d_model)
    normed_one = rms_norm(resid, gain_one).astype(BF16)
    half = d_model // 2
    order_low = seq_high + [near]
    order_high = [near] + seq_high
    normed_one, *late["pieces"] = together(normed_one, *late["pieces"])

    def while_start(block):
        block, late["up_got"] = together(block, late["up_got"])
        for step in dp_bits[:-1]:
            block = out_take(out_start(block, step), step)
        return out_start(block, dp_bits[-1])

    pieces = jnp.stack(late["pieces"]).reshape(per_head, 3, cols, d_model)
    ordered = [
        lax.dynamic_index_in_dim(pieces, (place_in_head - i) % per_head, 0, keepdims=False)
        for i in range(per_head)
    ]
    w_head = jnp.stack(ordered, axis=1).reshape(3 * HEAD_DIM, d_model)
    bias = call(
        bias_kernel, jax.ShapeDtypeStruct((SEG_Q, SEG_K), F32), [SMEM], (), 1 << 24, 1 << 20, 8
    )(my_table)
    def while_second(block):
        block, late["w_head"], late["bias"] = together(block, w_head, bias)
        return out_start(out_take(block, dp_bits[-1]), near)

    def while_last(block):
        return out_start(out_take(block, near), core)

    own_low = gather(
        normed_one[:, :half],
        order_low,
        False,
        {0: while_start, 1: while_second, len(order_low) - 1: while_last},
    )
    gate_up = jnp.concatenate([gate_up, late["gate_up"]], axis=0)
    for step in dp_bits[:-1]:
        gate_up = jnp.concatenate([gate_up, swap(gate_up, step)], axis=0)
    gate_up_got = swap(gate_up, dp_bits[-1])
    team_up = jnp.concatenate([late["up"], late["up_got"]], axis=0)
    team_up = jnp.concatenate([team_up, swap(team_up, core)], axis=0)
    w_head, bias = late["w_head"], late["bias"]
    own_high = gather(normed_one[:, half:], order_high, False)
    own_low, own_high, late["down"] = together(own_low, own_high, down_in)
    other_low, other_high = swap(own_low, core), swap(own_high, core)

    def my_rows(array):
        if twins == 1:
            return array
        view = array.reshape(chips, rows, tok, array.shape[1])
        view = lax.dynamic_slice_in_dim(view, twin * row_count, row_count, 1)
        return view.reshape(chips * row_count * tok, array.shape[1])

    normed_pairs = [
        (my_rows(own_low), my_rows(own_high)),
        (my_rows(other_low), my_rows(other_high)),
    ]
    qkv = [
        call(
            project_kernel,
            jax.ShapeDtypeStruct((chips, row_count, tok, 3 * HEAD_DIM), BF16),
            [VMEM] * 3,
            (),
            1 << 24,
            1 << 20,
            14,
        )(low, high, w_head)
        for low, high in normed_pairs
    ]
    down = late["down"]
    full_down, down_got = far_gather(down.reshape(d_model, units).T)
    lengths = lax.dynamic_slice_in_dim(text_lengths, twin * row_count, row_count, 0)
    me = seq_index.reshape(1).astype(jnp.int32)
    dims = (row_count, images, patch_dev, text_dev, slots)
    text_rows = seq_count * TEXT_PITCH
    patches = seq_count * patch_dev
    packed_shape = jax.ShapeDtypeStruct((seq_count, tok, row_count * HEAD_DIM), BF16)
    mixed = call(
        lambda *refs: forward_kernel(dims, *refs),
        packed_shape,
        [SMEM, SMEM, VMEM, VMEM, VMEM],
        (
            pltpu.VMEM((row_count, patches, 3 * HEAD_DIM), BF16),
            pltpu.VMEM((row_count, text_rows, 3 * HEAD_DIM), BF16),
            pltpu.VMEM((row_count, patches, HEAD_DIM), BF16),
            pltpu.VMEM((row_count, text_rows, HEAD_DIM), F32),
        ),
        1 << 24,
        1 << 20,
        20,
    )(me, lengths, bias, *qkv)
    mixed, gate_up_got, down_got = together(mixed, gate_up_got, down_got)
    full_gate, full_up = [
        jnp.concatenate([array[:, part] for array in (gate_up, gate_up_got)], axis=0)
        for part in (slice(0, d_model), slice(d_model, 2 * d_model))
    ]
    mixed_got = lax.all_to_all(mixed, SEQ, 0, 0, tiled=True)
    mixed_got = out_take(mixed_got, core)
    full_out = out_block["mine"]
    full_down = jnp.concatenate([full_down, down_got], axis=0)
    for step in dp_bits[:-1]:
        full_down = jnp.concatenate([full_down, swap(full_down, step)], axis=0)
    full_down = jnp.concatenate([full_down, swap(full_down, dp_bits[-1])], axis=0)
    attn_out, resid_one, normed_two = call(
        lambda *refs: mix_kernel(chips, twins, *refs),
        (
            jax.ShapeDtypeStruct((mine, d_model), BF16),
            jax.ShapeDtypeStruct((mine, d_model), F32),
            jax.ShapeDtypeStruct((mine, d_model), BF16),
        ),
        [VMEM, VMEM, VMEM, VMEM],
        (),
        1 << 24,
        1 << 20,
        12,
    )(mixed_got, full_out, resid, gain_two[None])
    team_normed = normed_two
    for step in team:
        got = swap(team_normed, step)
        if step == near:
            team_normed, full_gate, full_up, full_down = together(
                team_normed, full_gate, full_up, full_down
            )
        team_normed = jnp.concatenate([team_normed, got], axis=0)
    gate_pre = dot_nt(team_normed, full_gate)
    up_pre = dot_nt(team_normed, full_up)
    hidden, gated_back = jax.vjp(gated_unit, gate_pre, up_pre)
    hidden = hidden.astype(BF16)

    state = {}
    grad_down = dot_tn(hidden, team_up).astype(BF16)

    def down_start(step):
        count = grad_down_of["sum"].shape[0] // 2
        grad_down_of["keep"] = grad_down_of["sum"][:count]
        grad_down_of["got"] = swap(grad_down_of["sum"][count:].astype(BF16), step)

    def down_take(keep):
        keep, got = together(keep, grad_down_of["got"])
        grad_down_of["sum"] = grad_down_of["keep"].astype(F32) + got.astype(F32)
        return keep

    grad_down_of = {"sum": grad_down}
    down_start(dp_bits[-1])
    d_gate, d_up = gated_back(dot_nt(team_up, full_down))
    d_gate, d_up = d_gate.astype(BF16), d_up.astype(BF16)
    d_normed_two = dot_nn(d_gate, full_gate) + dot_nn(d_up, full_up)

    def ff_take(keep):
        keep, got = together(keep, state["ff_got"])
        state["ff"] = state["ff_keep"].astype(F32) + got.astype(F32)
        return keep

    def ff_start(keep, step):
        count = state["ff"].shape[0] // 2
        state["ff_keep"] = state["ff"][:count]
        keep, send = together(keep, state["ff"][count:].astype(BF16))
        state["ff_got"] = swap(send, step)
        return keep

    def while_team(keep):
        keep, *grads = together(keep, d_gate, d_up)
        state["ff"] = jnp.concatenate(
            [dot_tn(grad, team_normed).astype(BF16) for grad in grads], axis=1
        )
        return ff_start(keep, dp_bits[-1])

    def team_sum(part, step, hook=None):
        keep, send = halves(part, step, [step], False)
        got = swap(send.astype(BF16), step)
        return (hook(keep) if hook else keep) + got.astype(F32)

    d_normed_two = team_sum(d_normed_two, team[2])
    d_normed_two = team_sum(d_normed_two, team[1], while_team)
    turn_keep, send = halves(d_normed_two, team[0], [team[0]], False)
    turn_got = swap(send.astype(BF16), team[0])
    d_attn, d_resid_one, d_mix, grad_gain_two = call(
        lambda *refs: turn_kernel(chips, twins, *refs),
        (
            packed_shape,
            jax.ShapeDtypeStruct((mine, d_model), F32),
            jax.ShapeDtypeStruct((mine, d_model), BF16),
            jax.ShapeDtypeStruct((8, d_model), F32),
        ),
        [VMEM] * 6,
        (pltpu.VMEM((mine, d_model), BF16),),
        1 << 24,
        1 << 20,
        14,
    )(turn_keep, turn_got, resid_one, gain_two[None], upstream, full_out)
    grad_gain_two = grad_gain_two[0]
    d_attn_got = lax.all_to_all(d_attn, SEQ, 0, 0, tiled=True)

    out_grad = {"sum": dot_tn(d_mix, attn_out).astype(BF16), "left": list(every)}

    def out_grad_start(keep, step):
        out_grad["keep"], send = halves(out_grad["sum"], step, out_grad["left"], True)
        keep, send = together(keep, send.astype(BF16))
        out_grad["got"] = swap(send, step)
        return keep

    def out_grad_take(keep, step):
        keep, got = together(keep, out_grad["got"])
        out_grad["sum"] = out_grad["keep"].astype(F32) + got.astype(F32)
        out_grad["left"].remove(step)
        return keep

    d_mix = down_take(d_mix)
    for step in dp_bits[-2::-1] + ff_far[:0:-1]:
        down_start(step)
        d_mix = down_take(d_mix)
    down_start(ff_far[0])
    out_part = team_sum(dot_nn(hidden, full_down), core)
    out_keep, send = halves(out_part, team[1], [team[1]], False)
    d_attn_got, send = together(out_grad_start(d_attn_got, core), send.astype(BF16))
    out_got = swap(send, team[1])
    half_shape = jax.ShapeDtypeStruct(qkv[0].shape, BF16)
    d_own, d_other, d_bias = call(
        lambda *refs: backward_kernel(dims, *refs),
        (half_shape, half_shape, jax.ShapeDtypeStruct((SEG_Q, SEG_K), F32)),
        [SMEM, SMEM, VMEM, VMEM, VMEM, VMEM],
        (
            pltpu.VMEM((row_count, patches, 3 * HEAD_DIM), BF16),
            pltpu.VMEM((row_count, text_rows, 3 * HEAD_DIM), BF16),
            pltpu.VMEM((row_count, patches, HEAD_DIM), BF16),
            pltpu.VMEM((row_count, text_rows, HEAD_DIM), BF16),
            pltpu.VMEM((row_count, patches, 3 * HEAD_DIM), BF16),
            pltpu.VMEM((row_count, text_rows, 3 * HEAD_DIM), F32),
        ),
        1 << 24,
        1 << 20,
        28,
    )(me, lengths, bias, *qkv, d_attn_got)
    d_other, out_got = together(down_take(d_other), out_got)
    out_part = out_keep + out_got.astype(F32)
    down_back = grad_down_of["sum"].T.reshape(dev_count, cols, units)
    state["down_back"] = lax.all_to_all(down_back, BOTH, 0, 0, tiled=True)
    d_qkv = [array.reshape(chips * row_count * tok, 3 * HEAD_DIM) for array in (d_own, d_other)]

    def all_rows(array):
        if twins == 1:
            return array
        view = array.reshape(chips, row_count, tok, array.shape[1])
        zero = jnp.zeros((chips, rows, tok, array.shape[1]), array.dtype)
        view = lax.dynamic_update_slice_in_dim(zero, view, twin * row_count, 1)
        return view.reshape(chips * mine, array.shape[1])

    chip_bits = seq_high + [near]
    weights = (w_head[:, :half], w_head[:, half:])
    sends = together(*[all_rows(dot_nn(d_qkv[1], part).astype(BF16)) for part in weights], d_own)
    others = [swap(send, core) for send in sends[:2]]
    d_qkv[0] = sends[2].reshape(d_qkv[0].shape)
    owns = [
        all_rows(dot_nn(d_qkv[0], part)) + other.astype(F32) for part, other in zip(weights, others)
    ]
    def while_first(keep):
        keep = ff_take(keep)
        for step in dp_bits[-2::-1]:
            keep = ff_take(ff_start(keep, step))
        for step in ff_far[:0:-1]:
            keep = ff_take(ff_start(keep, step))
        keep = out_grad_take(keep, dp_bits[-1])
        for step in dp_bits[-2::-1]:
            keep = out_grad_take(out_grad_start(keep, step), step)
        return out_grad_start(keep, near)

    def while_middle(keep):
        keep = out_grad_start(out_grad_take(keep, core), dp_bits[-1])
        keep, grads_own, grads_other = together(keep, *d_qkv)
        d_head = jnp.concatenate(
            [
                dot_tn(grads_own, normed_pairs[0][which])
                + dot_tn(grads_other, normed_pairs[1][which])
                for which in range(2)
            ],
            axis=1,
        )
        d_head = d_head.reshape(3, per_head, cols, d_model).astype(BF16)
        sends = [
            lax.dynamic_index_in_dim(
                d_head, (place_in_head - turn) % per_head, 1, keepdims=False
            ).reshape(3 * cols, d_model)
            for turn in range(per_head)
        ]
        keep, *sends = together(keep, *sends)
        state["three"] = [
            lax.ppermute(send, BOTH, rounds(turn, True)) for turn, send in enumerate(sends)
        ]
        return keep

    def while_late(keep):
        keep, *state["three"] = together(keep, *state["three"])
        return keep

    low_sums, high_sums = scatter_add_pair(
        *owns,
        order_low[::-1],
        order_high[::-1],
        chip_bits,
        False,
        {0: while_middle, 1: while_first, len(order_low) - 1: while_late},
    )
    d_normed_one = jnp.concatenate([low_sums, high_sums], axis=1)
    d_table = call(
        bucket_kernel, jax.ShapeDtypeStruct((BUCKETS, 128), F32), [VMEM], (), 1 << 20, 1 << 20, 8
    )(d_bias)[:, 0]
    _, norm_back_one = jax.vjp(rms_norm, resid, gain_one)
    d_resid, grad_gain_one = norm_back_one(d_normed_one)
    d_resid = (d_resid + d_resid_one).reshape(rows, tok, d_model)
    text_grad = d_resid[:, patch_dev:]
    d_patch_rows = d_resid[:, :patch_dev].reshape(rows * patch_dev, d_model)
    d_low = d_patch_rows.astype(BF16)
    pos_grads = d_table[:, None] * (jnp.arange(HEADS)[None, :] == head).astype(F32)
    pos_grads = jnp.pad(
        pos_grads.reshape(dev_count, bias_count), ((0, 0), (0, cols - bias_count))
    ).reshape(1, d_model)
    small_grads = jnp.concatenate(
        [
            jnp.sum(d_patch_rows, axis=0)[None],
            grad_gain_one[None],
            grad_gain_two[None],
            pos_grads,
            jnp.zeros((12, d_model), F32),
        ],
        axis=0,
    ).astype(BF16)
    left = jnp.concatenate([d_low, small_grads], axis=0)
    right = jnp.concatenate(
        [
            jnp.pad(features, ((0, 0), (0, 128))),
            jnp.pad(jnp.eye(16, 128, dtype=BF16), ((0, 0), (vit, 0))),
        ],
        axis=0,
    )

    def while_core_again(keep):
        keep = ff_start(keep, ff_far[0])
        keep, part = together(keep, out_part)
        state["out_keep"], send = halves(part, team[0], [team[0]], False)
        state["out_got"] = swap(send.astype(BF16), team[0])
        keep, state["d_low"] = together(keep, d_low)
        return keep

    def while_half_again(keep):
        keep, state["out_got"] = together(ff_take(out_grad_take(keep, near)), state["out_got"])
        return keep

    def while_end(keep):
        keep, state["down_back"] = together(keep, state["down_back"])
        return keep

    in_low_sums, in_high_sums = scatter_add_pair(
        dot_tn(left, right[:, :half_in]).astype(BF16),
        dot_tn(left, right[:, half_in:]).astype(BF16),
        [core, near] + dp_bits[::-1],
        [core] + dp_bits[::-1] + [near],
        every,
        True,
        {0: while_core_again, 2: while_half_again},
    )
    in_grads = scatter_add(
        jnp.concatenate([in_low_sums, in_high_sums, out_grad["sum"]], axis=1),
        seq_high[::-1],
        seq_high,
        True,
        {0: while_end},
    )
    small_out, grad_w_out = in_grads[:, vit:wide], in_grads[:, wide:]
    d_low = state["d_low"]
    feature_grad = jnp.concatenate(
        [dot_nn(d_low, in_low), dot_nn(d_low, in_high[:, : vit - half_in])], axis=1
    ).reshape(rows, patch_dev, vit)
    result = resid_one + state["out_keep"] + state["out_got"].astype(F32)
    result = result.astype(BF16).reshape(rows, tok, d_model)
    grad_gate, grad_up = state["ff"][:, :d_model], state["ff"][:, d_model:]
    grad_down = jnp.transpose(state["down_back"], (0, 2, 1)).reshape(dev_count * units, cols)
    grad_down = grad_down.astype(F32)
    d_three = sum(got.astype(F32) for got in state["three"]).reshape(3, cols, d_model)
    return (
        result[:, :patch_dev],
        result[:, patch_dev:],
        feature_grad,
        text_grad,
        in_grads[:, :vit].T,
        small_out[:, 0],
        small_out[:, 1],
        d_three[0].T,
        d_three[1].T,
        d_three[2].T,
        grad_w_out.T,
        small_out[:, 2],
        grad_gate.T,
        grad_up.T,
        grad_down,
        small_out[:bias_count, 3],
    )


def solution(mesh):
    token = P("dp", SEQ, None)
    matrix = P(None, BOTH)
    vector = P(BOTH)
    return jax.shard_map(
        local,
        mesh=mesh,
        in_specs=(
            token, token, P("dp", None), matrix, vector, vector, matrix, matrix, matrix, matrix,
            vector, matrix, matrix, matrix, vector, token, token,
        ),
        out_specs=(
            token, token, token, token, matrix, vector, vector, matrix, matrix, matrix, matrix,
            vector, matrix, matrix, matrix, vector,
        ),
        check_vma=False,
    )
```

```python
import jax
import jax.numpy as jnp
from jax import lax
from jax.experimental import pallas as pl
from jax.experimental.pallas import tpu as pltpu
from jax.sharding import PartitionSpec as P

HEADS = 16
HEAD_DIM = 64
BUCKETS = 32
PATCHES_IMG = 256
TEXT_MOST = 192

EPSILON = 1e-06
MASKED = -1e30
STARTS = (0, 1, 2, 3, 4, 5, 6, 7, 8, 12, 16, 23, 32, 46, 64, 91)
BF16 = jnp.bfloat16
F32 = jnp.float32
INTERPRET = False

SEG_Q = PATCHES_IMG + TEXT_MOST
SEG_K = 2 * PATCHES_IMG
TEXT_K = SEG_K - PATCHES_IMG
TEXT_PITCH = 32


def dot_nt(left, right):
    return lax.dot_general(left, right, (((1,), (1,)), ((), ())), preferred_element_type=F32)


def dot_nn(left, right):
    return lax.dot_general(left, right, (((1,), (0,)), ((), ())), preferred_element_type=F32)


def dot_tn(left, right):
    return lax.dot_general(left, right, (((0,), (0,)), ((), ())), preferred_element_type=F32)


def rms_norm(values, gain):
    return values * lax.rsqrt(jnp.mean(values * values, axis=-1, keepdims=True) + EPSILON) * gain


def gelu_tanh(values):
    return (
        0.5
        * values
        * (1.0 + jnp.tanh(0.7978845608 * (values + 0.044715 * values * values * values)))
    )


def gated_unit(gate_pre, up_pre):
    return gelu_tanh(gate_pre) * up_pre


SEQ = "seq"
BOTH = ("dp", "seq")


def swap(array, step):
    axis, bit = step
    count = lax.axis_size(axis)
    return lax.ppermute(array, axis, [(i, i ^ (1 << bit)) for i in range(count)])


def my_bit(step):
    return (lax.axis_index(step[0]) >> step[1]) & 1


def rank(step):
    return (1000 if step[0] == "dp" else 0) + step[1]


def after(value, signal):
    return value + (signal[(0,) * signal.ndim] * 0).astype(value.dtype)


def together(*arrays):
    return lax.optimization_barrier(arrays)


def joined(mine, other, step, have, absolute):
    at = sum(1 for done in have if rank(done) > rank(step))
    if absolute:
        bit = my_bit(step) == 1
        mine, other = jnp.where(bit, other, mine), jnp.where(bit, mine, other)
    shape = (2**at, 1, mine.shape[0] >> at, mine.shape[1])
    return jnp.concatenate([mine.reshape(shape), other.reshape(shape)], axis=1).reshape(
        -1, mine.shape[1]
    )


def halves(grads, step, every, absolute):
    at = sum(1 for other in every if rank(other) > rank(step))
    rows, width = grads.shape[0] // 2, grads.shape[1]
    view = grads.reshape(2**at, 2, rows >> at, width)
    if absolute:
        bit = my_bit(step)
        keep = lax.dynamic_slice_in_dim(view, bit, 1, 1)
        send = lax.dynamic_slice_in_dim(view, 1 - bit, 1, 1)
    else:
        keep, send = view[:, 0], view[:, 1]
    return keep.reshape(rows, width), send.reshape(rows, width)


def gather(block, order, absolute, hooks=None, have=()):
    for number, step in enumerate(order):
        other = swap(block, step)
        if hooks and number in hooks:
            block = hooks[number](block)
        block = joined(block, other, step, list(have) + order[:number], absolute)
    return block


def scatter_add(grads, order, every, absolute, hooks=None):
    for number, step in enumerate(order):
        left = [other for other in every if other not in order[:number]]
        keep, send = halves(grads, step, left, absolute)
        other = swap(send.astype(BF16), step)
        if hooks and number in hooks:
            keep = hooks[number](keep)
        grads = keep.astype(F32) + other.astype(F32)
    return grads


def scatter_add_pair(low, high, order_low, order_high, every, absolute, hooks):
    for number, (step_low, step_high) in enumerate(zip(order_low, order_high)):
        left_low = [other for other in every if other not in order_low[:number]]
        left_high = [other for other in every if other not in order_high[:number]]
        keep_low, send_low = halves(low, step_low, left_low, absolute)
        keep_high, send_high = halves(high, step_high, left_high, absolute)
        send_low, send_high = together(send_low.astype(BF16), send_high.astype(BF16))
        got_low, got_high = swap(send_low, step_low), swap(send_high, step_high)
        if number in hooks:
            keep_low = hooks[number](keep_low)
        low = keep_low.astype(F32) + got_low.astype(F32)
        high = keep_high.astype(F32) + got_high.astype(F32)
    return low, high


def bias_kernel(table_ref, out_ref):
    delta = lax.broadcasted_iota(jnp.int32, out_ref.shape, 0) - lax.broadcasted_iota(
        jnp.int32, out_ref.shape, 1
    )
    value = jnp.full(out_ref.shape, table_ref[0, BUCKETS - 1], F32)
    for which in range(14, 0, -1):
        value = jnp.where(delta > -STARTS[which + 1], table_ref[0, 16 + which], value)
    for which in range(16):
        value = jnp.where(delta >= STARTS[which], table_ref[0, which], value)
    out_ref[...] = value


def bucket_kernel(d_ref, out_ref):
    shape = d_ref.shape
    delta = lax.broadcasted_iota(jnp.int32, shape, 0) - lax.broadcasted_iota(jnp.int32, shape, 1)
    values = d_ref[...]
    rows = []
    for which in range(BUCKETS):
        low = STARTS[which % 16]
        high = STARTS[which % 16 + 1] if which % 16 < 15 else 1 << 20
        if which < 16:
            inside = (delta >= low) & (delta < high)
        else:
            inside = (delta <= -max(low, 1)) & (delta > -high)
        rows.append(jnp.sum(jnp.where(inside, values, 0.0), axis=0, keepdims=True))
    sums = jnp.sum(jnp.concatenate(rows, axis=0), axis=1, keepdims=True)
    out_ref[...] = jnp.broadcast_to(sums, out_ref.shape)


def unpack(seq_count, where, row, pat_ref, txt_ref, patch_dev, text_dev, lanes):
    tail = TEXT_PITCH - text_dev
    for place in range(seq_count):
        block = where(place)
        patches = block[0:patch_dev, lanes]
        text = block[patch_dev : patch_dev + text_dev, lanes]
        pat_ref[row, place * patch_dev : (place + 1) * patch_dev, :] = patches
        txt_ref[row, place * TEXT_PITCH : place * TEXT_PITCH + text_dev, :] = text
        if tail:
            txt_ref[row, place * TEXT_PITCH + text_dev : (place + 1) * TEXT_PITCH, :] = jnp.zeros(
                (tail, text.shape[1]), text.dtype
            )


def picker(count, text_rows, text_dev, slot_count, first, length):
    column = lax.broadcasted_iota(jnp.int32, (1, text_rows), 1)
    inner = column & (TEXT_PITCH - 1)
    slot = (column // TEXT_PITCH) * text_dev + inner
    fill = jnp.where(slot >= slot_count // 2, slot - slot_count // 2, slot + slot_count // 2)
    fill = jnp.where(inner < text_dev, fill, -1)
    line = lax.broadcasted_iota(jnp.int32, (count, 1), 0)
    wanted = jnp.where(line < length, first + line, -2)
    return (fill == wanted).astype(F32).astype(BF16)


def masked_keys(keys, length):
    column = lax.broadcasted_iota(jnp.int32, (1, keys), 1)
    return jnp.where(column < length, 0.0, MASKED)


def softmax(scores):
    top = jnp.max(scores, axis=-1, keepdims=True)
    expd = jnp.exp(scores - top)
    return expd * (1.0 / jnp.sum(expd, axis=-1, keepdims=True))


def segment_start(len_ref, row, which):
    return lax.fori_loop(0, which, lambda at, total: total + len_ref[row, at], jnp.int32(0))


class Halves:
    def __init__(self, me, own_ref, other_ref, row):
        self.me, self.own, self.other, self.row = me, own_ref, other_ref, row

    def at(self, place):
        apart = place ^ self.me
        return apart & 1, apart >> 1

    def __call__(self, place):
        odd, index = self.at(place)
        return jnp.where(odd == 1, self.other[index, self.row], self.own[index, self.row])


def forward_kernel(dims, me_ref, len_ref, bias_ref, own_ref, other_ref, o_ref, pat, txt, opat, otxt):
    rows, images, patch_dev, text_dev, slots = dims
    seq_count = 2 * own_ref.shape[0]
    text_rows = seq_count * TEXT_PITCH
    for row in range(rows):
        unpack(
            seq_count, Halves(me_ref[0], own_ref, other_ref, row),
            row, pat, txt, patch_dev, text_dev, slice(None),
        )
    otxt[...] = jnp.zeros_like(otxt)

    def attend(compact, queries, keys, length):
        q = compact[:queries, :HEAD_DIM]
        k = compact[:keys, HEAD_DIM : 2 * HEAD_DIM]
        v = compact[:keys, 2 * HEAD_DIM :]
        scores = dot_nt(q, k) + bias_ref[:queries, :keys] + masked_keys(keys, length)
        probs = softmax(scores).astype(BF16)
        return dot_nn(probs, v).astype(BF16)

    def one_segment(step, carry):
        row, image = step // images, step % images
        length = len_ref[row, image]
        first = segment_start(len_ref, row, image)
        pick = picker(TEXT_K, text_rows, text_dev, slots, first, length)
        text = dot_nn(pick, txt[row]).astype(BF16)
        at = pl.multiple_of(image * PATCHES_IMG, PATCHES_IMG)
        compact = jnp.concatenate([pat[row, pl.ds(at, PATCHES_IMG), :], text], axis=0)
        out = attend(compact, SEG_Q, SEG_K, PATCHES_IMG + length)
        opat[row, pl.ds(at, PATCHES_IMG), :] = out[:PATCHES_IMG]
        otxt[row] = otxt[row] + dot_tn(pick[:TEXT_MOST], out[PATCHES_IMG:])
        return carry

    lax.fori_loop(0, rows * images, one_segment, 0)
    pad_q = slots // 4
    pad_k = -(-pad_q // 128) * 128
    for row in range(rows):
        first = segment_start(len_ref, row, images)
        pick = picker(pad_k, text_rows, text_dev, slots, first, pad_q)
        compact = dot_nn(pick, txt[row]).astype(BF16)
        out = attend(compact, pad_q, pad_k, pad_q)
        otxt[row] = otxt[row] + dot_tn(pick[:pad_q], out)
    for place in range(seq_count):
        o_ref[place, 0:patch_dev, :] = jnp.concatenate(
            [opat[row, place * patch_dev : (place + 1) * patch_dev, :] for row in range(rows)],
            axis=1,
        )
        low = place * TEXT_PITCH
        o_ref[place, patch_dev : patch_dev + text_dev, :] = jnp.concatenate(
            [otxt[row, low : low + text_dev, :].astype(BF16) for row in range(rows)], axis=1
        )


def backward_kernel(
    dims, me_ref, len_ref, bias_ref, own_ref, other_ref, do_ref, down_ref, dother_ref, dbias_ref,
    pat, txt, dpat, dtxt, gpat, gtxt,
):
    rows, images, patch_dev, text_dev, slots = dims
    seq_count = 2 * own_ref.shape[0]
    text_rows = seq_count * TEXT_PITCH
    for row in range(rows):
        unpack(
            seq_count, Halves(me_ref[0], own_ref, other_ref, row),
            row, pat, txt, patch_dev, text_dev, slice(None),
        )
        unpack(
            seq_count, lambda place: do_ref.at[place],
            row, dpat, dtxt, patch_dev, text_dev,
            slice(row * HEAD_DIM, (row + 1) * HEAD_DIM),
        )
    gtxt[...] = jnp.zeros_like(gtxt)
    dbias_ref[...] = jnp.zeros_like(dbias_ref)

    def attend_back(compact, d_out, queries, keys, length):
        q = compact[:queries, :HEAD_DIM]
        k = compact[:keys, HEAD_DIM : 2 * HEAD_DIM]
        v = compact[:keys, 2 * HEAD_DIM :]
        scores = dot_nt(q, k) + bias_ref[:queries, :keys] + masked_keys(keys, length)
        probs = softmax(scores)
        d_probs = dot_nt(d_out, v)
        centre = jnp.sum(d_probs * probs, axis=-1, keepdims=True)
        d_scores = probs * (d_probs - centre)
        d_low = d_scores.astype(BF16)
        d_q = dot_nn(d_low, k).astype(BF16)
        d_k = dot_tn(d_low, q).astype(BF16)
        d_v = dot_tn(probs.astype(BF16), d_out).astype(BF16)
        return d_scores, jnp.concatenate([d_q, d_k[:queries], d_v[:queries]], axis=1)

    def one_segment(step, carry):
        row, image = step // images, step % images
        length = len_ref[row, image]
        first = segment_start(len_ref, row, image)
        pick = picker(TEXT_K, text_rows, text_dev, slots, first, length)
        at = pl.multiple_of(image * PATCHES_IMG, PATCHES_IMG)
        text = dot_nn(pick, txt[row]).astype(BF16)
        compact = jnp.concatenate([pat[row, pl.ds(at, PATCHES_IMG), :], text], axis=0)
        text_do = dot_nn(pick[:TEXT_MOST], dtxt[row]).astype(BF16)
        d_out = jnp.concatenate([dpat[row, pl.ds(at, PATCHES_IMG), :], text_do], axis=0)
        d_scores, grads = attend_back(compact, d_out, SEG_Q, SEG_K, PATCHES_IMG + length)
        dbias_ref[...] = dbias_ref[...] + d_scores
        gpat[row, pl.ds(at, PATCHES_IMG), :] = grads[:PATCHES_IMG]
        gtxt[row] = gtxt[row] + dot_tn(pick[:TEXT_MOST], grads[PATCHES_IMG:])
        return carry

    lax.fori_loop(0, rows * images, one_segment, 0)
    pad_q = slots // 4
    pad_k = -(-pad_q // 128) * 128
    for row in range(rows):
        first = segment_start(len_ref, row, images)
        pick = picker(pad_k, text_rows, text_dev, slots, first, pad_q)
        compact = dot_nn(pick, txt[row]).astype(BF16)
        d_out = dot_nn(pick[:pad_q], dtxt[row]).astype(BF16)
        d_scores, grads = attend_back(compact, d_out, pad_q, pad_k, pad_q)
        dbias_ref[:pad_q, :pad_k] = dbias_ref[:pad_q, :pad_k] + d_scores
        gtxt[row] = gtxt[row] + dot_tn(pick[:pad_q], grads)
    for row in range(rows):
        for place in range(seq_count):
            odd, index = Halves(me_ref[0], own_ref, other_ref, row).at(place)
            low = place * TEXT_PITCH
            patches = gpat[row, place * patch_dev : (place + 1) * patch_dev, :]
            text = gtxt[row, low : low + text_dev, :].astype(BF16)

            def put(target):
                target[index, row, 0:patch_dev, :] = patches
                target[index, row, patch_dev : patch_dev + text_dev, :] = text

            pl.when(odd == 0)(lambda: put(down_ref))
            pl.when(odd == 1)(lambda: put(dother_ref))


def mix_kernel(chips, twins, got_ref, weight_ref, resid_ref, gain_ref, mixed_ref, sum_ref, norm_ref):
    tok, packed = got_ref.shape[1:]
    for twin in range(twins):
        for row in range(packed // HEAD_DIM):
            lanes = slice(row * HEAD_DIM, (row + 1) * HEAD_DIM)
            slots = [which * twins + twin for which in range(HEADS)]
            heads = [got_ref[2 * (slot % chips) + slot // chips, :, lanes] for slot in slots]
            low = (twin * (packed // HEAD_DIM) + row) * tok
            mixed_ref[low : low + tok, :] = jnp.concatenate(heads, axis=1)
    total = resid_ref[...] + dot_nt(mixed_ref[...], weight_ref[...])
    sum_ref[...] = total
    norm_ref[...] = rms_norm(total, gain_ref[...]).astype(BF16)


def project_kernel(low_ref, high_ref, weight_ref, out_ref):
    half = low_ref.shape[1]
    value = dot_nt(low_ref[...], weight_ref[:, :half]) + dot_nt(
        high_ref[...], weight_ref[:, half:]
    )
    out_ref[...] = value.reshape(out_ref.shape).astype(BF16)


def return_kernel(grad_ref, weight_ref, low_ref, high_ref):
    half = low_ref.shape[1]
    low_ref[...] = dot_nn(grad_ref[...], weight_ref[:, :half]).astype(BF16)
    high_ref[...] = dot_nn(grad_ref[...], weight_ref[:, half:]).astype(BF16)


def norm_back(values, gain, grad):
    scale = lax.rsqrt(jnp.mean(values * values, axis=-1, keepdims=True) + EPSILON)
    unit = values * scale
    scaled = grad * gain
    d_values = scale * (scaled - unit * jnp.mean(scaled * unit, axis=-1, keepdims=True))
    return d_values, jnp.sum(grad * unit, axis=0, keepdims=True)


def turn_kernel(
    chips, twins, keep_ref, got_ref, sum_ref, gain_ref, up_ref, weight_ref,
    packed_ref, d_sum_ref, low_ref, d_gain_ref, heads,
):
    grad = keep_ref[...] + got_ref[...].astype(F32)
    d_values, d_gain = norm_back(sum_ref[...], gain_ref[...], grad)
    total = d_values + up_ref[...].astype(F32)
    d_sum_ref[...] = total
    low_ref[...] = total.astype(BF16)
    d_gain_ref[...] = jnp.broadcast_to(d_gain, d_gain_ref.shape)
    heads[...] = dot_nn(low_ref[...], weight_ref[...]).astype(BF16)
    tok, packed = packed_ref.shape[1:]
    rows = packed // HEAD_DIM
    for twin in range(twins):
        for which in range(HEADS):
            slot = which * twins + twin
            parts = []
            for row in range(rows):
                low = (twin * rows + row) * tok
                parts.append(heads[low : low + tok, which * HEAD_DIM : (which + 1) * HEAD_DIM])
            packed_ref[2 * (slot % chips) + slot // chips] = jnp.concatenate(parts, axis=1)


SMEM = pl.BlockSpec(memory_space=pltpu.SMEM)
VMEM = pl.BlockSpec(memory_space=pltpu.VMEM)


def call(kernel, out_shape, in_specs, scratch=(), flops=0, bytes_accessed=0, vmem=16):
    single = not isinstance(out_shape, (tuple, list))
    return pl.pallas_call(
        kernel,
        out_shape=out_shape,
        in_specs=in_specs,
        out_specs=VMEM if single else [VMEM] * len(out_shape),
        scratch_shapes=list(scratch),
        cost_estimate=pl.CostEstimate(
            flops=flops, bytes_accessed=bytes_accessed, transcendentals=0
        ),
        compiler_params=pltpu.CompilerParams(vmem_limit_bytes=vmem << 20),
        interpret=INTERPRET,
    )


def local(
    patch_features, text_embeds, text_lengths, w_in, b_in, gain_attn, w_query, w_key, w_value,
    w_out, gain_ffn, w_gate, w_up, w_down, position_bias, d_patch, d_text,
):
    seq_count, dp_count = lax.axis_size(SEQ), lax.axis_size("dp")
    dev_count = seq_count * dp_count
    seq_index, dp_index = lax.axis_index(SEQ), lax.axis_index("dp")
    rows, patch_dev, vit = patch_features.shape
    text_dev = text_embeds.shape[1]
    tok = patch_dev + text_dev
    mine = rows * tok
    d_model = text_embeds.shape[2]
    cols = w_in.shape[1]
    images = text_lengths.shape[1]
    slots = text_dev * seq_count
    core, near = ("seq", 0), ("seq", 1)
    seq_high = [("seq", bit) for bit in range(seq_count.bit_length() - 2, 1, -1)]
    dp_bits = [("dp", bit) for bit in range(dp_count.bit_length() - 1)]
    every = dp_bits + seq_high + [near, core]

    bias_count = position_bias.shape[0]
    pack = jnp.concatenate(
        [
            w_in,
            b_in[None],
            gain_attn[None],
            gain_ffn[None],
            jnp.pad(position_bias, (0, cols - bias_count))[None],
            jnp.zeros((124, cols), BF16),
            w_out,
        ],
        axis=0,
    ).T
    wide = vit + 128
    half_in = wide // 256 * 128
    per_head = dev_count // HEADS
    twins = seq_count // HEADS
    chips = seq_count // 2
    head_slot = (seq_index % 2) * chips + seq_index // 2
    head = head_slot // twins
    twin = head_slot % twins
    place_in_head = dp_index * twins + twin
    row_count = rows // twins
    three = jnp.concatenate([w_query.T, w_key.T, w_value.T], axis=0)

    def to_rank(which_head, place):
        slot = which_head * twins + place % twins
        return (place // twins) * seq_count + 2 * (slot % chips) + slot // chips

    def rounds(turn, back):
        pairs = []
        for which_head in range(HEADS):
            for i in range(per_head):
                owner = which_head * per_head + i
                user = to_rank(which_head, (i + turn) % per_head)
                pairs.append((user, owner) if back else (owner, user))
        return pairs

    team = [("seq", 2), near, core]
    ff_far = [step for step in seq_high if step not in team]
    ff_order = ff_far + dp_bits
    units = w_gate.shape[1]
    down_out = jnp.transpose(w_down.reshape(dev_count, units, cols), (0, 2, 1))
    down_in = lax.all_to_all(down_out, BOTH, 0, 0, tiled=True)
    upstream = jnp.concatenate([d_patch, d_text], axis=1).reshape(mine, d_model)
    up_got = swap(upstream, team[0])
    late = {}

    def far_gather(block):
        for step in ff_far[:-1]:
            block = jnp.concatenate([block, swap(block, step)], axis=0)
        return block, swap(block, ff_far[-1])

    gate_up, gate_up_got = far_gather(jnp.concatenate([w_gate.T, w_up.T], axis=1))

    def while_near(block):
        block, late["gate_up"] = together(block, gate_up_got)
        return block

    def while_core(block):
        block, got = together(block, up_got)
        late["up"] = jnp.concatenate([upstream, got], axis=0)
        late["up_got"] = swap(late["up"], team[1])
        late["pieces"] = [lax.ppermute(three, BOTH, rounds(turn, False)) for turn in range(per_head)]
        return block

    pack = gather(pack, seq_high, True)
    in_low = gather(
        pack[:, :half_in],
        dp_bits + [near, core],
        True,
        {len(dp_bits): while_near, len(dp_bits) + 1: while_core},
        seq_high,
    )
    in_high = gather(pack[:, half_in:wide], [near] + dp_bits + [core], True, None, seq_high)
    out_block = {"mine": pack[:, wide:], "have": list(seq_high)}

    def out_start(block, step):
        block, send = together(block, out_block["mine"])
        out_block["mine"], out_block["got"] = send, swap(send, step)
        return block

    def out_take(block, step):
        block, got = together(block, out_block["got"])
        out_block["mine"] = joined(out_block["mine"], got, step, out_block["have"], True)
        out_block["have"].append(step)
        return block

    features = patch_features.reshape(rows * patch_dev, vit)
    ones = jnp.zeros((rows * patch_dev, 128), BF16).at[:, 0].set(1)
    features_more = jnp.concatenate([features, ones], axis=1)
    patch_rows = dot_nt(features_more[:, :half_in], in_low) + dot_nt(
        features_more[:, half_in:], in_high
    )
    units_eye = jnp.eye(8, 128, dtype=BF16)
    small = dot_nt(units_eye, in_high[:, wide - half_in - 128 :])
    gain_one, gain_two = small[1], small[2]
    table = small[3].reshape(dev_count, cols)[:, :bias_count].reshape(BUCKETS, HEADS)
    my_table = lax.dynamic_slice_in_dim(table, head, 1, 1).reshape(1, BUCKETS)
    resid = jnp.concatenate(
        [patch_rows.reshape(rows, patch_dev, d_model), text_embeds.astype(F32)], axis=1
    ).reshape(mine, d_model)
    normed_one = rms_norm(resid, gain_one).astype(BF16)
    half = d_model // 2
    order_low = seq_high + [near]
    order_high = [near] + seq_high
    normed_one, *late["pieces"] = together(normed_one, *late["pieces"])

    def while_start(block):
        for step in dp_bits[:-1]:
            block = out_take(out_start(block, step), step)
        return out_start(block, dp_bits[-1])

    pieces = jnp.stack(late["pieces"]).reshape(per_head, 3, cols, d_model)
    ordered = [
        lax.dynamic_index_in_dim(pieces, (place_in_head - i) % per_head, 0, keepdims=False)
        for i in range(per_head)
    ]
    w_head = jnp.stack(ordered, axis=1).reshape(3 * HEAD_DIM, d_model)
    bias = call(
        bias_kernel, jax.ShapeDtypeStruct((SEG_Q, SEG_K), F32), [SMEM], (), 1 << 24, 1 << 20, 8
    )(my_table)
    def while_second(block):
        block, late["up_got"] = together(block, late["up_got"])
        block, late["w_head"], late["bias"] = together(block, w_head, bias)
        return out_start(out_take(block, dp_bits[-1]), near)

    def while_last(block):
        return out_start(out_take(block, near), core)

    own_low = gather(
        normed_one[:, :half],
        order_low,
        False,
        {0: while_start, 1: while_second, len(order_low) - 1: while_last},
    )
    gate_up = jnp.concatenate([gate_up, late["gate_up"]], axis=0)
    for step in dp_bits[:-1]:
        gate_up = jnp.concatenate([gate_up, swap(gate_up, step)], axis=0)
    gate_up_got = swap(gate_up, dp_bits[-1])
    team_up = jnp.concatenate([late["up"], late["up_got"]], axis=0)
    team_up = jnp.concatenate([team_up, swap(team_up, core)], axis=0)
    w_head, bias = late["w_head"], late["bias"]
    own_high = gather(normed_one[:, half:], order_high, False)
    own_low, own_high, late["down"] = together(own_low, own_high, down_in)
    other_low, other_high = swap(own_low, core), swap(own_high, core)

    def my_rows(array):
        if twins == 1:
            return array
        view = array.reshape(chips, rows, tok, array.shape[1])
        view = lax.dynamic_slice_in_dim(view, twin * row_count, row_count, 1)
        return view.reshape(chips * row_count * tok, array.shape[1])

    normed_pairs = [
        (my_rows(own_low), my_rows(own_high)),
        (my_rows(other_low), my_rows(other_high)),
    ]
    qkv = [
        call(
            project_kernel,
            jax.ShapeDtypeStruct((chips, row_count, tok, 3 * HEAD_DIM), BF16),
            [VMEM] * 3,
            (),
            1 << 24,
            1 << 20,
            14,
        )(low, high, w_head)
        for low, high in normed_pairs
    ]
    down = late["down"]
    full_down, down_got = far_gather(down.reshape(d_model, units).T)
    lengths = lax.dynamic_slice_in_dim(text_lengths, twin * row_count, row_count, 0)
    me = seq_index.reshape(1).astype(jnp.int32)
    dims = (row_count, images, patch_dev, text_dev, slots)
    text_rows = seq_count * TEXT_PITCH
    patches = seq_count * patch_dev
    packed_shape = jax.ShapeDtypeStruct((seq_count, tok, row_count * HEAD_DIM), BF16)
    mixed = call(
        lambda *refs: forward_kernel(dims, *refs),
        packed_shape,
        [SMEM, SMEM, VMEM, VMEM, VMEM],
        (
            pltpu.VMEM((row_count, patches, 3 * HEAD_DIM), BF16),
            pltpu.VMEM((row_count, text_rows, 3 * HEAD_DIM), BF16),
            pltpu.VMEM((row_count, patches, HEAD_DIM), BF16),
            pltpu.VMEM((row_count, text_rows, HEAD_DIM), F32),
        ),
        1 << 24,
        1 << 20,
        20,
    )(me, lengths, bias, *qkv)
    mixed, gate_up_got, down_got = together(mixed, gate_up_got, down_got)
    full_gate, full_up = [
        jnp.concatenate([array[:, part] for array in (gate_up, gate_up_got)], axis=0)
        for part in (slice(0, d_model), slice(d_model, 2 * d_model))
    ]
    mixed_got = lax.all_to_all(mixed, SEQ, 0, 0, tiled=True)
    mixed_got = out_take(mixed_got, core)
    full_out = out_block["mine"]
    full_down = jnp.concatenate([full_down, down_got], axis=0)
    for step in dp_bits[:-1]:
        full_down = jnp.concatenate([full_down, swap(full_down, step)], axis=0)
    full_down = jnp.concatenate([full_down, swap(full_down, dp_bits[-1])], axis=0)
    attn_out, resid_one, normed_two = call(
        lambda *refs: mix_kernel(chips, twins, *refs),
        (
            jax.ShapeDtypeStruct((mine, d_model), BF16),
            jax.ShapeDtypeStruct((mine, d_model), F32),
            jax.ShapeDtypeStruct((mine, d_model), BF16),
        ),
        [VMEM, VMEM, VMEM, VMEM],
        (),
        1 << 24,
        1 << 20,
        12,
    )(mixed_got, full_out, resid, gain_two[None])
    team_normed = normed_two
    for step in team:
        got = swap(team_normed, step)
        if step == near:
            team_normed, full_gate, full_up, full_down = together(
                team_normed, full_gate, full_up, full_down
            )
        team_normed = jnp.concatenate([team_normed, got], axis=0)
    gate_pre = dot_nt(team_normed, full_gate)
    up_pre = dot_nt(team_normed, full_up)
    hidden, gated_back = jax.vjp(gated_unit, gate_pre, up_pre)
    hidden = hidden.astype(BF16)

    state = {}
    grad_down = dot_tn(hidden, team_up).astype(BF16)

    def down_start(step):
        count = grad_down_of["sum"].shape[0] // 2
        grad_down_of["keep"] = grad_down_of["sum"][:count]
        grad_down_of["got"] = swap(grad_down_of["sum"][count:].astype(BF16), step)

    def down_take(keep):
        keep, got = together(keep, grad_down_of["got"])
        grad_down_of["sum"] = grad_down_of["keep"].astype(F32) + got.astype(F32)
        return keep

    grad_down_of = {"sum": grad_down}
    down_start(dp_bits[-1])
    d_gate, d_up = gated_back(dot_nt(team_up, full_down))
    d_gate, d_up = d_gate.astype(BF16), d_up.astype(BF16)
    d_normed_two = dot_nn(d_gate, full_gate) + dot_nn(d_up, full_up)

    def ff_take(keep):
        keep, got = together(keep, state["ff_got"])
        state["ff"] = state["ff_keep"].astype(F32) + got.astype(F32)
        return keep

    def ff_start(keep, step):
        count = state["ff"].shape[0] // 2
        state["ff_keep"] = state["ff"][:count]
        keep, send = together(keep, state["ff"][count:].astype(BF16))
        state["ff_got"] = swap(send, step)
        return keep

    def while_team(keep):
        keep, *grads = together(keep, d_gate, d_up)
        state["ff"] = jnp.concatenate(
            [dot_tn(grad, team_normed).astype(BF16) for grad in grads], axis=1
        )
        return ff_start(keep, dp_bits[-1])

    def team_sum(part, step, hook=None):
        keep, send = halves(part, step, [step], False)
        got = swap(send.astype(BF16), step)
        return (hook(keep) if hook else keep) + got.astype(F32)

    d_normed_two = team_sum(d_normed_two, team[2])
    d_normed_two = team_sum(d_normed_two, team[1], while_team)
    turn_keep, send = halves(d_normed_two, team[0], [team[0]], False)
    turn_got = swap(send.astype(BF16), team[0])
    d_attn, d_resid_one, d_mix, grad_gain_two = call(
        lambda *refs: turn_kernel(chips, twins, *refs),
        (
            packed_shape,
            jax.ShapeDtypeStruct((mine, d_model), F32),
            jax.ShapeDtypeStruct((mine, d_model), BF16),
            jax.ShapeDtypeStruct((8, d_model), F32),
        ),
        [VMEM] * 6,
        (pltpu.VMEM((mine, d_model), BF16),),
        1 << 24,
        1 << 20,
        14,
    )(turn_keep, turn_got, resid_one, gain_two[None], upstream, full_out)
    grad_gain_two = grad_gain_two[0]
    d_attn_got = lax.all_to_all(d_attn, SEQ, 0, 0, tiled=True)

    out_grad = {"sum": dot_tn(d_mix, attn_out).astype(BF16), "left": list(every)}

    def out_grad_start(keep, step):
        out_grad["keep"], send = halves(out_grad["sum"], step, out_grad["left"], True)
        keep, send = together(keep, send.astype(BF16))
        out_grad["got"] = swap(send, step)
        return keep

    def out_grad_take(keep, step):
        keep, got = together(keep, out_grad["got"])
        out_grad["sum"] = out_grad["keep"].astype(F32) + got.astype(F32)
        out_grad["left"].remove(step)
        return keep

    d_mix = down_take(d_mix)
    for step in dp_bits[-2::-1] + ff_far[:0:-1]:
        down_start(step)
        d_mix = down_take(d_mix)
    down_start(ff_far[0])
    out_part = team_sum(dot_nn(hidden, full_down), core)
    out_keep, send = halves(out_part, team[1], [team[1]], False)
    d_attn_got, send = together(out_grad_start(d_attn_got, core), send.astype(BF16))
    out_got = swap(send, team[1])
    half_shape = jax.ShapeDtypeStruct(qkv[0].shape, BF16)
    d_own, d_other, d_bias = call(
        lambda *refs: backward_kernel(dims, *refs),
        (half_shape, half_shape, jax.ShapeDtypeStruct((SEG_Q, SEG_K), F32)),
        [SMEM, SMEM, VMEM, VMEM, VMEM, VMEM],
        (
            pltpu.VMEM((row_count, patches, 3 * HEAD_DIM), BF16),
            pltpu.VMEM((row_count, text_rows, 3 * HEAD_DIM), BF16),
            pltpu.VMEM((row_count, patches, HEAD_DIM), BF16),
            pltpu.VMEM((row_count, text_rows, HEAD_DIM), BF16),
            pltpu.VMEM((row_count, patches, 3 * HEAD_DIM), BF16),
            pltpu.VMEM((row_count, text_rows, 3 * HEAD_DIM), F32),
        ),
        1 << 24,
        1 << 20,
        28,
    )(me, lengths, bias, *qkv, d_attn_got)
    d_other, out_got = together(down_take(d_other), out_got)
    out_part = out_keep + out_got.astype(F32)
    down_back = grad_down_of["sum"].astype(BF16).T.reshape(dev_count, cols, units)
    state["down_back"] = lax.all_to_all(down_back, BOTH, 0, 0, tiled=True)
    d_qkv = [array.reshape(chips * row_count * tok, 3 * HEAD_DIM) for array in (d_own, d_other)]

    def all_rows(array):
        if twins == 1:
            return array
        view = array.reshape(chips, row_count, tok, array.shape[1])
        zero = jnp.zeros((chips, rows, tok, array.shape[1]), array.dtype)
        view = lax.dynamic_update_slice_in_dim(zero, view, twin * row_count, 1)
        return view.reshape(chips * mine, array.shape[1])

    chip_bits = seq_high + [near]
    weights = (w_head[:, :half], w_head[:, half:])
    part_shape = jax.ShapeDtypeStruct((d_qkv[1].shape[0], half), BF16)
    shares = call(return_kernel, (part_shape,) * 2, [VMEM] * 2, (), 1 << 24, 1 << 20, 14)(
        d_qkv[1], w_head
    )
    sends = together(*[all_rows(share) for share in shares], d_own)
    others = [swap(send, core) for send in sends[:2]]
    d_qkv[0] = sends[2].reshape(d_qkv[0].shape)
    owns = [
        all_rows(dot_nn(d_qkv[0], part)) + other.astype(F32) for part, other in zip(weights, others)
    ]
    def while_first(keep):
        keep = ff_take(keep)
        for step in dp_bits[-2::-1]:
            keep = ff_take(ff_start(keep, step))
        for step in ff_far[:0:-1]:
            keep = ff_take(ff_start(keep, step))
        keep = out_grad_take(keep, dp_bits[-1])
        for step in dp_bits[-2::-1]:
            keep = out_grad_take(out_grad_start(keep, step), step)
        return out_grad_start(keep, near)

    def while_middle(keep):
        keep = out_grad_start(out_grad_take(keep, core), dp_bits[-1])
        keep, grads_own, grads_other = together(keep, *d_qkv)
        d_head = jnp.concatenate(
            [
                dot_tn(grads_own, normed_pairs[0][which])
                + dot_tn(grads_other, normed_pairs[1][which])
                for which in range(2)
            ],
            axis=1,
        )
        d_head = d_head.reshape(3, per_head, cols, d_model).astype(BF16)
        sends = [
            lax.dynamic_index_in_dim(
                d_head, (place_in_head - turn) % per_head, 1, keepdims=False
            ).reshape(3 * cols, d_model)
            for turn in range(per_head)
        ]
        keep, *sends = together(keep, *sends)
        state["three"] = [
            lax.ppermute(send, BOTH, rounds(turn, True)) for turn, send in enumerate(sends)
        ]
        return keep

    def while_late(keep):
        keep, *state["three"] = together(keep, *state["three"])
        return keep

    low_sums, high_sums = scatter_add_pair(
        *owns,
        order_low[::-1],
        order_high[::-1],
        chip_bits,
        False,
        {0: while_middle, 1: while_first, len(order_low) - 1: while_late},
    )
    d_normed_one = jnp.concatenate([low_sums, high_sums], axis=1)
    d_table = call(
        bucket_kernel, jax.ShapeDtypeStruct((BUCKETS, 128), F32), [VMEM], (), 1 << 20, 1 << 20, 8
    )(d_bias)[:, 0]
    _, norm_back_one = jax.vjp(rms_norm, resid, gain_one)
    d_resid, grad_gain_one = norm_back_one(d_normed_one)
    d_resid = (d_resid + d_resid_one).reshape(rows, tok, d_model)
    text_grad = d_resid[:, patch_dev:]
    d_patch_rows = d_resid[:, :patch_dev].reshape(rows * patch_dev, d_model)
    d_low = d_patch_rows.astype(BF16)
    pos_grads = d_table[:, None] * (jnp.arange(HEADS)[None, :] == head).astype(F32)
    pos_grads = jnp.pad(
        pos_grads.reshape(dev_count, bias_count), ((0, 0), (0, cols - bias_count))
    ).reshape(1, d_model)
    small_grads = jnp.concatenate(
        [
            jnp.sum(d_patch_rows, axis=0)[None],
            grad_gain_one[None],
            grad_gain_two[None],
            pos_grads,
            jnp.zeros((12, d_model), F32),
        ],
        axis=0,
    ).astype(BF16)
    left = jnp.concatenate([d_low, small_grads], axis=0)
    right = jnp.concatenate(
        [
            jnp.pad(features, ((0, 0), (0, 128))),
            jnp.pad(jnp.eye(16, 128, dtype=BF16), ((0, 0), (vit, 0))),
        ],
        axis=0,
    )

    def while_core_again(keep):
        keep = ff_start(keep, ff_far[0])
        keep, part = together(keep, out_part)
        state["out_keep"], send = halves(part, team[0], [team[0]], False)
        state["out_got"] = swap(send.astype(BF16), team[0])
        keep, state["d_low"] = together(keep, d_low)
        return keep

    def while_half_again(keep):
        keep, state["out_got"] = together(ff_take(out_grad_take(keep, near)), state["out_got"])
        return keep

    def while_end(keep):
        keep, state["down_back"] = together(keep, state["down_back"])
        return keep

    in_low_sums, in_high_sums = scatter_add_pair(
        dot_tn(left, right[:, :half_in]).astype(BF16),
        dot_tn(left, right[:, half_in:]).astype(BF16),
        [core, near] + dp_bits[::-1],
        [core] + dp_bits[::-1] + [near],
        every,
        True,
        {0: while_core_again, 2: while_half_again},
    )
    in_grads = scatter_add(
        jnp.concatenate([in_low_sums, in_high_sums, out_grad["sum"]], axis=1),
        seq_high[::-1],
        seq_high,
        True,
        {0: while_end},
    )
    small_out, grad_w_out = in_grads[:, vit:wide], in_grads[:, wide:]
    d_low = state["d_low"]
    feature_grad = jnp.concatenate(
        [dot_nn(d_low, in_low), dot_nn(d_low, in_high[:, : vit - half_in])], axis=1
    ).reshape(rows, patch_dev, vit)
    result = resid_one + state["out_keep"] + state["out_got"].astype(F32)
    result = result.astype(BF16).reshape(rows, tok, d_model)
    grad_gate, grad_up = state["ff"][:, :d_model], state["ff"][:, d_model:]
    grad_down = jnp.transpose(state["down_back"], (0, 2, 1)).reshape(dev_count * units, cols)
    grad_down = grad_down.astype(F32)
    d_three = sum(got.astype(F32) for got in state["three"]).reshape(3, cols, d_model)
    return (
        result[:, :patch_dev],
        result[:, patch_dev:],
        feature_grad,
        text_grad,
        in_grads[:, :vit].T,
        small_out[:, 0],
        small_out[:, 1],
        d_three[0].T,
        d_three[1].T,
        d_three[2].T,
        grad_w_out.T,
        small_out[:, 2],
        grad_gate.T,
        grad_up.T,
        grad_down,
        small_out[:bias_count, 3],
    )


def solution(mesh):
    token = P("dp", SEQ, None)
    matrix = P(None, BOTH)
    vector = P(BOTH)
    return jax.shard_map(
        local,
        mesh=mesh,
        in_specs=(
            token, token, P("dp", None), matrix, vector, vector, matrix, matrix, matrix, matrix,
            vector, matrix, matrix, matrix, vector, token, token,
        ),
        out_specs=(
            token, token, token, token, matrix, vector, vector, matrix, matrix, matrix, matrix,
            vector, matrix, matrix, matrix, vector,
        ),
        check_vma=False,
    )
```
